256 devices in a mesh: tm: 16 (over y, z_lo, core), bank: 16 (over x, z_hi).
Axes of the slice: x: 4, y: 4, z: 8 (z_hi: 4, z_lo: 2; z = z_hi * 2 + z_lo), core: 2. Of those that a mesh axis runs over, the one named last changes fastest.
Arguments:
- spectrum: float32 [2, 64, 16384], P(None, None, 'tm'), may hold values from -6 to 6
- filters: bfloat16 [2, 512, 64, 16384], P(None, 'bank', None, 'tm'), may hold values from -0.005859375 to 0.005859375
- mixing: bfloat16 [2, 16384, 512], P(None, 'bank'), may hold values from -0.25 to 0.25
Outputs:
- snr_series: bfloat16 [2, 64, 16384, 128], P(None, 'tm', 'bank')
The draws below stay inside these ranges and needn't reach their ends.
All inputs are finite; a program needn't handle non-finite values.
Results may differ from the reference program's by a relative error of at most 0.007.
Values may be sent and summed in bfloat16 or wider, within the bound.
A program may use at most 128 MiB of HBM per device.

```python
import math
import jax
import jax.numpy as jnp
from jax import lax

NSAMP = 1048576
INNER = 64
BASIS = 512
TEMPLATES = 16384
OUTER = 16384
WROWS = 128
START = 8128


def spiked(drawn, stream_key, source, target, shards_of, factor):
    owner, partner = [(jnp.arange(drawn.shape[axis_at]) // (drawn.shape[axis_at] // shards_of)).reshape([-1 if axis == axis_at else 1 for axis in range(drawn.ndim)]) for axis_at in (source, target)]
    chosen = jax.random.permutation(stream_key, shards_of)[partner]
    strong = (owner == chosen) | (owner == (partner + shards_of // 2) % shards_of)
    return jnp.where(strong, factor * drawn, drawn)


def block_scale(rng, shape, pieces, least, largest):
    def one(position, parts):
        heights = jax.random.uniform(jax.random.fold_in(jax.random.fold_in(rng, 6), position), (parts,), jnp.float32, least / len(pieces), largest / len(pieces))
        return jnp.repeat(jnp.exp(heights), shape[position] // parts).reshape((-1,) + (1,) * (len(shape) - position - 1))

    gain = one(*pieces[0])
    for cut in pieces[1:]:
        gain = gain * one(*cut)
    return gain


def scatter_about(own_key, extent, deviation, limit, cuts=(), kind=jnp.bfloat16):
    loudness = block_scale(own_key, extent, cuts, -0.22, 0.18) if cuts else 1.0
    drawn = jax.random.normal(own_key, extent, jnp.float32) * deviation * loudness
    return jnp.minimum(jnp.maximum(drawn, -limit), limit).astype(kind)


def bell_draw_with(rng, extent, deviation, bound, shards, heavy, kind=jnp.bfloat16):
    drawn = deviation * jax.random.normal(rng, extent, jnp.float32)
    if shards:
        drawn = drawn * block_scale(rng, extent, shards, -0.22, 0.18)
    return jnp.clip(spiked(drawn, jax.random.fold_in(rng, 3), *heavy), -bound, bound).astype(kind)


def setup_inputs(seed: int = 0) -> dict:
    splits = jax.random.split(jax.random.key(seed), 4)
    return {
        "spectrum": scatter_about(splits[0], (2, INNER, OUTER), 1.0, 6.0, ((2, 16),), jnp.float32),
        "filters": scatter_about(splits[1], (2, BASIS, INNER, OUTER), NSAMP ** -0.5, 0.005859375, ((1, 16), (3, 16))),
        "mixing": bell_draw_with(splits[2], (2, TEMPLATES, BASIS), (2 * BASIS) ** -0.5, 0.25, ((1, 16),), (2, 1, 16, 2.0)),
    }


def first_table(inner):
    index = jnp.arange(inner, dtype=jnp.int32)
    phase = (index[:, None] * index[None, :]) % inner
    angle = phase.astype(jnp.float32) * (2.0 * math.pi / inner)
    cosine = jnp.cos(angle).astype(jnp.bfloat16)
    sine = jnp.sin(angle).astype(jnp.bfloat16)
    upper = jnp.concatenate([cosine, -sine], axis=1)
    lower = jnp.concatenate([sine, cosine], axis=1)
    return jnp.concatenate([upper, lower], axis=0)


def wave_tables(freqs, lags, period):
    phase = (freqs[:, None] * lags[None, :]) % period
    angle = phase.astype(jnp.float32) * (2.0 * math.pi / period)
    return jnp.cos(angle).astype(jnp.bfloat16), jnp.sin(angle).astype(jnp.bfloat16)


def twist_tables(freqs, inner, total):
    rows_index = jnp.arange(inner, dtype=jnp.int32)
    phase = (rows_index[:, None] * freqs[None, :]) % total
    angle = phase.astype(jnp.float32) * (2.0 * math.pi / total)
    return jnp.cos(angle), jnp.sin(angle)


def transform_block(spectrum, block, table, twist_cos, twist_sin, wave_cos, wave_sin):
    inner = block.shape[2]
    filt_real = block[:, 0].astype(jnp.float32)
    filt_imag = block[:, 1].astype(jnp.float32)
    prod_real = spectrum[0] * filt_real + spectrum[1] * filt_imag
    prod_imag = spectrum[1] * filt_real - spectrum[0] * filt_imag
    packed = jnp.concatenate([prod_real, prod_imag], axis=1).astype(jnp.bfloat16)
    section = jnp.einsum('uv,kvf->kuf', table.astype(jnp.float32), packed.astype(jnp.float32))
    section_real = section[:, :inner]
    section_imag = section[:, inner:]
    quarter_real = (section_real * twist_cos - section_imag * twist_sin).astype(jnp.bfloat16).astype(jnp.float32)
    quarter_imag = (section_real * twist_sin + section_imag * twist_cos).astype(jnp.bfloat16).astype(jnp.float32)
    wave_c = wave_cos.astype(jnp.float32)
    wave_s = wave_sin.astype(jnp.float32)
    series_real = jnp.einsum('krf,fb->krb', quarter_real, wave_c) - jnp.einsum('krf,fb->krb', quarter_imag, wave_s)
    series_imag = jnp.einsum('krf,fb->krb', quarter_real, wave_s) + jnp.einsum('krf,fb->krb', quarter_imag, wave_c)
    return jnp.stack([series_real, series_imag], axis=1).astype(jnp.bfloat16)


def reference(spectrum, filters, mixing):
    inner = INNER
    outer = NSAMP // INNER
    table = first_table(inner)
    freqs = jnp.arange(outer, dtype=jnp.int32)
    twist_cos, twist_sin = twist_tables(freqs, inner, NSAMP)
    lags = START + jnp.arange(WROWS, dtype=jnp.int32)
    wave_cos, wave_sin = wave_tables(freqs, lags, outer)
    group = math.gcd(BASIS, 32)
    blocks = filters.reshape(2, BASIS // group, group, inner, outer).transpose(1, 2, 0, 3, 4)

    def one_block(block):
        return transform_block(spectrum, block, table, twist_cos, twist_sin, wave_cos, wave_sin)

    series = lax.map(one_block, blocks).reshape(BASIS, 2, inner, WROWS)
    series_real = series[:, 0].astype(jnp.float32)
    series_imag = series[:, 1].astype(jnp.float32)
    mix_real = mixing[0].astype(jnp.float32)
    mix_imag = mixing[1].astype(jnp.float32)
    out_real = jnp.einsum('jk,krb->rjb', mix_real, series_real) - jnp.einsum('jk,krb->rjb', mix_imag, series_imag)
    out_imag = jnp.einsum('jk,krb->rjb', mix_real, series_imag) + jnp.einsum('jk,krb->rjb', mix_imag, series_real)
    return jnp.stack([out_real, out_imag], axis=0).astype(jnp.bfloat16)
```

```python
import math

import jax
import jax.numpy as jnp
from jax import lax
from jax.sharding import PartitionSpec as P

NSAMP = 1048576
INNER = 64
WROWS = 128
START = 8128


def first_table(inner):
    index = jnp.arange(inner, dtype=jnp.int32)
    phase = index[:, None] * index[None, :] % inner
    angle = phase.astype(jnp.float32) * (2.0 * math.pi / inner)
    cosine = jnp.cos(angle).astype(jnp.bfloat16)
    sine = jnp.sin(angle).astype(jnp.bfloat16)
    upper = jnp.concatenate([cosine, -sine], axis=1)
    lower = jnp.concatenate([sine, cosine], axis=1)
    return jnp.concatenate([upper, lower], axis=0)


def wave_block(freqs, lags, period):
    phase = freqs[:, None] * lags[None, :] % period
    angle = phase.astype(jnp.float32) * (2.0 * math.pi / period)
    cosine = jnp.cos(angle).astype(jnp.bfloat16)
    sine = jnp.sin(angle).astype(jnp.bfloat16)
    upper = jnp.concatenate([cosine, sine], axis=1)
    lower = jnp.concatenate([-sine, cosine], axis=1)
    return jnp.concatenate([upper, lower], axis=0)


def twist_tables(freqs, inner, total):
    rows_index = jnp.arange(inner, dtype=jnp.int32)
    phase = rows_index[:, None] * freqs[None, :] % total
    angle = phase.astype(jnp.float32) * (2.0 * math.pi / total)
    return (jnp.cos(angle), jnp.sin(angle))


def on_device(spectrum, filters, mixing):
    tm_index = lax.axis_index("tm")
    local_freq = filters.shape[3]
    local_basis = filters.shape[1]
    inner = INNER
    outer = NSAMP // INNER
    table = first_table(inner)
    freqs = tm_index * local_freq + jnp.arange(local_freq, dtype=jnp.int32)
    twist_cos, twist_sin = twist_tables(freqs, inner, NSAMP)
    filt_real = filters[0].astype(jnp.float32)
    filt_imag = filters[1].astype(jnp.float32)
    prod_real = spectrum[0] * filt_real + spectrum[1] * filt_imag
    prod_imag = spectrum[1] * filt_real - spectrum[0] * filt_imag
    packed = jnp.concatenate([prod_real, prod_imag], axis=1).astype(jnp.bfloat16)
    section = jnp.einsum("uv,kvf->kuf", table, packed, preferred_element_type=jnp.float32)
    section_real = section[:, :inner]
    section_imag = section[:, inner:]
    quarter_real = (section_real * twist_cos - section_imag * twist_sin).astype(jnp.bfloat16)
    quarter_imag = (section_real * twist_sin + section_imag * twist_cos).astype(jnp.bfloat16)
    quarter = jnp.concatenate([quarter_real, quarter_imag], axis=2)
    lags = START + jnp.arange(WROWS, dtype=jnp.int32)
    wave = wave_block(freqs, lags, outer)
    partial = jnp.einsum("ktf,fs->tks", quarter, wave, preferred_element_type=jnp.float32)
    summed = lax.psum_scatter(partial, "tm", scatter_dimension=0, tiled=True)
    series = summed.astype(jnp.bfloat16)
    piece = lax.all_gather(series, "bank", axis=0, tiled=False)
    groups = piece.shape[0]
    rows = piece.shape[1]
    piece_real = piece[..., :WROWS]
    piece_imag = piece[..., WROWS:]
    templates = mixing.shape[1]
    mix_real = mixing[0].reshape(templates, groups, local_basis)
    mix_imag = mixing[1].reshape(templates, groups, local_basis)
    real_sum = jnp.einsum(
        "jgk,gtks->tjs", mix_real, piece_real, preferred_element_type=jnp.float32
    ) - jnp.einsum("jgk,gtks->tjs", mix_imag, piece_imag, preferred_element_type=jnp.float32)
    imag_sum = jnp.einsum(
        "jgk,gtks->tjs", mix_real, piece_imag, preferred_element_type=jnp.float32
    ) + jnp.einsum("jgk,gtks->tjs", mix_imag, piece_real, preferred_element_type=jnp.float32)
    del rows
    return jnp.stack([real_sum, imag_sum], axis=0).astype(jnp.bfloat16)


def solution(mesh):
    return jax.shard_map(
        on_device,
        mesh=mesh,
        in_specs=(P(None, None, "tm"), P(None, "bank", None, "tm"), P(None, "bank", None)),
        out_specs=P(None, "tm", "bank", None),
        check_vma=False,
    )
```

```python
import functools
import math

import jax
import jax.numpy as jnp
from jax import lax
from jax.experimental import pallas as pl
from jax.experimental.pallas import tpu as pltpu
from jax.sharding import PartitionSpec as P

NSAMP = 1048576
INNER = 64
WROWS = 128
START = 8128


def first_table(inner):
    index = jnp.arange(inner, dtype=jnp.int32)
    phase = index[:, None] * index[None, :] % inner
    angle = phase.astype(jnp.float32) * (2.0 * math.pi / inner)
    cosine = jnp.cos(angle).astype(jnp.bfloat16)
    sine = jnp.sin(angle).astype(jnp.bfloat16)
    upper = jnp.concatenate([cosine, -sine], axis=1)
    lower = jnp.concatenate([sine, cosine], axis=1)
    return jnp.concatenate([upper, lower], axis=0)


def wave_block(freqs, lags, period):
    phase = freqs[:, None] * lags[None, :] % period
    angle = phase.astype(jnp.float32) * (2.0 * math.pi / period)
    cosine = jnp.cos(angle).astype(jnp.bfloat16)
    sine = jnp.sin(angle).astype(jnp.bfloat16)
    upper = jnp.concatenate([cosine, sine], axis=1)
    lower = jnp.concatenate([-sine, cosine], axis=1)
    return jnp.concatenate([upper, lower], axis=0)


def twist_tables(freqs, inner, total):
    rows_index = jnp.arange(inner, dtype=jnp.int32)
    phase = rows_index[:, None] * freqs[None, :] % total
    angle = phase.astype(jnp.float32) * (2.0 * math.pi / total)
    return (jnp.cos(angle), jnp.sin(angle))


MESH = pl.DeviceIdType.MESH


def greet(axis, n, other):
    me = lax.axis_index(axis)
    barrier = pltpu.get_barrier_semaphore()
    for step in range(1, n):
        peer = (me + step) % n
        pl.semaphore_signal(barrier, inc=1, device_id=other(peer), device_id_type=MESH)
    pl.semaphore_wait(barrier, n - 1)
    return me


def scatter_sum_kernel(n, x_ref, o_ref, slots, send_sem, recv_sem):
    bank = lax.axis_index("bank")
    place = lambda peer: (peer, bank)
    me = greet("tm", n, place)
    rows = o_ref.shape[0]
    sends = []
    for step in range(1, n):
        peer = (me + step) % n
        copy = pltpu.make_async_remote_copy(
            src_ref=x_ref.at[pl.ds(peer * rows, rows)],
            dst_ref=slots.at[me],
            send_sem=send_sem.at[peer],
            recv_sem=recv_sem.at[me],
            device_id=place(peer),
            device_id_type=MESH,
        )
        copy.start()
        sends.append(copy)
    total = x_ref[pl.ds(me * rows, rows)]
    for step in range(1, n):
        source = (me + n - step) % n
        pltpu.make_async_remote_copy(
            src_ref=x_ref.at[pl.ds(0, rows)],
            dst_ref=slots.at[source],
            send_sem=send_sem.at[source],
            recv_sem=recv_sem.at[source],
            device_id=place(source),
            device_id_type=MESH,
        ).wait_recv()
        total = total + slots[source]
    for copy in sends:
        copy.wait_send()
    o_ref[...] = total.astype(o_ref.dtype)


def scatter_sum(x, n):
    rows = x.shape[0] // n
    shape = (rows,) + x.shape[1:]
    return pl.pallas_call(
        functools.partial(scatter_sum_kernel, n),
        out_shape=jax.ShapeDtypeStruct(shape, jnp.bfloat16),
        in_specs=[pl.BlockSpec(memory_space=pltpu.VMEM)],
        out_specs=pl.BlockSpec(memory_space=pltpu.VMEM),
        scratch_shapes=[
            pltpu.VMEM((n,) + shape, x.dtype),
            pltpu.SemaphoreType.DMA((n,)),
            pltpu.SemaphoreType.DMA((n,)),
        ],
        compiler_params=pltpu.CompilerParams(collective_id=0, has_side_effects=True),
    )(x)


def gather_kernel(n, x_ref, o_ref, send_sem, recv_sem):
    tm = lax.axis_index("tm")
    place = lambda peer: (tm, peer)
    me = greet("bank", n, place)
    sends = []
    for step in range(1, n):
        peer = (me + step) % n
        copy = pltpu.make_async_remote_copy(
            src_ref=x_ref,
            dst_ref=o_ref.at[me],
            send_sem=send_sem.at[peer],
            recv_sem=recv_sem.at[me],
            device_id=place(peer),
            device_id_type=MESH,
        )
        copy.start()
        sends.append(copy)
    o_ref[me] = x_ref[...]
    for step in range(1, n):
        source = (me + n - step) % n
        pltpu.make_async_remote_copy(
            src_ref=x_ref,
            dst_ref=o_ref.at[source],
            send_sem=send_sem.at[source],
            recv_sem=recv_sem.at[source],
            device_id=place(source),
            device_id_type=MESH,
        ).wait_recv()
    for copy in sends:
        copy.wait_send()


def gather(x, n):
    return pl.pallas_call(
        functools.partial(gather_kernel, n),
        out_shape=jax.ShapeDtypeStruct((n,) + x.shape, x.dtype),
        in_specs=[pl.BlockSpec(memory_space=pltpu.VMEM)],
        out_specs=pl.BlockSpec(memory_space=pltpu.VMEM),
        scratch_shapes=[
            pltpu.SemaphoreType.DMA((n,)),
            pltpu.SemaphoreType.DMA((n,)),
        ],
        compiler_params=pltpu.CompilerParams(collective_id=1, has_side_effects=True),
    )(x)


def on_device(spectrum, filters, mixing):
    tm_index = lax.axis_index("tm")
    local_freq = filters.shape[3]
    local_basis = filters.shape[1]
    inner = INNER
    outer = NSAMP // INNER
    table = first_table(inner)
    freqs = tm_index * local_freq + jnp.arange(local_freq, dtype=jnp.int32)
    twist_cos, twist_sin = twist_tables(freqs, inner, NSAMP)
    filt_real = filters[0].astype(jnp.float32)
    filt_imag = filters[1].astype(jnp.float32)
    prod_real = spectrum[0] * filt_real + spectrum[1] * filt_imag
    prod_imag = spectrum[1] * filt_real - spectrum[0] * filt_imag
    packed = jnp.concatenate([prod_real, prod_imag], axis=1).astype(jnp.bfloat16)
    section = jnp.einsum("uv,kvf->kuf", table, packed, preferred_element_type=jnp.float32)
    section_real = section[:, :inner]
    section_imag = section[:, inner:]
    quarter_real = (section_real * twist_cos - section_imag * twist_sin).astype(jnp.bfloat16)
    quarter_imag = (section_real * twist_sin + section_imag * twist_cos).astype(jnp.bfloat16)
    quarter = jnp.concatenate([quarter_real, quarter_imag], axis=2)
    lags = START + jnp.arange(WROWS, dtype=jnp.int32)
    wave = wave_block(freqs, lags, outer)
    partial = jnp.einsum("ktf,fs->tks", quarter, wave, preferred_element_type=jnp.float32)
    series = scatter_sum(partial, lax.axis_size("tm"))
    piece = gather(series, lax.axis_size("bank"))
    groups = piece.shape[0]
    rows = piece.shape[1]
    piece_real = piece[..., :WROWS]
    piece_imag = piece[..., WROWS:]
    templates = mixing.shape[1]
    mix_real = mixing[0].reshape(templates, groups, local_basis)
    mix_imag = mixing[1].reshape(templates, groups, local_basis)
    real_sum = jnp.einsum(
        "jgk,gtks->tjs", mix_real, piece_real, preferred_element_type=jnp.float32
    ) - jnp.einsum("jgk,gtks->tjs", mix_imag, piece_imag, preferred_element_type=jnp.float32)
    imag_sum = jnp.einsum(
        "jgk,gtks->tjs", mix_real, piece_imag, preferred_element_type=jnp.float32
    ) + jnp.einsum("jgk,gtks->tjs", mix_imag, piece_real, preferred_element_type=jnp.float32)
    del rows
    return jnp.stack([real_sum, imag_sum], axis=0).astype(jnp.bfloat16)


def solution(mesh):
    return jax.shard_map(
        on_device,
        mesh=mesh,
        in_specs=(P(None, None, "tm"), P(None, "bank", None, "tm"), P(None, "bank", None)),
        out_specs=P(None, "tm", "bank", None),
        check_vma=False,
    )
```

```python
import functools
import math

import jax
import jax.numpy as jnp
from jax import lax
from jax.experimental import pallas as pl
from jax.experimental.pallas import tpu as pltpu
from jax.sharding import PartitionSpec as P

NSAMP = 1048576
INNER = 64
WROWS = 128
START = 8128


def first_table(inner):
    index = jnp.arange(inner, dtype=jnp.int32)
    phase = index[:, None] * index[None, :] % inner
    angle = phase.astype(jnp.float32) * (2.0 * math.pi / inner)
    cosine = jnp.cos(angle).astype(jnp.bfloat16)
    sine = jnp.sin(angle).astype(jnp.bfloat16)
    upper = jnp.concatenate([cosine, -sine], axis=1)
    lower = jnp.concatenate([sine, cosine], axis=1)
    return jnp.concatenate([upper, lower], axis=0)


def wave_block(freqs, lags, period):
    phase = freqs[:, None] * lags[None, :] % period
    angle = phase.astype(jnp.float32) * (2.0 * math.pi / period)
    cosine = jnp.cos(angle).astype(jnp.bfloat16)
    sine = jnp.sin(angle).astype(jnp.bfloat16)
    upper = jnp.concatenate([cosine, sine], axis=1)
    lower = jnp.concatenate([-sine, cosine], axis=1)
    return jnp.concatenate([upper, lower], axis=0)


def twist_tables(freqs, inner, total):
    rows_index = jnp.arange(inner, dtype=jnp.int32)
    phase = rows_index[:, None] * freqs[None, :] % total
    angle = phase.astype(jnp.float32) * (2.0 * math.pi / total)
    return (jnp.cos(angle), jnp.sin(angle))


MESH = pl.DeviceIdType.MESH


def greet(axis, n, other):
    me = lax.axis_index(axis)
    barrier = pltpu.get_barrier_semaphore()
    for step in range(1, n):
        peer = (me + step) % n
        pl.semaphore_signal(barrier, inc=1, device_id=other(peer), device_id_type=MESH)
    pl.semaphore_wait(barrier, n - 1)
    return me


def scatter_sum_kernel(n, x_ref, o_ref, slots, send_sem, recv_sem):
    bank = lax.axis_index("bank")
    place = lambda peer: (peer, bank)
    me = greet("tm", n, place)
    rows = o_ref.shape[0]
    sends = []
    for step in range(1, n):
        peer = (me + step) % n
        copy = pltpu.make_async_remote_copy(
            src_ref=x_ref.at[pl.ds(peer * rows, rows)],
            dst_ref=slots.at[me],
            send_sem=send_sem.at[peer],
            recv_sem=recv_sem.at[me],
            device_id=place(peer),
            device_id_type=MESH,
        )
        copy.start()
        sends.append(copy)
    total = x_ref[pl.ds(me * rows, rows)]
    for step in range(1, n):
        source = (me + n - step) % n
        pltpu.make_async_remote_copy(
            src_ref=x_ref.at[pl.ds(0, rows)],
            dst_ref=slots.at[source],
            send_sem=send_sem.at[source],
            recv_sem=recv_sem.at[source],
            device_id=place(source),
            device_id_type=MESH,
        ).wait_recv()
        total = total + slots[source]
    for copy in sends:
        copy.wait_send()
    o_ref[...] = total.astype(o_ref.dtype)


def scatter_sum(x, n):
    rows = x.shape[0] // n
    shape = (rows,) + x.shape[1:]
    return pl.pallas_call(
        functools.partial(scatter_sum_kernel, n),
        out_shape=jax.ShapeDtypeStruct(shape, jnp.bfloat16),
        in_specs=[pl.BlockSpec(memory_space=pltpu.VMEM)],
        out_specs=pl.BlockSpec(memory_space=pltpu.VMEM),
        scratch_shapes=[
            pltpu.VMEM((n,) + shape, x.dtype),
            pltpu.SemaphoreType.DMA((n,)),
            pltpu.SemaphoreType.DMA((n,)),
        ],
        compiler_params=pltpu.CompilerParams(collective_id=0, has_side_effects=True),
    )(x)


def gather_kernel(n, x_ref, o_ref, send_sem, recv_sem):
    tm = lax.axis_index("tm")
    place = lambda peer: (tm, peer)
    me = greet("bank", n, place)
    sends = []
    for step in range(1, n):
        peer = (me + step) % n
        copy = pltpu.make_async_remote_copy(
            src_ref=x_ref,
            dst_ref=o_ref.at[me],
            send_sem=send_sem.at[peer],
            recv_sem=recv_sem.at[me],
            device_id=place(peer),
            device_id_type=MESH,
        )
        copy.start()
        sends.append(copy)
    o_ref[me] = x_ref[...]
    for step in range(1, n):
        source = (me + n - step) % n
        pltpu.make_async_remote_copy(
            src_ref=x_ref,
            dst_ref=o_ref.at[source],
            send_sem=send_sem.at[source],
            recv_sem=recv_sem.at[source],
            device_id=place(source),
            device_id_type=MESH,
        ).wait_recv()
    for copy in sends:
        copy.wait_send()


def gather(x, n):
    return pl.pallas_call(
        functools.partial(gather_kernel, n),
        out_shape=jax.ShapeDtypeStruct((n,) + x.shape, x.dtype),
        in_specs=[pl.BlockSpec(memory_space=pltpu.VMEM)],
        out_specs=pl.BlockSpec(memory_space=pltpu.VMEM),
        scratch_shapes=[
            pltpu.SemaphoreType.DMA((n,)),
            pltpu.SemaphoreType.DMA((n,)),
        ],
        compiler_params=pltpu.CompilerParams(collective_id=1, has_side_effects=True),
    )(x)


def front_kernel(spec_ref, filt_ref, table_ref, tcos_ref, tsin_ref, wave_ref, o_ref, quarter):
    block, inner = filt_ref.shape[1], filt_ref.shape[2]
    spec_real = spec_ref[0]
    spec_imag = spec_ref[1]
    table = table_ref[...]
    twist_cos = tcos_ref[...]
    twist_sin = tsin_ref[...]
    for kk in range(block):
        filt_real = filt_ref[0, kk].astype(jnp.float32)
        filt_imag = filt_ref[1, kk].astype(jnp.float32)
        prod_real = spec_real * filt_real + spec_imag * filt_imag
        prod_imag = spec_imag * filt_real - spec_real * filt_imag
        packed = jnp.concatenate([prod_real, prod_imag], axis=0).astype(jnp.bfloat16)
        section = jnp.dot(table, packed, preferred_element_type=jnp.float32)
        section_real = section[:inner]
        section_imag = section[inner:]
        quarter_real = section_real * twist_cos - section_imag * twist_sin
        quarter_imag = section_real * twist_sin + section_imag * twist_cos
        width = quarter_real.shape[1]
        rows = pl.ds(kk * inner, inner)
        quarter[rows, pl.ds(0, width)] = quarter_real.astype(jnp.bfloat16)
        quarter[rows, pl.ds(width, width)] = quarter_imag.astype(jnp.bfloat16)
    result = jnp.dot(quarter[...], wave_ref[...], preferred_element_type=jnp.float32)
    o_ref[...] = result.reshape(o_ref.shape)


def front(spectrum, filters, table, twist_cos, twist_sin, wave, block=8):
    _, basis, inner, freq = filters.shape
    cols = wave.shape[1]
    whole = lambda *shape: pl.BlockSpec(shape, lambda i: (0,) * len(shape))
    return pl.pallas_call(
        front_kernel,
        grid=(basis // block,),
        out_shape=jax.ShapeDtypeStruct((basis, inner, cols), jnp.float32),
        in_specs=[
            whole(2, inner, freq),
            pl.BlockSpec((2, block, inner, freq), lambda i: (0, i, 0, 0)),
            whole(2 * inner, 2 * inner),
            whole(inner, freq),
            whole(inner, freq),
            whole(2 * freq, cols),
        ],
        out_specs=pl.BlockSpec((block, inner, cols), lambda i: (i, 0, 0)),
        scratch_shapes=[pltpu.VMEM((block * inner, 2 * freq), jnp.bfloat16)],
        compiler_params=pltpu.CompilerParams(vmem_limit_bytes=48 * 1024 * 1024),
    )(spectrum, filters, table, twist_cos, twist_sin, wave)


def on_device(spectrum, filters, mixing):
    tm_index = lax.axis_index("tm")
    local_freq = filters.shape[3]
    local_basis = filters.shape[1]
    inner = INNER
    outer = NSAMP // INNER
    table = first_table(inner)
    freqs = tm_index * local_freq + jnp.arange(local_freq, dtype=jnp.int32)
    twist_cos, twist_sin = twist_tables(freqs, inner, NSAMP)
    lags = START + jnp.arange(WROWS, dtype=jnp.int32)
    wave = wave_block(freqs, lags, outer)
    partial = front(spectrum, filters, table, twist_cos, twist_sin, wave).transpose(1, 0, 2)
    series = scatter_sum(partial, lax.axis_size("tm"))
    piece = gather(series, lax.axis_size("bank"))
    groups = piece.shape[0]
    rows = piece.shape[1]
    piece_real = piece[..., :WROWS]
    piece_imag = piece[..., WROWS:]
    templates = mixing.shape[1]
    mix_real = mixing[0].reshape(templates, groups, local_basis)
    mix_imag = mixing[1].reshape(templates, groups, local_basis)
    real_sum = jnp.einsum(
        "jgk,gtks->tjs", mix_real, piece_real, preferred_element_type=jnp.float32
    ) - jnp.einsum("jgk,gtks->tjs", mix_imag, piece_imag, preferred_element_type=jnp.float32)
    imag_sum = jnp.einsum(
        "jgk,gtks->tjs", mix_real, piece_imag, preferred_element_type=jnp.float32
    ) + jnp.einsum("jgk,gtks->tjs", mix_imag, piece_real, preferred_element_type=jnp.float32)
    del rows
    return jnp.stack([real_sum, imag_sum], axis=0).astype(jnp.bfloat16)


def solution(mesh):
    return jax.shard_map(
        on_device,
        mesh=mesh,
        in_specs=(P(None, None, "tm"), P(None, "bank", None, "tm"), P(None, "bank", None)),
        out_specs=P(None, "tm", "bank", None),
        check_vma=False,
    )
```

```python
import functools
import math

import jax
import jax.numpy as jnp
from jax import lax
from jax.experimental import pallas as pl
from jax.experimental.pallas import tpu as pltpu
from jax.sharding import PartitionSpec as P

NSAMP = 1048576
INNER = 64
WROWS = 128
START = 8128


def first_table(inner):
    index = jnp.arange(inner, dtype=jnp.int32)
    phase = index[:, None] * index[None, :] % inner
    angle = phase.astype(jnp.float32) * (2.0 * math.pi / inner)
    cosine = jnp.cos(angle).astype(jnp.bfloat16)
    sine = jnp.sin(angle).astype(jnp.bfloat16)
    upper = jnp.concatenate([cosine, -sine], axis=1)
    lower = jnp.concatenate([sine, cosine], axis=1)
    return jnp.concatenate([upper, lower], axis=0)


def wave_block(freqs, lags, period):
    phase = freqs[:, None] * lags[None, :] % period
    angle = phase.astype(jnp.float32) * (2.0 * math.pi / period)
    cosine = jnp.cos(angle).astype(jnp.bfloat16)
    sine = jnp.sin(angle).astype(jnp.bfloat16)
    upper = jnp.concatenate([cosine, sine], axis=1)
    lower = jnp.concatenate([-sine, cosine], axis=1)
    return jnp.concatenate([upper, lower], axis=0)


def twist_tables(freqs, inner, total):
    rows_index = jnp.arange(inner, dtype=jnp.int32)
    phase = rows_index[:, None] * freqs[None, :] % total
    angle = phase.astype(jnp.float32) * (2.0 * math.pi / total)
    return (jnp.cos(angle), jnp.sin(angle))


MESH = pl.DeviceIdType.MESH


def greet(axis, n, other):
    me = lax.axis_index(axis)
    barrier = pltpu.get_barrier_semaphore()
    for step in range(1, n):
        peer = (me + step) % n
        pl.semaphore_signal(barrier, inc=1, device_id=other(peer), device_id_type=MESH)
    pl.semaphore_wait(barrier, n - 1)
    return me


def scatter_sum_kernel(n, x_ref, o_ref, slots, send_sem, recv_sem):
    bank = lax.axis_index("bank")
    place = lambda peer: (peer, bank)
    me = greet("tm", n, place)
    rows = o_ref.shape[0]
    sends = []
    for step in range(1, n):
        peer = (me + step) % n
        copy = pltpu.make_async_remote_copy(
            src_ref=x_ref.at[pl.ds(peer * rows, rows)],
            dst_ref=slots.at[me],
            send_sem=send_sem.at[peer],
            recv_sem=recv_sem.at[me],
            device_id=place(peer),
            device_id_type=MESH,
        )
        copy.start()
        sends.append(copy)
    total = x_ref[pl.ds(me * rows, rows)].astype(jnp.float32)
    for step in range(1, n):
        source = (me + n - step) % n
        pltpu.make_async_remote_copy(
            src_ref=x_ref.at[pl.ds(0, rows)],
            dst_ref=slots.at[source],
            send_sem=send_sem.at[source],
            recv_sem=recv_sem.at[source],
            device_id=place(source),
            device_id_type=MESH,
        ).wait_recv()
        total = total + slots[source].astype(jnp.float32)
    for copy in sends:
        copy.wait_send()
    o_ref[...] = total.astype(o_ref.dtype)


def scatter_sum(x, n):
    rows = x.shape[0] // n
    shape = (rows,) + x.shape[1:]
    return pl.pallas_call(
        functools.partial(scatter_sum_kernel, n),
        out_shape=jax.ShapeDtypeStruct(shape, jnp.bfloat16),
        in_specs=[pl.BlockSpec(memory_space=pltpu.VMEM)],
        out_specs=pl.BlockSpec(memory_space=pltpu.VMEM),
        scratch_shapes=[
            pltpu.VMEM((n,) + shape, x.dtype),
            pltpu.SemaphoreType.DMA((n,)),
            pltpu.SemaphoreType.DMA((n,)),
        ],
        compiler_params=pltpu.CompilerParams(collective_id=0, has_side_effects=True),
    )(x)


def gather_kernel(n, x_ref, o_ref, send_sem, recv_sem):
    tm = lax.axis_index("tm")
    place = lambda peer: (tm, peer)
    me = greet("bank", n, place)
    sends = []
    for step in range(1, n):
        peer = (me + step) % n
        copy = pltpu.make_async_remote_copy(
            src_ref=x_ref,
            dst_ref=o_ref.at[me],
            send_sem=send_sem.at[peer],
            recv_sem=recv_sem.at[me],
            device_id=place(peer),
            device_id_type=MESH,
        )
        copy.start()
        sends.append(copy)
    o_ref[me] = x_ref[...]
    for step in range(1, n):
        source = (me + n - step) % n
        pltpu.make_async_remote_copy(
            src_ref=x_ref,
            dst_ref=o_ref.at[source],
            send_sem=send_sem.at[source],
            recv_sem=recv_sem.at[source],
            device_id=place(source),
            device_id_type=MESH,
        ).wait_recv()
    for copy in sends:
        copy.wait_send()


def gather(x, n):
    return pl.pallas_call(
        functools.partial(gather_kernel, n),
        out_shape=jax.ShapeDtypeStruct((n,) + x.shape, x.dtype),
        in_specs=[pl.BlockSpec(memory_space=pltpu.VMEM)],
        out_specs=pl.BlockSpec(memory_space=pltpu.VMEM),
        scratch_shapes=[
            pltpu.SemaphoreType.DMA((n,)),
            pltpu.SemaphoreType.DMA((n,)),
        ],
        compiler_params=pltpu.CompilerParams(collective_id=1, has_side_effects=True),
    )(x)


def front_kernel(spec_ref, filt_ref, table_ref, tcos_ref, tsin_ref, wave_ref, o_ref, quarter):
    block, inner = filt_ref.shape[1], filt_ref.shape[2]
    spec_real = spec_ref[0]
    spec_imag = spec_ref[1]
    table = table_ref[...]
    twist_cos = tcos_ref[...]
    twist_sin = tsin_ref[...]
    for kk in range(block):
        filt_real = filt_ref[0, kk].astype(jnp.float32)
        filt_imag = filt_ref[1, kk].astype(jnp.float32)
        prod_real = spec_real * filt_real + spec_imag * filt_imag
        prod_imag = spec_imag * filt_real - spec_real * filt_imag
        packed = jnp.concatenate([prod_real, prod_imag], axis=0).astype(jnp.bfloat16)
        section = jnp.dot(table, packed, preferred_element_type=jnp.float32)
        section_real = section[:inner]
        section_imag = section[inner:]
        quarter_real = section_real * twist_cos - section_imag * twist_sin
        quarter_imag = section_real * twist_sin + section_imag * twist_cos
        width = quarter_real.shape[1]
        rows = pl.ds(kk * inner, inner)
        quarter[rows, pl.ds(0, width)] = quarter_real.astype(jnp.bfloat16)
        quarter[rows, pl.ds(width, width)] = quarter_imag.astype(jnp.bfloat16)
    result = jnp.dot(quarter[...], wave_ref[...], preferred_element_type=jnp.float32)
    o_ref[...] = result.reshape(o_ref.shape).astype(o_ref.dtype)


def front(spectrum, filters, table, twist_cos, twist_sin, wave, block=8):
    _, basis, inner, freq = filters.shape
    cols = wave.shape[1]
    whole = lambda *shape: pl.BlockSpec(shape, lambda i: (0,) * len(shape))
    return pl.pallas_call(
        front_kernel,
        grid=(basis // block,),
        out_shape=jax.ShapeDtypeStruct((basis, inner, cols), jnp.bfloat16),
        in_specs=[
            whole(2, inner, freq),
            pl.BlockSpec((2, block, inner, freq), lambda i: (0, i, 0, 0)),
            whole(2 * inner, 2 * inner),
            whole(inner, freq),
            whole(inner, freq),
            whole(2 * freq, cols),
        ],
        out_specs=pl.BlockSpec((block, inner, cols), lambda i: (i, 0, 0)),
        scratch_shapes=[pltpu.VMEM((block * inner, 2 * freq), jnp.bfloat16)],
        compiler_params=pltpu.CompilerParams(vmem_limit_bytes=48 * 1024 * 1024),
    )(spectrum, filters, table, twist_cos, twist_sin, wave)


def on_device(spectrum, filters, mixing):
    tm_index = lax.axis_index("tm")
    local_freq = filters.shape[3]
    local_basis = filters.shape[1]
    inner = INNER
    outer = NSAMP // INNER
    table = first_table(inner)
    freqs = tm_index * local_freq + jnp.arange(local_freq, dtype=jnp.int32)
    twist_cos, twist_sin = twist_tables(freqs, inner, NSAMP)
    lags = START + jnp.arange(WROWS, dtype=jnp.int32)
    wave = wave_block(freqs, lags, outer)
    partial = front(spectrum, filters, table, twist_cos, twist_sin, wave).transpose(1, 0, 2)
    series = scatter_sum(partial, lax.axis_size("tm"))
    piece = gather(series, lax.axis_size("bank"))
    groups = piece.shape[0]
    rows = piece.shape[1]
    piece_real = piece[..., :WROWS]
    piece_imag = piece[..., WROWS:]
    templates = mixing.shape[1]
    mix_real = mixing[0].reshape(templates, groups, local_basis)
    mix_imag = mixing[1].reshape(templates, groups, local_basis)
    real_sum = jnp.einsum(
        "jgk,gtks->tjs", mix_real, piece_real, preferred_element_type=jnp.float32
    ) - jnp.einsum("jgk,gtks->tjs", mix_imag, piece_imag, preferred_element_type=jnp.float32)
    imag_sum = jnp.einsum(
        "jgk,gtks->tjs", mix_real, piece_imag, preferred_element_type=jnp.float32
    ) + jnp.einsum("jgk,gtks->tjs", mix_imag, piece_real, preferred_element_type=jnp.float32)
    del rows
    return jnp.stack([real_sum, imag_sum], axis=0).astype(jnp.bfloat16)


def solution(mesh):
    return jax.shard_map(
        on_device,
        mesh=mesh,
        in_specs=(P(None, None, "tm"), P(None, "bank", None, "tm"), P(None, "bank", None)),
        out_specs=P(None, "tm", "bank", None),
        check_vma=False,
    )
```

```python
import functools
import math

import jax
import jax.numpy as jnp
from jax import lax
from jax.experimental import pallas as pl
from jax.experimental.pallas import tpu as pltpu
from jax.sharding import PartitionSpec as P

NSAMP = 1048576
INNER = 64
WROWS = 128
START = 8128


def first_table(inner):
    index = jnp.arange(inner, dtype=jnp.int32)
    phase = index[:, None] * index[None, :] % inner
    angle = phase.astype(jnp.float32) * (2.0 * math.pi / inner)
    cosine = jnp.cos(angle).astype(jnp.bfloat16)
    sine = jnp.sin(angle).astype(jnp.bfloat16)
    upper = jnp.concatenate([cosine, -sine], axis=1)
    lower = jnp.concatenate([sine, cosine], axis=1)
    return jnp.concatenate([upper, lower], axis=0)


def wave_block(freqs, lags, period):
    phase = freqs[:, None] * lags[None, :] % period
    angle = phase.astype(jnp.float32) * (2.0 * math.pi / period)
    cosine = jnp.cos(angle).astype(jnp.bfloat16)
    sine = jnp.sin(angle).astype(jnp.bfloat16)
    upper = jnp.concatenate([cosine, sine], axis=1)
    lower = jnp.concatenate([-sine, cosine], axis=1)
    return jnp.concatenate([upper, lower], axis=0)


def twist_tables(freqs, inner, total):
    rows_index = jnp.arange(inner, dtype=jnp.int32)
    phase = rows_index[:, None] * freqs[None, :] % total
    angle = phase.astype(jnp.float32) * (2.0 * math.pi / total)
    return (jnp.cos(angle), jnp.sin(angle))


MESH = pl.DeviceIdType.MESH


def greet(axis, n, other):
    me = lax.axis_index(axis)
    barrier = pltpu.get_barrier_semaphore()
    for step in range(1, n):
        peer = (me + step) % n
        pl.semaphore_signal(barrier, inc=1, device_id=other(peer), device_id_type=MESH)
    pl.semaphore_wait(barrier, n - 1)
    return me


def scatter_sum_kernel(n, x_ref, o_ref, slots, send_sem, recv_sem):
    bank = lax.axis_index("bank")
    place = lambda peer: (peer, bank)
    me = greet("tm", n, place)
    rows = o_ref.shape[0]
    sends = []
    for step in range(1, n):
        peer = (me + step) % n
        copy = pltpu.make_async_remote_copy(
            src_ref=x_ref.at[pl.ds(peer * rows, rows)],
            dst_ref=slots.at[me],
            send_sem=send_sem.at[peer],
            recv_sem=recv_sem.at[me],
            device_id=place(peer),
            device_id_type=MESH,
        )
        copy.start()
        sends.append(copy)
    total = x_ref[pl.ds(me * rows, rows)].astype(jnp.float32)
    for step in range(1, n):
        source = (me + n - step) % n
        pltpu.make_async_remote_copy(
            src_ref=x_ref.at[pl.ds(0, rows)],
            dst_ref=slots.at[source],
            send_sem=send_sem.at[source],
            recv_sem=recv_sem.at[source],
            device_id=place(source),
            device_id_type=MESH,
        ).wait_recv()
        total = total + slots[source].astype(jnp.float32)
    for copy in sends:
        copy.wait_send()
    o_ref[...] = total.astype(o_ref.dtype)


def scatter_sum(x, n):
    rows = x.shape[0] // n
    shape = (rows,) + x.shape[1:]
    return pl.pallas_call(
        functools.partial(scatter_sum_kernel, n),
        out_shape=jax.ShapeDtypeStruct(shape, jnp.bfloat16),
        in_specs=[pl.BlockSpec(memory_space=pltpu.VMEM)],
        out_specs=pl.BlockSpec(memory_space=pltpu.VMEM),
        scratch_shapes=[
            pltpu.VMEM((n,) + shape, x.dtype),
            pltpu.SemaphoreType.DMA((n,)),
            pltpu.SemaphoreType.DMA((n,)),
        ],
        compiler_params=pltpu.CompilerParams(collective_id=0, has_side_effects=True),
    )(x)


def gather_kernel(width, x_ref, o_ref, own_sem, send_sem, recv_sem):
    n = lax.axis_size("bank")
    depth = n // width
    half = width // 2
    tm = lax.axis_index("tm")
    bank = lax.axis_index("bank")
    x = bank // depth
    z = bank % depth
    up = (z + 1) % depth
    down = (z + depth - 1) % depth
    across = (z + 2) % depth
    place = lambda xx, zz: (tm, xx * depth + zz)
    peers = [place((x + d) % width, z) for d in range(1, width)] + [place(x, up), place(x, down)]
    barrier = pltpu.get_barrier_semaphore()
    for peer in peers:
        pl.semaphore_signal(barrier, inc=1, device_id=peer, device_id_type=MESH)
    pl.semaphore_wait(barrier, len(peers))

    def remote(src, dst, send, recv, device):
        return pltpu.make_async_remote_copy(
            src_ref=src, dst_ref=dst, send_sem=send_sem.at[send], recv_sem=recv_sem.at[recv],
            device_id=device, device_id_type=MESH,
        )

    own = pltpu.make_async_copy(x_ref, o_ref.at[z * width + x], own_sem)
    own.start()
    sends = []
    for d in range(1, width):
        xx = (x + d) % width
        copy = remote(x_ref, o_ref.at[z * width + x], d - 1, x, place(xx, z))
        copy.start()
        sends.append(copy)
    own.wait()
    for d in range(1, width):
        xx = (x + d) % width
        remote(x_ref, o_ref.at[z * width + xx], d - 1, xx, place(xx, z)).wait_recv()
    row = lambda zz, start, size: o_ref.at[pl.ds(zz * width + start, size)]
    for slot, (target, step) in enumerate(((up, width - 1), (down, width))):
        copy = remote(row(z, 0, width), row(z, 0, width), step, width + slot, place(x, target))
        copy.start()
        sends.append(copy)
    remote(row(down, 0, width), row(down, 0, width), width - 1, width, place(x, down)).wait_recv()
    remote(row(up, 0, width), row(up, 0, width), width, width + 1, place(x, up)).wait_recv()
    forwards = (
        (row(down, 0, half), up, width + 1, width + 2),
        (row(up, half, half), down, width + 2, width + 3),
    )
    for src, target, send, recv in forwards:
        copy = remote(src, src, send, recv, place(x, target))
        copy.start()
        sends.append(copy)
    remote(row(across, 0, half), row(across, 0, half), width + 1, width + 2, place(x, down)).wait_recv()
    remote(row(across, half, half), row(across, half, half), width + 2, width + 3, place(x, up)).wait_recv()
    for copy in sends:
        copy.wait_send()


def gather(x, n, width):
    return pl.pallas_call(
        functools.partial(gather_kernel, width),
        out_shape=jax.ShapeDtypeStruct((n,) + x.shape, x.dtype),
        in_specs=[pl.BlockSpec(memory_space=pltpu.VMEM)],
        out_specs=pl.BlockSpec(memory_space=pltpu.VMEM),
        scratch_shapes=[
            pltpu.SemaphoreType.DMA(()),
            pltpu.SemaphoreType.DMA((width + 3,)),
            pltpu.SemaphoreType.DMA((width + 4,)),
        ],
        compiler_params=pltpu.CompilerParams(collective_id=1, has_side_effects=True),
    )(x)


def front_kernel(spec_ref, filt_ref, table_ref, tcos_ref, tsin_ref, wave_ref, o_ref, quarter):
    block, inner = filt_ref.shape[1], filt_ref.shape[2]
    spec_real = spec_ref[0]
    spec_imag = spec_ref[1]
    table = table_ref[...]
    twist_cos = tcos_ref[...]
    twist_sin = tsin_ref[...]
    for kk in range(block):
        filt_real = filt_ref[0, kk].astype(jnp.float32)
        filt_imag = filt_ref[1, kk].astype(jnp.float32)
        prod_real = spec_real * filt_real + spec_imag * filt_imag
        prod_imag = spec_imag * filt_real - spec_real * filt_imag
        packed = jnp.concatenate([prod_real, prod_imag], axis=0).astype(jnp.bfloat16)
        section = jnp.dot(table, packed, preferred_element_type=jnp.float32)
        section_real = section[:inner]
        section_imag = section[inner:]
        quarter_real = section_real * twist_cos - section_imag * twist_sin
        quarter_imag = section_real * twist_sin + section_imag * twist_cos
        width = quarter_real.shape[1]
        rows = pl.ds(kk * inner, inner)
        quarter[rows, pl.ds(0, width)] = quarter_real.astype(jnp.bfloat16)
        quarter[rows, pl.ds(width, width)] = quarter_imag.astype(jnp.bfloat16)
    result = jnp.dot(quarter[...], wave_ref[...], preferred_element_type=jnp.float32)
    o_ref[...] = result.reshape(o_ref.shape).astype(o_ref.dtype)


def front(spectrum, filters, table, twist_cos, twist_sin, wave, block=8):
    _, basis, inner, freq = filters.shape
    cols = wave.shape[1]
    whole = lambda *shape: pl.BlockSpec(shape, lambda i: (0,) * len(shape))
    return pl.pallas_call(
        front_kernel,
        grid=(basis // block,),
        out_shape=jax.ShapeDtypeStruct((basis, inner, cols), jnp.bfloat16),
        in_specs=[
            whole(2, inner, freq),
            pl.BlockSpec((2, block, inner, freq), lambda i: (0, i, 0, 0)),
            whole(2 * inner, 2 * inner),
            whole(inner, freq),
            whole(inner, freq),
            whole(2 * freq, cols),
        ],
        out_specs=pl.BlockSpec((block, inner, cols), lambda i: (i, 0, 0)),
        scratch_shapes=[pltpu.VMEM((block * inner, 2 * freq), jnp.bfloat16)],
        compiler_params=pltpu.CompilerParams(vmem_limit_bytes=48 * 1024 * 1024),
    )(spectrum, filters, table, twist_cos, twist_sin, wave)


def on_device(spectrum, filters, mixing):
    tm_index = lax.axis_index("tm")
    local_freq = filters.shape[3]
    local_basis = filters.shape[1]
    inner = INNER
    outer = NSAMP // INNER
    table = first_table(inner)
    freqs = tm_index * local_freq + jnp.arange(local_freq, dtype=jnp.int32)
    twist_cos, twist_sin = twist_tables(freqs, inner, NSAMP)
    lags = START + jnp.arange(WROWS, dtype=jnp.int32)
    wave = wave_block(freqs, lags, outer)
    partial = front(spectrum, filters, table, twist_cos, twist_sin, wave).transpose(1, 0, 2)
    series = scatter_sum(partial, lax.axis_size("tm"))
    width = 4
    slots = gather(series, lax.axis_size("bank"), width)
    depth = slots.shape[0] // width
    piece = slots.reshape((depth, width) + slots.shape[1:]).swapaxes(0, 1).reshape(slots.shape)
    groups = piece.shape[0]
    rows = piece.shape[1]
    piece_real = piece[..., :WROWS]
    piece_imag = piece[..., WROWS:]
    templates = mixing.shape[1]
    mix_real = mixing[0].reshape(templates, groups, local_basis)
    mix_imag = mixing[1].reshape(templates, groups, local_basis)
    real_sum = jnp.einsum(
        "jgk,gtks->tjs", mix_real, piece_real, preferred_element_type=jnp.float32
    ) - jnp.einsum("jgk,gtks->tjs", mix_imag, piece_imag, preferred_element_type=jnp.float32)
    imag_sum = jnp.einsum(
        "jgk,gtks->tjs", mix_real, piece_imag, preferred_element_type=jnp.float32
    ) + jnp.einsum("jgk,gtks->tjs", mix_imag, piece_real, preferred_element_type=jnp.float32)
    del rows
    return jnp.stack([real_sum, imag_sum], axis=0).astype(jnp.bfloat16)


def solution(mesh):
    return jax.shard_map(
        on_device,
        mesh=mesh,
        in_specs=(P(None, None, "tm"), P(None, "bank", None, "tm"), P(None, "bank", None)),
        out_specs=P(None, "tm", "bank", None),
        check_vma=False,
    )
```

```python
import functools
import math

import jax
import jax.numpy as jnp
from jax import lax
from jax.experimental import pallas as pl
from jax.experimental.pallas import tpu as pltpu
from jax.sharding import PartitionSpec as P

NSAMP = 1048576
INNER = 64
WROWS = 128
START = 8128


def first_table(inner):
    index = jnp.arange(inner, dtype=jnp.int32)
    phase = index[:, None] * index[None, :] % inner
    angle = phase.astype(jnp.float32) * (2.0 * math.pi / inner)
    cosine = jnp.cos(angle).astype(jnp.bfloat16)
    sine = jnp.sin(angle).astype(jnp.bfloat16)
    upper = jnp.concatenate([cosine, -sine], axis=1)
    lower = jnp.concatenate([sine, cosine], axis=1)
    return jnp.concatenate([upper, lower], axis=0)


def wave_block(freqs, lags, period):
    phase = freqs[:, None] * lags[None, :] % period
    angle = phase.astype(jnp.float32) * (2.0 * math.pi / period)
    cosine = jnp.cos(angle).astype(jnp.bfloat16)
    sine = jnp.sin(angle).astype(jnp.bfloat16)
    upper = jnp.concatenate([cosine, sine], axis=1)
    lower = jnp.concatenate([-sine, cosine], axis=1)
    return jnp.concatenate([upper, lower], axis=0)


def twist_tables(freqs, inner, total):
    rows_index = jnp.arange(inner, dtype=jnp.int32)
    phase = rows_index[:, None] * freqs[None, :] % total
    angle = phase.astype(jnp.float32) * (2.0 * math.pi / total)
    return (jnp.cos(angle), jnp.sin(angle))


MESH = pl.DeviceIdType.MESH


def greet(axis, n, other):
    me = lax.axis_index(axis)
    barrier = pltpu.get_barrier_semaphore()
    for step in range(1, n):
        peer = (me + step) % n
        pl.semaphore_signal(barrier, inc=1, device_id=other(peer), device_id_type=MESH)
    pl.semaphore_wait(barrier, n - 1)
    return me


def scatter_sum_kernel(n, x_ref, o_ref, slots, send_sem, recv_sem):
    bank = lax.axis_index("bank")
    place = lambda peer: (peer, bank)
    me = greet("tm", n, place)
    rows = o_ref.shape[0]
    sends = []
    for step in range(1, n):
        peer = (me + step) % n
        copy = pltpu.make_async_remote_copy(
            src_ref=x_ref.at[pl.ds(peer * rows, rows)],
            dst_ref=slots.at[me],
            send_sem=send_sem.at[peer],
            recv_sem=recv_sem.at[me],
            device_id=place(peer),
            device_id_type=MESH,
        )
        copy.start()
        sends.append(copy)
    total = x_ref[pl.ds(me * rows, rows)].astype(jnp.float32)
    for step in range(1, n):
        source = (me + n - step) % n
        pltpu.make_async_remote_copy(
            src_ref=x_ref.at[pl.ds(0, rows)],
            dst_ref=slots.at[source],
            send_sem=send_sem.at[source],
            recv_sem=recv_sem.at[source],
            device_id=place(source),
            device_id_type=MESH,
        ).wait_recv()
        total = total + slots[source].astype(jnp.float32)
    for copy in sends:
        copy.wait_send()
    o_ref[...] = total.astype(o_ref.dtype)


def scatter_sum(x, n):
    rows = x.shape[0] // n
    shape = (rows,) + x.shape[1:]
    return pl.pallas_call(
        functools.partial(scatter_sum_kernel, n),
        out_shape=jax.ShapeDtypeStruct(shape, jnp.bfloat16),
        in_specs=[pl.BlockSpec(memory_space=pltpu.VMEM)],
        out_specs=pl.BlockSpec(memory_space=pltpu.VMEM),
        scratch_shapes=[
            pltpu.VMEM((n,) + shape, x.dtype),
            pltpu.SemaphoreType.DMA((n,)),
            pltpu.SemaphoreType.DMA((n,)),
        ],
        compiler_params=pltpu.CompilerParams(collective_id=0, has_side_effects=True),
    )(x)


def gather_kernel(width, x_ref, o_ref, own_sem, send_sem, recv_sem):
    n = lax.axis_size("bank")
    depth = n // width
    half = width // 2
    tm = lax.axis_index("tm")
    bank = lax.axis_index("bank")
    x = bank // depth
    z = bank % depth
    up = (z + 1) % depth
    down = (z + depth - 1) % depth
    across = (z + 2) % depth
    place = lambda xx, zz: (tm, xx * depth + zz)
    peers = [place((x + d) % width, z) for d in range(1, width)] + [place(x, up), place(x, down)]
    barrier = pltpu.get_barrier_semaphore()
    for peer in peers:
        pl.semaphore_signal(barrier, inc=1, device_id=peer, device_id_type=MESH)
    pl.semaphore_wait(barrier, len(peers))

    def remote(src, dst, send, recv, device):
        return pltpu.make_async_remote_copy(
            src_ref=src, dst_ref=dst, send_sem=send_sem.at[send], recv_sem=recv_sem.at[recv],
            device_id=device, device_id_type=MESH,
        )

    own = pltpu.make_async_copy(x_ref, o_ref.at[z * width + x], own_sem)
    own.start()
    sends = []
    for d in range(1, width):
        xx = (x + d) % width
        copy = remote(x_ref, o_ref.at[z * width + x], d - 1, x, place(xx, z))
        copy.start()
        sends.append(copy)
    own.wait()
    for d in range(1, width):
        xx = (x + d) % width
        remote(x_ref, o_ref.at[z * width + xx], d - 1, xx, place(xx, z)).wait_recv()
    row = lambda zz, start, size: o_ref.at[pl.ds(zz * width + start, size)]
    for slot, (target, step) in enumerate(((up, width - 1), (down, width))):
        copy = remote(row(z, 0, width), row(z, 0, width), step, width + slot, place(x, target))
        copy.start()
        sends.append(copy)
    remote(row(down, 0, width), row(down, 0, width), width - 1, width, place(x, down)).wait_recv()
    remote(row(up, 0, width), row(up, 0, width), width, width + 1, place(x, up)).wait_recv()
    forwards = (
        (row(down, 0, half), up, width + 1, width + 2),
        (row(up, half, half), down, width + 2, width + 3),
    )
    for src, target, send, recv in forwards:
        copy = remote(src, src, send, recv, place(x, target))
        copy.start()
        sends.append(copy)
    remote(row(across, 0, half), row(across, 0, half), width + 1, width + 2, place(x, down)).wait_recv()
    remote(row(across, half, half), row(across, half, half), width + 2, width + 3, place(x, up)).wait_recv()
    for copy in sends:
        copy.wait_send()


def gather(x, n, width):
    return pl.pallas_call(
        functools.partial(gather_kernel, width),
        out_shape=jax.ShapeDtypeStruct((n,) + x.shape, x.dtype),
        in_specs=[pl.BlockSpec(memory_space=pltpu.VMEM)],
        out_specs=pl.BlockSpec(memory_space=pltpu.VMEM),
        scratch_shapes=[
            pltpu.SemaphoreType.DMA(()),
            pltpu.SemaphoreType.DMA((width + 3,)),
            pltpu.SemaphoreType.DMA((width + 4,)),
        ],
        compiler_params=pltpu.CompilerParams(collective_id=1, has_side_effects=True),
    )(x)


def mix_kernel(width, mix_ref, slots_ref, o_ref):
    n, rows, _, cols = slots_ref.shape
    depth = n // width
    half = cols // 2
    order = [z * width + x for x in range(width) for z in range(depth)]
    mix_real = mix_ref[0]
    mix_imag = mix_ref[1]
    for t in range(rows):
        plain = jnp.concatenate([slots_ref[slot, t] for slot in order], axis=0)
        turned = jnp.concatenate([-plain[:, half:], plain[:, :half]], axis=1)
        result = jnp.dot(mix_real, plain, preferred_element_type=jnp.float32) + jnp.dot(
            mix_imag, turned, preferred_element_type=jnp.float32
        )
        o_ref[0, t] = result[:, :half].astype(o_ref.dtype)
        o_ref[1, t] = result[:, half:].astype(o_ref.dtype)


def mix(mixing, slots, width):
    _, rows, _, cols = slots.shape
    templates = mixing.shape[1]
    return pl.pallas_call(
        functools.partial(mix_kernel, width),
        out_shape=jax.ShapeDtypeStruct((2, rows, templates, cols // 2), jnp.bfloat16),
        in_specs=[pl.BlockSpec(memory_space=pltpu.VMEM)] * 2,
        out_specs=pl.BlockSpec(memory_space=pltpu.VMEM),
    )(mixing, slots)


def front_kernel(spec_ref, filt_ref, table_ref, tcos_ref, tsin_ref, wave_ref, o_ref, quarter):
    block, inner = filt_ref.shape[1], filt_ref.shape[2]
    spec_real = spec_ref[0]
    spec_imag = spec_ref[1]
    table = table_ref[...]
    twist_cos = tcos_ref[...]
    twist_sin = tsin_ref[...]
    for kk in range(block):
        filt_real = filt_ref[0, kk].astype(jnp.float32)
        filt_imag = filt_ref[1, kk].astype(jnp.float32)
        prod_real = spec_real * filt_real + spec_imag * filt_imag
        prod_imag = spec_imag * filt_real - spec_real * filt_imag
        packed = jnp.concatenate([prod_real, prod_imag], axis=0).astype(jnp.bfloat16)
        section = jnp.dot(table, packed, preferred_element_type=jnp.float32)
        section_real = section[:inner]
        section_imag = section[inner:]
        quarter_real = section_real * twist_cos - section_imag * twist_sin
        quarter_imag = section_real * twist_sin + section_imag * twist_cos
        width = quarter_real.shape[1]
        rows = pl.ds(kk * inner, inner)
        quarter[rows, pl.ds(0, width)] = quarter_real.astype(jnp.bfloat16)
        quarter[rows, pl.ds(width, width)] = quarter_imag.astype(jnp.bfloat16)
    result = jnp.dot(quarter[...], wave_ref[...], preferred_element_type=jnp.float32)
    o_ref[...] = result.reshape(o_ref.shape).astype(o_ref.dtype)


def front(spectrum, filters, table, twist_cos, twist_sin, wave, block=8):
    _, basis, inner, freq = filters.shape
    cols = wave.shape[1]
    whole = lambda *shape: pl.BlockSpec(shape, lambda i: (0,) * len(shape))
    return pl.pallas_call(
        front_kernel,
        grid=(basis // block,),
        out_shape=jax.ShapeDtypeStruct((basis, inner, cols), jnp.bfloat16),
        in_specs=[
            whole(2, inner, freq),
            pl.BlockSpec((2, block, inner, freq), lambda i: (0, i, 0, 0)),
            whole(2 * inner, 2 * inner),
            whole(inner, freq),
            whole(inner, freq),
            whole(2 * freq, cols),
        ],
        out_specs=pl.BlockSpec((block, inner, cols), lambda i: (i, 0, 0)),
        scratch_shapes=[pltpu.VMEM((block * inner, 2 * freq), jnp.bfloat16)],
        compiler_params=pltpu.CompilerParams(vmem_limit_bytes=48 * 1024 * 1024),
    )(spectrum, filters, table, twist_cos, twist_sin, wave)


def on_device(spectrum, filters, mixing):
    tm_index = lax.axis_index("tm")
    local_freq = filters.shape[3]
    local_basis = filters.shape[1]
    inner = INNER
    outer = NSAMP // INNER
    table = first_table(inner)
    freqs = tm_index * local_freq + jnp.arange(local_freq, dtype=jnp.int32)
    twist_cos, twist_sin = twist_tables(freqs, inner, NSAMP)
    lags = START + jnp.arange(WROWS, dtype=jnp.int32)
    wave = wave_block(freqs, lags, outer)
    partial = front(spectrum, filters, table, twist_cos, twist_sin, wave).transpose(1, 0, 2)
    series = scatter_sum(partial, lax.axis_size("tm"))
    width = 4
    slots = gather(series, lax.axis_size("bank"), width)
    return mix(mixing, slots, width)


def solution(mesh):
    return jax.shard_map(
        on_device,
        mesh=mesh,
        in_specs=(P(None, None, "tm"), P(None, "bank", None, "tm"), P(None, "bank", None)),
        out_specs=P(None, "tm", "bank", None),
        check_vma=False,
    )
```

```python
import functools
import math

import jax
import jax.numpy as jnp
from jax import lax
from jax.experimental import pallas as pl
from jax.experimental.pallas import tpu as pltpu
from jax.sharding import PartitionSpec as P

NSAMP = 1048576
INNER = 64
WROWS = 128
START = 8128


def first_table(inner):
    index = jnp.arange(inner, dtype=jnp.int32)
    phase = index[:, None] * index[None, :] % inner
    angle = phase.astype(jnp.float32) * (2.0 * math.pi / inner)
    cosine = jnp.cos(angle).astype(jnp.bfloat16)
    sine = jnp.sin(angle).astype(jnp.bfloat16)
    upper = jnp.concatenate([cosine, -sine], axis=1)
    lower = jnp.concatenate([sine, cosine], axis=1)
    return jnp.concatenate([upper, lower], axis=0)


def wave_block(freqs, lags, period):
    phase = freqs[:, None] * lags[None, :] % period
    angle = phase.astype(jnp.float32) * (2.0 * math.pi / period)
    cosine = jnp.cos(angle).astype(jnp.bfloat16)
    sine = jnp.sin(angle).astype(jnp.bfloat16)
    upper = jnp.concatenate([cosine, sine], axis=1)
    lower = jnp.concatenate([-sine, cosine], axis=1)
    return jnp.concatenate([upper, lower], axis=0)


def twist_tables(freqs, inner, total):
    rows_index = jnp.arange(inner, dtype=jnp.int32)
    phase = rows_index[:, None] * freqs[None, :] % total
    angle = phase.astype(jnp.float32) * (2.0 * math.pi / total)
    return (jnp.cos(angle), jnp.sin(angle))


MESH = pl.DeviceIdType.MESH


def exchange_kernel(x_ref, o_ref, slots, scatter_send, scatter_recv, gather_send, gather_recv):
    n_tm, n_bank = slots.shape[1], o_ref.shape[0]
    rows = o_ref.shape[1]
    me_tm = lax.axis_index("tm")
    me_bank = lax.axis_index("bank")
    at_tm = lambda peer: (peer, me_bank)
    at_bank = lambda peer: (me_tm, peer)
    barrier = pltpu.get_barrier_semaphore()
    for step in range(1, n_tm):
        pl.semaphore_signal(barrier, inc=1, device_id=at_tm((me_tm + step) % n_tm), device_id_type=MESH)
    for step in range(1, n_bank):
        pl.semaphore_signal(barrier, inc=1, device_id=at_bank((me_bank + step) % n_bank), device_id_type=MESH)
    pl.semaphore_wait(barrier, n_tm + n_bank - 2)

    def remote(src, dst, send, recv, device):
        return pltpu.make_async_remote_copy(
            src_ref=src, dst_ref=dst, send_sem=send, recv_sem=recv, device_id=device, device_id_type=MESH
        )

    sends = []
    for r in range(rows):
        for step in range(1, n_tm):
            peer = (me_tm + step) % n_tm
            copy = remote(
                x_ref.at[peer * rows + r], slots.at[r, me_tm],
                scatter_send.at[r, peer], scatter_recv.at[r, me_tm], at_tm(peer),
            )
            copy.start()
            sends.append(copy)
    for r in range(rows):
        total = x_ref[me_tm * rows + r].astype(jnp.float32)
        for step in range(1, n_tm):
            source = (me_tm + n_tm - step) % n_tm
            remote(
                x_ref.at[r], slots.at[r, source],
                scatter_send.at[r, source], scatter_recv.at[r, source], at_tm(source),
            ).wait_recv()
            total = total + slots[r, source].astype(jnp.float32)
        o_ref[me_bank, r] = total.astype(o_ref.dtype)
        for step in range(1, n_bank):
            peer = (me_bank + step) % n_bank
            copy = remote(
                o_ref.at[me_bank, r], o_ref.at[me_bank, r],
                gather_send.at[r, peer], gather_recv.at[r, me_bank], at_bank(peer),
            )
            copy.start()
            sends.append(copy)
    for r in range(rows):
        for step in range(1, n_bank):
            source = (me_bank + n_bank - step) % n_bank
            remote(
                o_ref.at[source, r], o_ref.at[source, r],
                gather_send.at[r, source], gather_recv.at[r, source], at_bank(source),
            ).wait_recv()
    for copy in sends:
        copy.wait_send()


def exchange(x, n_tm, n_bank):
    rows = x.shape[0] // n_tm
    block = x.shape[1:]
    return pl.pallas_call(
        exchange_kernel,
        out_shape=jax.ShapeDtypeStruct((n_bank, rows) + block, x.dtype),
        in_specs=[pl.BlockSpec(memory_space=pltpu.VMEM)],
        out_specs=pl.BlockSpec(memory_space=pltpu.VMEM),
        scratch_shapes=[
            pltpu.VMEM((rows, n_tm) + block, x.dtype),
            pltpu.SemaphoreType.DMA((rows, n_tm)),
            pltpu.SemaphoreType.DMA((rows, n_tm)),
            pltpu.SemaphoreType.DMA((rows, n_bank)),
            pltpu.SemaphoreType.DMA((rows, n_bank)),
        ],
        compiler_params=pltpu.CompilerParams(collective_id=0, has_side_effects=True),
    )(x)


def mix_kernel(mix_ref, slots_ref, o_ref):
    n, rows, _, cols = slots_ref.shape
    half = cols // 2
    order = range(n)
    mix_real = mix_ref[0]
    mix_imag = mix_ref[1]
    for t in range(rows):
        plain = jnp.concatenate([slots_ref[slot, t] for slot in order], axis=0)
        turned = jnp.concatenate([-plain[:, half:], plain[:, :half]], axis=1)
        result = jnp.dot(mix_real, plain, preferred_element_type=jnp.float32) + jnp.dot(
            mix_imag, turned, preferred_element_type=jnp.float32
        )
        o_ref[0, t] = result[:, :half].astype(o_ref.dtype)
        o_ref[1, t] = result[:, half:].astype(o_ref.dtype)


def mix(mixing, slots):
    _, rows, _, cols = slots.shape
    templates = mixing.shape[1]
    return pl.pallas_call(
        mix_kernel,
        out_shape=jax.ShapeDtypeStruct((2, rows, templates, cols // 2), jnp.bfloat16),
        in_specs=[pl.BlockSpec(memory_space=pltpu.VMEM)] * 2,
        out_specs=pl.BlockSpec(memory_space=pltpu.VMEM),
    )(mixing, slots)


def front_kernel(spec_ref, filt_ref, table_ref, tcos_ref, tsin_ref, wave_ref, o_ref, quarter):
    block, inner = filt_ref.shape[1], filt_ref.shape[2]
    spec_real = spec_ref[0]
    spec_imag = spec_ref[1]
    table = table_ref[...]
    twist_cos = tcos_ref[...]
    twist_sin = tsin_ref[...]
    for kk in range(block):
        filt_real = filt_ref[0, kk].astype(jnp.float32)
        filt_imag = filt_ref[1, kk].astype(jnp.float32)
        prod_real = spec_real * filt_real + spec_imag * filt_imag
        prod_imag = spec_imag * filt_real - spec_real * filt_imag
        packed = jnp.concatenate([prod_real, prod_imag], axis=0).astype(jnp.bfloat16)
        section = jnp.dot(table, packed, preferred_element_type=jnp.float32)
        section_real = section[:inner]
        section_imag = section[inner:]
        quarter_real = section_real * twist_cos - section_imag * twist_sin
        quarter_imag = section_real * twist_sin + section_imag * twist_cos
        width = quarter_real.shape[1]
        rows = pl.ds(kk * inner, inner)
        quarter[rows, pl.ds(0, width)] = quarter_real.astype(jnp.bfloat16)
        quarter[rows, pl.ds(width, width)] = quarter_imag.astype(jnp.bfloat16)
    result = jnp.dot(quarter[...], wave_ref[...], preferred_element_type=jnp.float32)
    o_ref[...] = result.reshape(o_ref.shape).astype(o_ref.dtype)


def front(spectrum, filters, table, twist_cos, twist_sin, wave, block=8):
    _, basis, inner, freq = filters.shape
    cols = wave.shape[1]
    whole = lambda *shape: pl.BlockSpec(shape, lambda i: (0,) * len(shape))
    return pl.pallas_call(
        front_kernel,
        grid=(basis // block,),
        out_shape=jax.ShapeDtypeStruct((basis, inner, cols), jnp.bfloat16),
        in_specs=[
            whole(2, inner, freq),
            pl.BlockSpec((2, block, inner, freq), lambda i: (0, i, 0, 0)),
            whole(2 * inner, 2 * inner),
            whole(inner, freq),
            whole(inner, freq),
            whole(2 * freq, cols),
        ],
        out_specs=pl.BlockSpec((block, inner, cols), lambda i: (i, 0, 0)),
        scratch_shapes=[pltpu.VMEM((block * inner, 2 * freq), jnp.bfloat16)],
        compiler_params=pltpu.CompilerParams(vmem_limit_bytes=48 * 1024 * 1024),
    )(spectrum, filters, table, twist_cos, twist_sin, wave)


def on_device(spectrum, filters, mixing):
    tm_index = lax.axis_index("tm")
    local_freq = filters.shape[3]
    local_basis = filters.shape[1]
    inner = INNER
    outer = NSAMP // INNER
    table = first_table(inner)
    freqs = tm_index * local_freq + jnp.arange(local_freq, dtype=jnp.int32)
    twist_cos, twist_sin = twist_tables(freqs, inner, NSAMP)
    lags = START + jnp.arange(WROWS, dtype=jnp.int32)
    wave = wave_block(freqs, lags, outer)
    partial = front(spectrum, filters, table, twist_cos, twist_sin, wave).transpose(1, 0, 2)
    slots = exchange(partial, lax.axis_size("tm"), lax.axis_size("bank"))
    return mix(mixing, slots)


def solution(mesh):
    return jax.shard_map(
        on_device,
        mesh=mesh,
        in_specs=(P(None, None, "tm"), P(None, "bank", None, "tm"), P(None, "bank", None)),
        out_specs=P(None, "tm", "bank", None),
        check_vma=False,
    )
```

```python
import functools
import math

import jax
import jax.numpy as jnp
from jax import lax
from jax.experimental import pallas as pl
from jax.experimental.pallas import tpu as pltpu
from jax.sharding import PartitionSpec as P

NSAMP = 1048576
INNER = 64
WROWS = 128
START = 8128


def first_table(inner):
    index = jnp.arange(inner, dtype=jnp.int32)
    phase = index[:, None] * index[None, :] % inner
    angle = phase.astype(jnp.float32) * (2.0 * math.pi / inner)
    cosine = jnp.cos(angle).astype(jnp.bfloat16)
    sine = jnp.sin(angle).astype(jnp.bfloat16)
    upper = jnp.concatenate([cosine, -sine], axis=1)
    lower = jnp.concatenate([sine, cosine], axis=1)
    return jnp.concatenate([upper, lower], axis=0)


def wave_block(freqs, lags, period):
    phase = freqs[:, None] * lags[None, :] % period
    angle = phase.astype(jnp.float32) * (2.0 * math.pi / period)
    cosine = jnp.cos(angle).astype(jnp.bfloat16)
    sine = jnp.sin(angle).astype(jnp.bfloat16)
    upper = jnp.concatenate([cosine, sine], axis=1)
    lower = jnp.concatenate([-sine, cosine], axis=1)
    return jnp.concatenate([upper, lower], axis=0)


def twist_tables(freqs, inner, total):
    rows_index = jnp.arange(inner, dtype=jnp.int32)
    phase = rows_index[:, None] * freqs[None, :] % total
    angle = phase.astype(jnp.float32) * (2.0 * math.pi / total)
    return (jnp.cos(angle), jnp.sin(angle))


MESH = pl.DeviceIdType.MESH


def exchange_kernel(width, x_ref, o_ref, slots, scatter_send, scatter_recv, gather_send, gather_recv,
                    relay_send, relay_recv):
    n_tm, n_bank = slots.shape[1], o_ref.shape[0]
    depth = n_bank // width
    rows, basis = o_ref.shape[1], o_ref.shape[2]
    half = basis // 2
    me_tm = lax.axis_index("tm")
    me_bank = lax.axis_index("bank")
    x = me_bank // depth
    z = me_bank % depth
    up = (z + 1) % depth
    down = (z + depth - 1) % depth
    at_tm = lambda peer: (peer, me_bank)
    at_bank = lambda peer: (me_tm, peer)
    near = [(x + step) % width * depth + z for step in range(1, width)]
    near += [xx * depth + up for xx in range(width)] + [xx * depth + down for xx in range(width)]
    barrier = pltpu.get_barrier_semaphore()
    for step in range(1, n_tm):
        pl.semaphore_signal(barrier, inc=1, device_id=at_tm((me_tm + step) % n_tm), device_id_type=MESH)
    for peer in near:
        pl.semaphore_signal(barrier, inc=1, device_id=at_bank(peer), device_id_type=MESH)
    pl.semaphore_wait(barrier, n_tm - 1 + len(near))

    def remote(src, dst, send, recv, device):
        return pltpu.make_async_remote_copy(
            src_ref=src, dst_ref=dst, send_sem=send, recv_sem=recv, device_id=device, device_id_type=MESH
        )

    def relays(r):
        out = []
        for xx in range(width):
            out.append((xx * depth + down, 0, x * depth + up, 0, xx))
            out.append((xx * depth + up, half, x * depth + down, 1, xx))
        return out

    sends = []
    for r in range(rows):
        for step in range(1, n_tm):
            peer = (me_tm + step) % n_tm
            copy = remote(
                x_ref.at[peer * rows + r], slots.at[r, me_tm],
                scatter_send.at[r, peer], scatter_recv.at[r, me_tm], at_tm(peer),
            )
            copy.start()
            sends.append(copy)

    def forward(r):
        for source in near:
            remote(
                o_ref.at[source, r], o_ref.at[source, r],
                gather_send.at[r, source], gather_recv.at[r, source], at_bank(source),
            ).wait_recv()
        for slot, start, target, way, xx in relays(r):
            block = o_ref.at[slot, r, pl.ds(start, half)]
            copy = remote(block, block, relay_send.at[r, way, xx], relay_recv.at[r, way, xx], at_bank(target))
            copy.start()
            sends.append(copy)

    for r in range(rows):
        total = x_ref[me_tm * rows + r].astype(jnp.float32)
        for step in range(1, n_tm):
            source = (me_tm + n_tm - step) % n_tm
            remote(
                x_ref.at[r], slots.at[r, source],
                scatter_send.at[r, source], scatter_recv.at[r, source], at_tm(source),
            ).wait_recv()
            total = total + slots[r, source].astype(jnp.float32)
        o_ref[me_bank, r] = total.astype(o_ref.dtype)
        for peer in near:
            copy = remote(
                o_ref.at[me_bank, r], o_ref.at[me_bank, r],
                gather_send.at[r, peer], gather_recv.at[r, me_bank], at_bank(peer),
            )
            copy.start()
            sends.append(copy)
        if r >= 1:
            forward(r - 1)
    forward(rows - 1)
    across = (z + 2) % depth
    for r in range(rows):
        for xx in range(width):
            for way, start, via in ((0, 0, down), (1, half, up)):
                block = o_ref.at[xx * depth + across, r, pl.ds(start, half)]
                remote(
                    block, block, relay_send.at[r, way, xx], relay_recv.at[r, way, xx], at_bank(x * depth + via)
                ).wait_recv()
    for copy in sends:
        copy.wait_send()


def exchange(x, n_tm, n_bank, width):
    rows = x.shape[0] // n_tm
    block = x.shape[1:]
    return pl.pallas_call(
        functools.partial(exchange_kernel, width),
        out_shape=jax.ShapeDtypeStruct((n_bank, rows) + block, x.dtype),
        in_specs=[pl.BlockSpec(memory_space=pltpu.VMEM)],
        out_specs=pl.BlockSpec(memory_space=pltpu.VMEM),
        scratch_shapes=[
            pltpu.VMEM((rows, n_tm) + block, x.dtype),
            pltpu.SemaphoreType.DMA((rows, n_tm)),
            pltpu.SemaphoreType.DMA((rows, n_tm)),
            pltpu.SemaphoreType.DMA((rows, n_bank)),
            pltpu.SemaphoreType.DMA((rows, n_bank)),
            pltpu.SemaphoreType.DMA((rows, 2, width)),
            pltpu.SemaphoreType.DMA((rows, 2, width)),
        ],
        compiler_params=pltpu.CompilerParams(collective_id=0, has_side_effects=True),
    )(x)


def mix_kernel(mix_ref, slots_ref, o_ref):
    n, rows, _, cols = slots_ref.shape
    half = cols // 2
    order = range(n)
    mix_real = mix_ref[0]
    mix_imag = mix_ref[1]
    for t in range(rows):
        plain = jnp.concatenate([slots_ref[slot, t] for slot in order], axis=0)
        turned = jnp.concatenate([-plain[:, half:], plain[:, :half]], axis=1)
        result = jnp.dot(mix_real, plain, preferred_element_type=jnp.float32) + jnp.dot(
            mix_imag, turned, preferred_element_type=jnp.float32
        )
        o_ref[0, t] = result[:, :half].astype(o_ref.dtype)
        o_ref[1, t] = result[:, half:].astype(o_ref.dtype)


def mix(mixing, slots):
    _, rows, _, cols = slots.shape
    templates = mixing.shape[1]
    return pl.pallas_call(
        mix_kernel,
        out_shape=jax.ShapeDtypeStruct((2, rows, templates, cols // 2), jnp.bfloat16),
        in_specs=[pl.BlockSpec(memory_space=pltpu.VMEM)] * 2,
        out_specs=pl.BlockSpec(memory_space=pltpu.VMEM),
    )(mixing, slots)


def front_kernel(spec_ref, filt_ref, table_ref, tcos_ref, tsin_ref, wave_ref, o_ref, quarter):
    block, inner = filt_ref.shape[1], filt_ref.shape[2]
    spec_real = spec_ref[0]
    spec_imag = spec_ref[1]
    table = table_ref[...]
    twist_cos = tcos_ref[...]
    twist_sin = tsin_ref[...]
    for kk in range(block):
        filt_real = filt_ref[0, kk].astype(jnp.float32)
        filt_imag = filt_ref[1, kk].astype(jnp.float32)
        prod_real = spec_real * filt_real + spec_imag * filt_imag
        prod_imag = spec_imag * filt_real - spec_real * filt_imag
        packed = jnp.concatenate([prod_real, prod_imag], axis=0).astype(jnp.bfloat16)
        section = jnp.dot(table, packed, preferred_element_type=jnp.float32)
        section_real = section[:inner]
        section_imag = section[inner:]
        quarter_real = section_real * twist_cos - section_imag * twist_sin
        quarter_imag = section_real * twist_sin + section_imag * twist_cos
        width = quarter_real.shape[1]
        rows = pl.ds(kk * inner, inner)
        quarter[rows, pl.ds(0, width)] = quarter_real.astype(jnp.bfloat16)
        quarter[rows, pl.ds(width, width)] = quarter_imag.astype(jnp.bfloat16)
    result = jnp.dot(quarter[...], wave_ref[...], preferred_element_type=jnp.float32)
    o_ref[...] = result.reshape(o_ref.shape).astype(o_ref.dtype)


def front(spectrum, filters, table, twist_cos, twist_sin, wave, block=8):
    _, basis, inner, freq = filters.shape
    cols = wave.shape[1]
    whole = lambda *shape: pl.BlockSpec(shape, lambda i: (0,) * len(shape))
    return pl.pallas_call(
        front_kernel,
        grid=(basis // block,),
        out_shape=jax.ShapeDtypeStruct((basis, inner, cols), jnp.bfloat16),
        in_specs=[
            whole(2, inner, freq),
            pl.BlockSpec((2, block, inner, freq), lambda i: (0, i, 0, 0)),
            whole(2 * inner, 2 * inner),
            whole(inner, freq),
            whole(inner, freq),
            whole(2 * freq, cols),
        ],
        out_specs=pl.BlockSpec((block, inner, cols), lambda i: (i, 0, 0)),
        scratch_shapes=[pltpu.VMEM((block * inner, 2 * freq), jnp.bfloat16)],
        compiler_params=pltpu.CompilerParams(vmem_limit_bytes=48 * 1024 * 1024),
    )(spectrum, filters, table, twist_cos, twist_sin, wave)


def on_device(spectrum, filters, mixing):
    tm_index = lax.axis_index("tm")
    local_freq = filters.shape[3]
    local_basis = filters.shape[1]
    inner = INNER
    outer = NSAMP // INNER
    table = first_table(inner)
    freqs = tm_index * local_freq + jnp.arange(local_freq, dtype=jnp.int32)
    twist_cos, twist_sin = twist_tables(freqs, inner, NSAMP)
    lags = START + jnp.arange(WROWS, dtype=jnp.int32)
    wave = wave_block(freqs, lags, outer)
    partial = front(spectrum, filters, table, twist_cos, twist_sin, wave).transpose(1, 0, 2)
    slots = exchange(partial, lax.axis_size("tm"), lax.axis_size("bank"), 4)
    return mix(mixing, slots)


def solution(mesh):
    return jax.shard_map(
        on_device,
        mesh=mesh,
        in_specs=(P(None, None, "tm"), P(None, "bank", None, "tm"), P(None, "bank", None)),
        out_specs=P(None, "tm", "bank", None),
        check_vma=False,
    )
```

```python
import functools
import math

import jax
import jax.numpy as jnp
from jax import lax
from jax.experimental import pallas as pl
from jax.experimental.pallas import tpu as pltpu
from jax.sharding import PartitionSpec as P

NSAMP = 1048576
INNER = 64
WROWS = 128
START = 8128


def first_table(inner):
    index = jnp.arange(inner, dtype=jnp.int32)
    phase = index[:, None] * index[None, :] % inner
    angle = phase.astype(jnp.float32) * (2.0 * math.pi / inner)
    cosine = jnp.cos(angle).astype(jnp.bfloat16)
    sine = jnp.sin(angle).astype(jnp.bfloat16)
    upper = jnp.concatenate([cosine, -sine], axis=1)
    lower = jnp.concatenate([sine, cosine], axis=1)
    return jnp.concatenate([upper, lower], axis=0)


def wave_block(freqs, lags, period):
    phase = freqs[:, None] * lags[None, :] % period
    angle = phase.astype(jnp.float32) * (2.0 * math.pi / period)
    cosine = jnp.cos(angle).astype(jnp.bfloat16)
    sine = jnp.sin(angle).astype(jnp.bfloat16)
    return jnp.concatenate([cosine, sine], axis=1)


def twist_tables(freqs, inner, total):
    rows_index = jnp.arange(inner, dtype=jnp.int32)
    phase = rows_index[:, None] * freqs[None, :] % total
    angle = phase.astype(jnp.float32) * (2.0 * math.pi / total)
    return (jnp.cos(angle), jnp.sin(angle))


MESH = pl.DeviceIdType.MESH


def exchange_kernel(width, x_ref, o_ref, slots, scatter_send, scatter_recv, gather_send, gather_recv,
                    relay_send, relay_recv):
    n_tm, n_bank = slots.shape[1], o_ref.shape[0]
    depth = n_bank // width
    rows, basis = o_ref.shape[1], o_ref.shape[2]
    half = basis // 2
    me_tm = lax.axis_index("tm")
    me_bank = lax.axis_index("bank")
    x = me_bank // depth
    z = me_bank % depth
    up = (z + 1) % depth
    down = (z + depth - 1) % depth
    at_tm = lambda peer: (peer, me_bank)
    at_bank = lambda peer: (me_tm, peer)
    near = [(x + step) % width * depth + z for step in range(1, width)]
    near += [xx * depth + up for xx in range(width)] + [xx * depth + down for xx in range(width)]
    barrier = pltpu.get_barrier_semaphore()
    for step in range(1, n_tm):
        pl.semaphore_signal(barrier, inc=1, device_id=at_tm((me_tm + step) % n_tm), device_id_type=MESH)
    for peer in near:
        pl.semaphore_signal(barrier, inc=1, device_id=at_bank(peer), device_id_type=MESH)
    pl.semaphore_wait(barrier, n_tm - 1 + len(near))

    def remote(src, dst, send, recv, device):
        return pltpu.make_async_remote_copy(
            src_ref=src, dst_ref=dst, send_sem=send, recv_sem=recv, device_id=device, device_id_type=MESH
        )

    def relays(r):
        out = []
        for xx in range(width):
            out.append((xx * depth + down, 0, x * depth + up, 0, xx))
            out.append((xx * depth + up, half, x * depth + down, 1, xx))
        return out

    sends = []
    for r in range(rows):
        for step in range(1, n_tm):
            peer = (me_tm + step) % n_tm
            copy = remote(
                x_ref.at[peer * rows + r], slots.at[r, me_tm],
                scatter_send.at[r, peer], scatter_recv.at[r, me_tm], at_tm(peer),
            )
            copy.start()
            sends.append(copy)

    def forward(r):
        for source in near:
            remote(
                o_ref.at[source, r], o_ref.at[source, r],
                gather_send.at[r, source], gather_recv.at[r, source], at_bank(source),
            ).wait_recv()
        for slot, start, target, way, xx in relays(r):
            block = o_ref.at[slot, r, pl.ds(start, half)]
            copy = remote(block, block, relay_send.at[r, way, xx], relay_recv.at[r, way, xx], at_bank(target))
            copy.start()
            sends.append(copy)

    for r in range(rows):
        total = x_ref[me_tm * rows + r].astype(jnp.float32)
        for step in range(1, n_tm):
            source = (me_tm + n_tm - step) % n_tm
            remote(
                x_ref.at[r], slots.at[r, source],
                scatter_send.at[r, source], scatter_recv.at[r, source], at_tm(source),
            ).wait_recv()
            total = total + slots[r, source].astype(jnp.float32)
        o_ref[me_bank, r] = total.astype(o_ref.dtype)
        for peer in near:
            copy = remote(
                o_ref.at[me_bank, r], o_ref.at[me_bank, r],
                gather_send.at[r, peer], gather_recv.at[r, me_bank], at_bank(peer),
            )
            copy.start()
            sends.append(copy)
        if r >= 1:
            forward(r - 1)
    forward(rows - 1)
    across = (z + 2) % depth
    for r in range(rows):
        for xx in range(width):
            for way, start, via in ((0, 0, down), (1, half, up)):
                block = o_ref.at[xx * depth + across, r, pl.ds(start, half)]
                remote(
                    block, block, relay_send.at[r, way, xx], relay_recv.at[r, way, xx], at_bank(x * depth + via)
                ).wait_recv()
    for copy in sends:
        copy.wait_send()


def exchange(x, n_tm, n_bank, width):
    rows = x.shape[0] // n_tm
    block = x.shape[1:]
    return pl.pallas_call(
        functools.partial(exchange_kernel, width),
        out_shape=jax.ShapeDtypeStruct((n_bank, rows) + block, x.dtype),
        in_specs=[pl.BlockSpec(memory_space=pltpu.VMEM)],
        out_specs=pl.BlockSpec(memory_space=pltpu.VMEM),
        scratch_shapes=[
            pltpu.VMEM((rows, n_tm) + block, x.dtype),
            pltpu.SemaphoreType.DMA((rows, n_tm)),
            pltpu.SemaphoreType.DMA((rows, n_tm)),
            pltpu.SemaphoreType.DMA((rows, n_bank)),
            pltpu.SemaphoreType.DMA((rows, n_bank)),
            pltpu.SemaphoreType.DMA((rows, 2, width)),
            pltpu.SemaphoreType.DMA((rows, 2, width)),
        ],
        compiler_params=pltpu.CompilerParams(collective_id=0, has_side_effects=True),
    )(x)


def mix_kernel(mix_ref, slots_ref, o_ref):
    n, rows, _, cols = slots_ref.shape
    half = cols // 2
    order = range(n)
    mix_real = mix_ref[0]
    mix_imag = mix_ref[1]
    for t in range(rows):
        plain = jnp.concatenate([slots_ref[slot, t] for slot in order], axis=0)
        turned = jnp.concatenate([-plain[:, half:], plain[:, :half]], axis=1)
        result = jnp.dot(mix_real, plain, preferred_element_type=jnp.float32) + jnp.dot(
            mix_imag, turned, preferred_element_type=jnp.float32
        )
        o_ref[0, t] = result[:, :half].astype(o_ref.dtype)
        o_ref[1, t] = result[:, half:].astype(o_ref.dtype)


def mix(mixing, slots):
    _, rows, _, cols = slots.shape
    templates = mixing.shape[1]
    return pl.pallas_call(
        mix_kernel,
        out_shape=jax.ShapeDtypeStruct((2, rows, templates, cols // 2), jnp.bfloat16),
        in_specs=[pl.BlockSpec(memory_space=pltpu.VMEM)] * 2,
        out_specs=pl.BlockSpec(memory_space=pltpu.VMEM),
    )(mixing, slots)


def front_kernel(spec_ref, filt_ref, table_ref, tcos_ref, tsin_ref, wave_ref, o_ref, quarter):
    block, inner = filt_ref.shape[1], filt_ref.shape[2]
    spec_real = spec_ref[0]
    spec_imag = spec_ref[1]
    table = table_ref[...]
    twist_cos = tcos_ref[...]
    twist_sin = tsin_ref[...]
    for kk in range(block):
        filt_real = filt_ref[0, kk].astype(jnp.float32)
        filt_imag = filt_ref[1, kk].astype(jnp.float32)
        prod_real = spec_real * filt_real + spec_imag * filt_imag
        prod_imag = spec_imag * filt_real - spec_real * filt_imag
        packed = jnp.concatenate([prod_real, prod_imag], axis=0).astype(jnp.bfloat16)
        section = jnp.dot(table, packed, preferred_element_type=jnp.float32)
        section_real = section[:inner]
        section_imag = section[inner:]
        quarter_real = section_real * twist_cos - section_imag * twist_sin
        quarter_imag = section_real * twist_sin + section_imag * twist_cos
        width = quarter_real.shape[1]
        rows = pl.ds(kk * inner, inner)
        quarter[rows, pl.ds(0, width)] = quarter_real.astype(jnp.bfloat16)
        quarter[rows, pl.ds(width, width)] = quarter_imag.astype(jnp.bfloat16)
    wave = wave_ref[...]
    cols = wave.shape[1] // 2
    from_real = jnp.dot(quarter[:, :width], wave, preferred_element_type=jnp.float32)
    from_imag = jnp.dot(quarter[:, width:], wave, preferred_element_type=jnp.float32)
    result = jnp.concatenate(
        [from_real[:, :cols] - from_imag[:, cols:], from_real[:, cols:] + from_imag[:, :cols]], axis=1
    )
    o_ref[...] = result.reshape(o_ref.shape).astype(o_ref.dtype)


def front(spectrum, filters, table, twist_cos, twist_sin, wave, block=8):
    _, basis, inner, freq = filters.shape
    cols = wave.shape[1]
    whole = lambda *shape: pl.BlockSpec(shape, lambda i: (0,) * len(shape))
    return pl.pallas_call(
        front_kernel,
        grid=(basis // block,),
        out_shape=jax.ShapeDtypeStruct((basis, inner, cols), jnp.bfloat16),
        in_specs=[
            whole(2, inner, freq),
            pl.BlockSpec((2, block, inner, freq), lambda i: (0, i, 0, 0)),
            whole(2 * inner, 2 * inner),
            whole(inner, freq),
            whole(inner, freq),
            whole(freq, cols),
        ],
        out_specs=pl.BlockSpec((block, inner, cols), lambda i: (i, 0, 0)),
        scratch_shapes=[pltpu.VMEM((block * inner, 2 * freq), jnp.bfloat16)],
        compiler_params=pltpu.CompilerParams(vmem_limit_bytes=48 * 1024 * 1024),
    )(spectrum, filters, table, twist_cos, twist_sin, wave)


def on_device(spectrum, filters, mixing):
    tm_index = lax.axis_index("tm")
    local_freq = filters.shape[3]
    local_basis = filters.shape[1]
    inner = INNER
    outer = NSAMP // INNER
    table = first_table(inner)
    freqs = tm_index * local_freq + jnp.arange(local_freq, dtype=jnp.int32)
    twist_cos, twist_sin = twist_tables(freqs, inner, NSAMP)
    lags = START + jnp.arange(WROWS, dtype=jnp.int32)
    wave = wave_block(freqs, lags, outer)
    partial = front(spectrum, filters, table, twist_cos, twist_sin, wave).transpose(1, 0, 2)
    slots = exchange(partial, lax.axis_size("tm"), lax.axis_size("bank"), 4)
    return mix(mixing, slots)


def solution(mesh):
    return jax.shard_map(
        on_device,
        mesh=mesh,
        in_specs=(P(None, None, "tm"), P(None, "bank", None, "tm"), P(None, "bank", None)),
        out_specs=P(None, "tm", "bank", None),
        check_vma=False,
    )
```

```python
import functools
import math

import jax
import jax.numpy as jnp
from jax import lax
from jax.experimental import pallas as pl
from jax.experimental.pallas import tpu as pltpu
from jax.sharding import PartitionSpec as P

NSAMP = 1048576
INNER = 64
WROWS = 128
START = 8128


def first_table(inner):
    index = jnp.arange(inner, dtype=jnp.int32)
    phase = index[:, None] * index[None, :] % inner
    angle = phase.astype(jnp.float32) * (2.0 * math.pi / inner)
    cosine = jnp.cos(angle).astype(jnp.bfloat16)
    sine = jnp.sin(angle).astype(jnp.bfloat16)
    upper = jnp.concatenate([cosine, -sine], axis=1)
    lower = jnp.concatenate([sine, cosine], axis=1)
    return jnp.concatenate([upper, lower], axis=0)


def wave_block(freqs, lags, period):
    phase = freqs[:, None] * lags[None, :] % period
    angle = phase.astype(jnp.float32) * (2.0 * math.pi / period)
    cosine = jnp.cos(angle).astype(jnp.bfloat16)
    sine = jnp.sin(angle).astype(jnp.bfloat16)
    return jnp.concatenate([cosine, sine], axis=1)


def twist_tables(freqs, inner, total):
    rows_index = jnp.arange(inner, dtype=jnp.int32)
    phase = rows_index[:, None] * freqs[None, :] % total
    angle = phase.astype(jnp.float32) * (2.0 * math.pi / total)
    return (jnp.cos(angle), jnp.sin(angle))


MESH = pl.DeviceIdType.MESH


def exchange_kernel(width, x_ref, o_ref, slots, scatter_send, scatter_recv, gather_send, gather_recv,
                    relay_send, relay_recv):
    n_tm, n_bank = slots.shape[1], o_ref.shape[0]
    depth = n_bank // width
    rows, basis = o_ref.shape[1], o_ref.shape[2]
    half = basis // 2
    me_tm = lax.axis_index("tm")
    me_bank = lax.axis_index("bank")
    x = me_bank // depth
    z = me_bank % depth
    up = (z + 1) % depth
    down = (z + depth - 1) % depth
    at_tm = lambda peer: (peer, me_bank)
    at_bank = lambda peer: (me_tm, peer)
    near = [(x + step) % width * depth + z for step in range(1, width)]
    near += [xx * depth + up for xx in range(width)] + [xx * depth + down for xx in range(width)]
    barrier = pltpu.get_barrier_semaphore()
    for step in range(1, n_tm):
        pl.semaphore_signal(barrier, inc=1, device_id=at_tm((me_tm + step) % n_tm), device_id_type=MESH)
    for peer in near:
        pl.semaphore_signal(barrier, inc=1, device_id=at_bank(peer), device_id_type=MESH)
    pl.semaphore_wait(barrier, n_tm - 1 + len(near))

    def remote(src, dst, send, recv, device):
        return pltpu.make_async_remote_copy(
            src_ref=src, dst_ref=dst, send_sem=send, recv_sem=recv, device_id=device, device_id_type=MESH
        )

    def relays(r):
        out = []
        for xx in range(width):
            out.append((xx * depth + down, 0, x * depth + up, 0, xx))
            out.append((xx * depth + up, half, x * depth + down, 1, xx))
        return out

    sends = []

    def scatter(r):
        for step in range(1, n_tm):
            peer = (me_tm + step) % n_tm
            copy = remote(
                x_ref.at[peer * rows + r], slots.at[r, me_tm],
                scatter_send.at[r, peer], scatter_recv.at[r, me_tm], at_tm(peer),
            )
            copy.start()
            sends.append(copy)

    ahead = 2
    for r in range(min(ahead, rows)):
        scatter(r)

    def forward(r):
        for source in near:
            remote(
                o_ref.at[source, r], o_ref.at[source, r],
                gather_send.at[r, source], gather_recv.at[r, source], at_bank(source),
            ).wait_recv()
        for slot, start, target, way, xx in relays(r):
            block = o_ref.at[slot, r, pl.ds(start, half)]
            copy = remote(block, block, relay_send.at[r, way, xx], relay_recv.at[r, way, xx], at_bank(target))
            copy.start()
            sends.append(copy)

    for r in range(rows):
        total = x_ref[me_tm * rows + r].astype(jnp.float32)
        for step in range(1, n_tm):
            source = (me_tm + n_tm - step) % n_tm
            remote(
                x_ref.at[r], slots.at[r, source],
                scatter_send.at[r, source], scatter_recv.at[r, source], at_tm(source),
            ).wait_recv()
            total = total + slots[r, source].astype(jnp.float32)
        o_ref[me_bank, r] = total.astype(o_ref.dtype)
        for peer in near:
            copy = remote(
                o_ref.at[me_bank, r], o_ref.at[me_bank, r],
                gather_send.at[r, peer], gather_recv.at[r, me_bank], at_bank(peer),
            )
            copy.start()
            sends.append(copy)
        if r + ahead < rows:
            scatter(r + ahead)
        if r >= 1:
            forward(r - 1)
    forward(rows - 1)
    across = (z + 2) % depth
    for r in range(rows):
        for xx in range(width):
            for way, start, via in ((0, 0, down), (1, half, up)):
                block = o_ref.at[xx * depth + across, r, pl.ds(start, half)]
                remote(
                    block, block, relay_send.at[r, way, xx], relay_recv.at[r, way, xx], at_bank(x * depth + via)
                ).wait_recv()
    for copy in sends:
        copy.wait_send()


def exchange(x, n_tm, n_bank, width):
    rows = x.shape[0] // n_tm
    block = x.shape[1:]
    return pl.pallas_call(
        functools.partial(exchange_kernel, width),
        out_shape=jax.ShapeDtypeStruct((n_bank, rows) + block, x.dtype),
        in_specs=[pl.BlockSpec(memory_space=pltpu.VMEM)],
        out_specs=pl.BlockSpec(memory_space=pltpu.VMEM),
        scratch_shapes=[
            pltpu.VMEM((rows, n_tm) + block, x.dtype),
            pltpu.SemaphoreType.DMA((rows, n_tm)),
            pltpu.SemaphoreType.DMA((rows, n_tm)),
            pltpu.SemaphoreType.DMA((rows, n_bank)),
            pltpu.SemaphoreType.DMA((rows, n_bank)),
            pltpu.SemaphoreType.DMA((rows, 2, width)),
            pltpu.SemaphoreType.DMA((rows, 2, width)),
        ],
        compiler_params=pltpu.CompilerParams(collective_id=0, has_side_effects=True),
    )(x)


def mix_kernel(mix_ref, slots_ref, o_ref):
    n, rows, _, cols = slots_ref.shape
    half = cols // 2
    order = range(n)
    mix_real = mix_ref[0]
    mix_imag = mix_ref[1]
    for t in range(rows):
        plain = jnp.concatenate([slots_ref[slot, t] for slot in order], axis=0)
        turned = jnp.concatenate([-plain[:, half:], plain[:, :half]], axis=1)
        result = jnp.dot(mix_real, plain, preferred_element_type=jnp.float32) + jnp.dot(
            mix_imag, turned, preferred_element_type=jnp.float32
        )
        o_ref[0, t] = result[:, :half].astype(o_ref.dtype)
        o_ref[1, t] = result[:, half:].astype(o_ref.dtype)


def mix(mixing, slots):
    _, rows, _, cols = slots.shape
    templates = mixing.shape[1]
    return pl.pallas_call(
        mix_kernel,
        out_shape=jax.ShapeDtypeStruct((2, rows, templates, cols // 2), jnp.bfloat16),
        in_specs=[pl.BlockSpec(memory_space=pltpu.VMEM)] * 2,
        out_specs=pl.BlockSpec(memory_space=pltpu.VMEM),
    )(mixing, slots)


def front_kernel(spec_ref, filt_ref, table_ref, tcos_ref, tsin_ref, wave_ref, o_ref, quarter):
    block, inner = filt_ref.shape[1], filt_ref.shape[2]
    spec_real = spec_ref[0]
    spec_imag = spec_ref[1]
    table = table_ref[...]
    twist_cos = tcos_ref[...]
    twist_sin = tsin_ref[...]
    for kk in range(block):
        filt_real = filt_ref[0, kk].astype(jnp.float32)
        filt_imag = filt_ref[1, kk].astype(jnp.float32)
        prod_real = spec_real * filt_real + spec_imag * filt_imag
        prod_imag = spec_imag * filt_real - spec_real * filt_imag
        packed = jnp.concatenate([prod_real, prod_imag], axis=0).astype(jnp.bfloat16)
        section = jnp.dot(table, packed, preferred_element_type=jnp.float32)
        section_real = section[:inner]
        section_imag = section[inner:]
        quarter_real = section_real * twist_cos - section_imag * twist_sin
        quarter_imag = section_real * twist_sin + section_imag * twist_cos
        width = quarter_real.shape[1]
        rows = pl.ds(kk * inner, inner)
        quarter[rows, pl.ds(0, width)] = quarter_real.astype(jnp.bfloat16)
        quarter[rows, pl.ds(width, width)] = quarter_imag.astype(jnp.bfloat16)
    wave = wave_ref[...]
    cols = wave.shape[1] // 2
    from_real = jnp.dot(quarter[:, :width], wave, preferred_element_type=jnp.float32)
    from_imag = jnp.dot(quarter[:, width:], wave, preferred_element_type=jnp.float32)
    result = jnp.concatenate(
        [from_real[:, :cols] - from_imag[:, cols:], from_real[:, cols:] + from_imag[:, :cols]], axis=1
    )
    o_ref[...] = result.reshape(o_ref.shape).astype(o_ref.dtype)


def front(spectrum, filters, table, twist_cos, twist_sin, wave, block=8):
    _, basis, inner, freq = filters.shape
    cols = wave.shape[1]
    whole = lambda *shape: pl.BlockSpec(shape, lambda i: (0,) * len(shape))
    return pl.pallas_call(
        front_kernel,
        grid=(basis // block,),
        out_shape=jax.ShapeDtypeStruct((basis, inner, cols), jnp.bfloat16),
        in_specs=[
            whole(2, inner, freq),
            pl.BlockSpec((2, block, inner, freq), lambda i: (0, i, 0, 0)),
            whole(2 * inner, 2 * inner),
            whole(inner, freq),
            whole(inner, freq),
            whole(freq, cols),
        ],
        out_specs=pl.BlockSpec((block, inner, cols), lambda i: (i, 0, 0)),
        scratch_shapes=[pltpu.VMEM((block * inner, 2 * freq), jnp.bfloat16)],
        compiler_params=pltpu.CompilerParams(vmem_limit_bytes=48 * 1024 * 1024),
    )(spectrum, filters, table, twist_cos, twist_sin, wave)


def on_device(spectrum, filters, mixing):
    tm_index = lax.axis_index("tm")
    local_freq = filters.shape[3]
    local_basis = filters.shape[1]
    inner = INNER
    outer = NSAMP // INNER
    table = first_table(inner)
    freqs = tm_index * local_freq + jnp.arange(local_freq, dtype=jnp.int32)
    twist_cos, twist_sin = twist_tables(freqs, inner, NSAMP)
    lags = START + jnp.arange(WROWS, dtype=jnp.int32)
    wave = wave_block(freqs, lags, outer)
    partial = front(spectrum, filters, table, twist_cos, twist_sin, wave).transpose(1, 0, 2)
    slots = exchange(partial, lax.axis_size("tm"), lax.axis_size("bank"), 4)
    return mix(mixing, slots)


def solution(mesh):
    return jax.shard_map(
        on_device,
        mesh=mesh,
        in_specs=(P(None, None, "tm"), P(None, "bank", None, "tm"), P(None, "bank", None)),
        out_specs=P(None, "tm", "bank", None),
        check_vma=False,
    )
```

```python
import functools
import math

import jax
import jax.numpy as jnp
from jax import lax
from jax.experimental import pallas as pl
from jax.experimental.pallas import tpu as pltpu
from jax.sharding import PartitionSpec as P

NSAMP = 1048576
INNER = 64
WROWS = 128
START = 8128


def first_table(inner):
    index = jnp.arange(inner, dtype=jnp.int32)
    phase = index[:, None] * index[None, :] % inner
    angle = phase.astype(jnp.float32) * (2.0 * math.pi / inner)
    cosine = jnp.cos(angle).astype(jnp.bfloat16)
    sine = jnp.sin(angle).astype(jnp.bfloat16)
    upper = jnp.concatenate([cosine, -sine], axis=1)
    lower = jnp.concatenate([sine, cosine], axis=1)
    return jnp.concatenate([upper, lower], axis=0)


def wave_block(freqs, lags, period):
    phase = freqs[:, None] * lags[None, :] % period
    angle = phase.astype(jnp.float32) * (2.0 * math.pi / period)
    cosine = jnp.cos(angle).astype(jnp.bfloat16)
    sine = jnp.sin(angle).astype(jnp.bfloat16)
    return jnp.concatenate([cosine, sine], axis=1)


def twist_tables(freqs, inner, total):
    rows_index = jnp.arange(inner, dtype=jnp.int32)
    phase = rows_index[:, None] * freqs[None, :] % total
    angle = phase.astype(jnp.float32) * (2.0 * math.pi / total)
    return (jnp.cos(angle), jnp.sin(angle))


MESH = pl.DeviceIdType.MESH


def exchange_kernel(width, x_ref, o_ref, slots, scatter_send, scatter_recv, gather_send, gather_recv,
                    relay_send, relay_recv):
    n_tm, n_bank = slots.shape[1], o_ref.shape[1]
    depth = n_bank // width
    rows, basis = o_ref.shape[0], o_ref.shape[2]
    half = basis // 2
    me_tm = lax.axis_index("tm")
    me_bank = lax.axis_index("bank")
    x = me_bank // depth
    z = me_bank % depth
    up = (z + 1) % depth
    down = (z + depth - 1) % depth
    at_tm = lambda peer: (peer, me_bank)
    at_bank = lambda peer: (me_tm, peer)
    near = [(x + step) % width * depth + z for step in range(1, width)]
    near += [xx * depth + up for xx in range(width)] + [xx * depth + down for xx in range(width)]
    barrier = pltpu.get_barrier_semaphore()
    for step in range(1, n_tm):
        pl.semaphore_signal(barrier, inc=1, device_id=at_tm((me_tm + step) % n_tm), device_id_type=MESH)
    for peer in near:
        pl.semaphore_signal(barrier, inc=1, device_id=at_bank(peer), device_id_type=MESH)
    pl.semaphore_wait(barrier, n_tm - 1 + len(near))

    def remote(src, dst, send, recv, device):
        return pltpu.make_async_remote_copy(
            src_ref=src, dst_ref=dst, send_sem=send, recv_sem=recv, device_id=device, device_id_type=MESH
        )

    def relays(r):
        out = []
        for xx in range(width):
            out.append((xx * depth + down, 0, x * depth + up, 0, xx))
            out.append((xx * depth + up, half, x * depth + down, 1, xx))
        return out

    sends = []
    for r in range(rows):
        for step in range(1, n_tm):
            peer = (me_tm + step) % n_tm
            copy = remote(
                x_ref.at[peer * rows + r], slots.at[r, me_tm],
                scatter_send.at[r, peer], scatter_recv.at[r, me_tm], at_tm(peer),
            )
            copy.start()
            sends.append(copy)

    def forward(r):
        for source in near:
            remote(
                o_ref.at[r, source], o_ref.at[r, source],
                gather_send.at[r, source], gather_recv.at[r, source], at_bank(source),
            ).wait_recv()
        for slot, start, target, way, xx in relays(r):
            block = o_ref.at[r, slot, pl.ds(start, half)]
            copy = remote(block, block, relay_send.at[r, way, xx], relay_recv.at[r, way, xx], at_bank(target))
            copy.start()
            sends.append(copy)

    for r in range(rows):
        total = x_ref[me_tm * rows + r].astype(jnp.float32)
        for step in range(1, n_tm):
            source = (me_tm + n_tm - step) % n_tm
            remote(
                x_ref.at[r], slots.at[r, source],
                scatter_send.at[r, source], scatter_recv.at[r, source], at_tm(source),
            ).wait_recv()
            total = total + slots[r, source].astype(jnp.float32)
        o_ref[r, me_bank] = total.astype(o_ref.dtype)
        for peer in near:
            copy = remote(
                o_ref.at[r, me_bank], o_ref.at[r, me_bank],
                gather_send.at[r, peer], gather_recv.at[r, me_bank], at_bank(peer),
            )
            copy.start()
            sends.append(copy)
        if r >= 1:
            forward(r - 1)
    forward(rows - 1)
    across = (z + 2) % depth
    for r in range(rows):
        for xx in range(width):
            for way, start, via in ((0, 0, down), (1, half, up)):
                block = o_ref.at[r, xx * depth + across, pl.ds(start, half)]
                remote(
                    block, block, relay_send.at[r, way, xx], relay_recv.at[r, way, xx], at_bank(x * depth + via)
                ).wait_recv()
    for copy in sends:
        copy.wait_send()


def exchange(x, n_tm, n_bank, width):
    rows = x.shape[0] // n_tm
    block = x.shape[1:]
    return pl.pallas_call(
        functools.partial(exchange_kernel, width),
        out_shape=jax.ShapeDtypeStruct((rows, n_bank) + block, x.dtype),
        in_specs=[pl.BlockSpec(memory_space=pltpu.VMEM)],
        out_specs=pl.BlockSpec(memory_space=pltpu.VMEM),
        scratch_shapes=[
            pltpu.VMEM((rows, n_tm) + block, x.dtype),
            pltpu.SemaphoreType.DMA((rows, n_tm)),
            pltpu.SemaphoreType.DMA((rows, n_tm)),
            pltpu.SemaphoreType.DMA((rows, n_bank)),
            pltpu.SemaphoreType.DMA((rows, n_bank)),
            pltpu.SemaphoreType.DMA((rows, 2, width)),
            pltpu.SemaphoreType.DMA((rows, 2, width)),
        ],
        compiler_params=pltpu.CompilerParams(collective_id=0, has_side_effects=True),
    )(x)


def mix_kernel(mix_ref, slots_ref, o_ref):
    rows, n, basis, cols = slots_ref.shape
    half = cols // 2
    mix_real = mix_ref[0]
    mix_imag = mix_ref[1]
    for t in range(rows):
        plain = slots_ref[t].reshape(n * basis, cols)
        from_real = jnp.dot(mix_real, plain, preferred_element_type=jnp.float32)
        from_imag = jnp.dot(mix_imag, plain, preferred_element_type=jnp.float32)
        o_ref[0, t] = (from_real[:, :half] - from_imag[:, half:]).astype(o_ref.dtype)
        o_ref[1, t] = (from_real[:, half:] + from_imag[:, :half]).astype(o_ref.dtype)


def mix(mixing, slots):
    rows, _, _, cols = slots.shape
    templates = mixing.shape[1]
    return pl.pallas_call(
        mix_kernel,
        out_shape=jax.ShapeDtypeStruct((2, rows, templates, cols // 2), jnp.bfloat16),
        in_specs=[pl.BlockSpec(memory_space=pltpu.VMEM)] * 2,
        out_specs=pl.BlockSpec(memory_space=pltpu.VMEM),
    )(mixing, slots)


def front_kernel(spec_ref, filt_ref, table_ref, tcos_ref, tsin_ref, wave_ref, o_ref, quarter):
    block, inner = filt_ref.shape[1], filt_ref.shape[2]
    spec_real = spec_ref[0]
    spec_imag = spec_ref[1]
    table = table_ref[...]
    twist_cos = tcos_ref[...]
    twist_sin = tsin_ref[...]
    for kk in range(block):
        filt_real = filt_ref[0, kk].astype(jnp.float32)
        filt_imag = filt_ref[1, kk].astype(jnp.float32)
        prod_real = spec_real * filt_real + spec_imag * filt_imag
        prod_imag = spec_imag * filt_real - spec_real * filt_imag
        packed = jnp.concatenate([prod_real, prod_imag], axis=0).astype(jnp.bfloat16)
        section = jnp.dot(table, packed, preferred_element_type=jnp.float32)
        section_real = section[:inner]
        section_imag = section[inner:]
        quarter_real = section_real * twist_cos - section_imag * twist_sin
        quarter_imag = section_real * twist_sin + section_imag * twist_cos
        width = quarter_real.shape[1]
        rows = pl.ds(kk * inner, inner)
        quarter[rows, pl.ds(0, width)] = quarter_real.astype(jnp.bfloat16)
        quarter[rows, pl.ds(width, width)] = quarter_imag.astype(jnp.bfloat16)
    wave = wave_ref[...]
    cols = wave.shape[1] // 2
    from_real = jnp.dot(quarter[:, :width], wave, preferred_element_type=jnp.float32)
    from_imag = jnp.dot(quarter[:, width:], wave, preferred_element_type=jnp.float32)
    result = jnp.concatenate(
        [from_real[:, :cols] - from_imag[:, cols:], from_real[:, cols:] + from_imag[:, :cols]], axis=1
    )
    o_ref[...] = result.reshape(o_ref.shape).astype(o_ref.dtype)


def front(spectrum, filters, table, twist_cos, twist_sin, wave, block=8):
    _, basis, inner, freq = filters.shape
    cols = wave.shape[1]
    whole = lambda *shape: pl.BlockSpec(shape, lambda i: (0,) * len(shape))
    return pl.pallas_call(
        front_kernel,
        grid=(basis // block,),
        out_shape=jax.ShapeDtypeStruct((basis, inner, cols), jnp.bfloat16),
        in_specs=[
            whole(2, inner, freq),
            pl.BlockSpec((2, block, inner, freq), lambda i: (0, i, 0, 0)),
            whole(2 * inner, 2 * inner),
            whole(inner, freq),
            whole(inner, freq),
            whole(freq, cols),
        ],
        out_specs=pl.BlockSpec((block, inner, cols), lambda i: (i, 0, 0)),
        scratch_shapes=[pltpu.VMEM((block * inner, 2 * freq), jnp.bfloat16)],
        compiler_params=pltpu.CompilerParams(vmem_limit_bytes=48 * 1024 * 1024),
    )(spectrum, filters, table, twist_cos, twist_sin, wave)


def on_device(spectrum, filters, mixing):
    tm_index = lax.axis_index("tm")
    local_freq = filters.shape[3]
    local_basis = filters.shape[1]
    inner = INNER
    outer = NSAMP // INNER
    table = first_table(inner)
    freqs = tm_index * local_freq + jnp.arange(local_freq, dtype=jnp.int32)
    twist_cos, twist_sin = twist_tables(freqs, inner, NSAMP)
    lags = START + jnp.arange(WROWS, dtype=jnp.int32)
    wave = wave_block(freqs, lags, outer)
    partial = front(spectrum, filters, table, twist_cos, twist_sin, wave).transpose(1, 0, 2)
    slots = exchange(partial, lax.axis_size("tm"), lax.axis_size("bank"), 4)
    return mix(mixing, slots)


def solution(mesh):
    return jax.shard_map(
        on_device,
        mesh=mesh,
        in_specs=(P(None, None, "tm"), P(None, "bank", None, "tm"), P(None, "bank", None)),
        out_specs=P(None, "tm", "bank", None),
        check_vma=False,
    )
```

```python
import functools
import math

import jax
import jax.numpy as jnp
from jax import lax
from jax.experimental import pallas as pl
from jax.experimental.pallas import tpu as pltpu
from jax.sharding import PartitionSpec as P

NSAMP = 1048576
INNER = 64
WROWS = 128
START = 8128


def first_table(inner):
    index = jnp.arange(inner, dtype=jnp.int32)
    phase = index[:, None] * index[None, :] % inner
    angle = phase.astype(jnp.float32) * (2.0 * math.pi / inner)
    cosine = jnp.cos(angle).astype(jnp.bfloat16)
    sine = jnp.sin(angle).astype(jnp.bfloat16)
    upper = jnp.concatenate([cosine, -sine], axis=1)
    lower = jnp.concatenate([sine, cosine], axis=1)
    return jnp.concatenate([upper, lower], axis=0)


def wave_block(freqs, lags, period):
    phase = freqs[:, None] * lags[None, :] % period
    angle = phase.astype(jnp.float32) * (2.0 * math.pi / period)
    cosine = jnp.cos(angle).astype(jnp.bfloat16)
    sine = jnp.sin(angle).astype(jnp.bfloat16)
    return jnp.concatenate([cosine, sine], axis=1)


def twist_tables(freqs, inner, total):
    rows_index = jnp.arange(inner, dtype=jnp.int32)
    phase = rows_index[:, None] * freqs[None, :] % total
    angle = phase.astype(jnp.float32) * (2.0 * math.pi / total)
    return (jnp.cos(angle), jnp.sin(angle))


MESH = pl.DeviceIdType.MESH


def exchange_kernel(width, x_ref, o_ref, plane_slots, part_buf, cross_slot, plane_send, plane_recv, cross_send,
                    cross_recv, gather_send, gather_recv, relay_send, relay_recv):
    plane = plane_slots.shape[2]
    n_bank = o_ref.shape[1]
    depth = n_bank // width
    rows, basis = o_ref.shape[0], o_ref.shape[2]
    half = basis // 2
    me_tm = lax.axis_index("tm")
    me_bank = lax.axis_index("bank")
    side = (me_tm // 2) % 2
    partner = me_tm + 2 - 4 * side
    in_plane = lambda q: (q // 2) * 4 + side * 2 + q % 2
    partner_of = lambda t: t + 2 - 4 * side
    me_q = (me_tm // 4) * 2 + me_tm % 2
    x = me_bank // depth
    z = me_bank % depth
    up = (z + 1) % depth
    down = (z + depth - 1) % depth
    at_tm = lambda peer: (peer, me_bank)
    at_bank = lambda peer: (me_tm, peer)
    near = [(x + step) % width * depth + z for step in range(1, width)]
    near += [xx * depth + up for xx in range(width)] + [xx * depth + down for xx in range(width)]
    barrier = pltpu.get_barrier_semaphore()
    for step in range(1, plane):
        pl.semaphore_signal(barrier, inc=1, device_id=at_tm(in_plane((me_q + step) % plane)), device_id_type=MESH)
    pl.semaphore_signal(barrier, inc=1, device_id=at_tm(partner), device_id_type=MESH)
    for peer in near:
        pl.semaphore_signal(barrier, inc=1, device_id=at_bank(peer), device_id_type=MESH)
    pl.semaphore_wait(barrier, plane + len(near))

    def remote(src, dst, send, recv, device):
        return pltpu.make_async_remote_copy(
            src_ref=src, dst_ref=dst, send_sem=send, recv_sem=recv, device_id=device, device_id_type=MESH
        )

    sends = []
    for r in range(rows):
        for step in range(1, plane):
            q = (me_q + step) % plane
            peer = in_plane(q)
            for which, owner in ((0, peer), (1, partner_of(peer))):
                copy = remote(
                    x_ref.at[owner * rows + r], plane_slots.at[r, which, me_q],
                    plane_send.at[r, which, q], plane_recv.at[r, which, me_q], at_tm(peer),
                )
                copy.start()
                sends.append(copy)

    def cross(r):
        return remote(part_buf.at[r], cross_slot.at[r], cross_send.at[r], cross_recv.at[r], at_tm(partner))

    def reduce_plane(r):
        own = x_ref[me_tm * rows + r].astype(jnp.float32)
        other = x_ref[partner * rows + r].astype(jnp.float32)
        for step in range(1, plane):
            q = (me_q + plane - step) % plane
            for which in (0, 1):
                remote(
                    x_ref.at[r], plane_slots.at[r, which, q],
                    plane_send.at[r, which, q], plane_recv.at[r, which, q], at_tm(in_plane(q)),
                ).wait_recv()
            own = own + plane_slots[r, 0, q].astype(jnp.float32)
            other = other + plane_slots[r, 1, q].astype(jnp.float32)
        part_buf[r] = other
        copy = cross(r)
        copy.start()
        sends.append(copy)
        return own

    def finish(r, own):
        cross(r).wait_recv()
        o_ref[r, me_bank] = (own + cross_slot[r]).astype(o_ref.dtype)
        for peer in near:
            copy = remote(
                o_ref.at[r, me_bank], o_ref.at[r, me_bank],
                gather_send.at[r, peer], gather_recv.at[r, me_bank], at_bank(peer),
            )
            copy.start()
            sends.append(copy)

    def forward(r):
        for source in near:
            remote(
                o_ref.at[r, source], o_ref.at[r, source],
                gather_send.at[r, source], gather_recv.at[r, source], at_bank(source),
            ).wait_recv()
        for xx in range(width):
            for slot, start, target, way in (
                (xx * depth + down, 0, x * depth + up, 0),
                (xx * depth + up, half, x * depth + down, 1),
            ):
                block = o_ref.at[r, slot, pl.ds(start, half)]
                copy = remote(block, block, relay_send.at[r, way, xx], relay_recv.at[r, way, xx], at_bank(target))
                copy.start()
                sends.append(copy)

    sums = [None] * rows
    for r in range(rows + 2):
        if r < rows:
            sums[r] = reduce_plane(r)
        if 1 <= r <= rows:
            finish(r - 1, sums[r - 1])
        if r >= 2:
            forward(r - 2)
    across = (z + 2) % depth
    for r in range(rows):
        for xx in range(width):
            for way, start, via in ((0, 0, down), (1, half, up)):
                block = o_ref.at[r, xx * depth + across, pl.ds(start, half)]
                remote(
                    block, block, relay_send.at[r, way, xx], relay_recv.at[r, way, xx], at_bank(x * depth + via)
                ).wait_recv()
    for copy in sends:
        copy.wait_send()


def exchange(x, n_tm, n_bank, width):
    rows = x.shape[0] // n_tm
    block = x.shape[1:]
    plane = n_tm // 2
    return pl.pallas_call(
        functools.partial(exchange_kernel, width),
        out_shape=jax.ShapeDtypeStruct((rows, n_bank) + block, x.dtype),
        in_specs=[pl.BlockSpec(memory_space=pltpu.VMEM)],
        out_specs=pl.BlockSpec(memory_space=pltpu.VMEM),
        scratch_shapes=[
            pltpu.VMEM((rows, 2, plane) + block, x.dtype),
            pltpu.VMEM((rows,) + block, jnp.float32),
            pltpu.VMEM((rows,) + block, jnp.float32),
            pltpu.SemaphoreType.DMA((rows, 2, plane)),
            pltpu.SemaphoreType.DMA((rows, 2, plane)),
            pltpu.SemaphoreType.DMA((rows,)),
            pltpu.SemaphoreType.DMA((rows,)),
            pltpu.SemaphoreType.DMA((rows, n_bank)),
            pltpu.SemaphoreType.DMA((rows, n_bank)),
            pltpu.SemaphoreType.DMA((rows, 2, width)),
            pltpu.SemaphoreType.DMA((rows, 2, width)),
        ],
        compiler_params=pltpu.CompilerParams(collective_id=0, has_side_effects=True),
    )(x)


def mix_kernel(mix_ref, slots_ref, o_ref):
    rows, n, basis, cols = slots_ref.shape
    half = cols // 2
    mix_real = mix_ref[0]
    mix_imag = mix_ref[1]
    for t in range(rows):
        plain = slots_ref[t].reshape(n * basis, cols)
        from_real = jnp.dot(mix_real, plain, preferred_element_type=jnp.float32)
        from_imag = jnp.dot(mix_imag, plain, preferred_element_type=jnp.float32)
        o_ref[0, t] = (from_real[:, :half] - from_imag[:, half:]).astype(o_ref.dtype)
        o_ref[1, t] = (from_real[:, half:] + from_imag[:, :half]).astype(o_ref.dtype)


def mix(mixing, slots):
    rows, _, _, cols = slots.shape
    templates = mixing.shape[1]
    return pl.pallas_call(
        mix_kernel,
        out_shape=jax.ShapeDtypeStruct((2, rows, templates, cols // 2), jnp.bfloat16),
        in_specs=[pl.BlockSpec(memory_space=pltpu.VMEM)] * 2,
        out_specs=pl.BlockSpec(memory_space=pltpu.VMEM),
    )(mixing, slots)


def front_kernel(spec_ref, filt_ref, table_ref, tcos_ref, tsin_ref, wave_ref, o_ref, quarter):
    block, inner = filt_ref.shape[1], filt_ref.shape[2]
    spec_real = spec_ref[0]
    spec_imag = spec_ref[1]
    table = table_ref[...]
    twist_cos = tcos_ref[...]
    twist_sin = tsin_ref[...]
    for kk in range(block):
        filt_real = filt_ref[0, kk].astype(jnp.float32)
        filt_imag = filt_ref[1, kk].astype(jnp.float32)
        prod_real = spec_real * filt_real + spec_imag * filt_imag
        prod_imag = spec_imag * filt_real - spec_real * filt_imag
        packed = jnp.concatenate([prod_real, prod_imag], axis=0).astype(jnp.bfloat16)
        section = jnp.dot(table, packed, preferred_element_type=jnp.float32)
        section_real = section[:inner]
        section_imag = section[inner:]
        quarter_real = section_real * twist_cos - section_imag * twist_sin
        quarter_imag = section_real * twist_sin + section_imag * twist_cos
        width = quarter_real.shape[1]
        rows = pl.ds(kk * inner, inner)
        quarter[rows, pl.ds(0, width)] = quarter_real.astype(jnp.bfloat16)
        quarter[rows, pl.ds(width, width)] = quarter_imag.astype(jnp.bfloat16)
    wave = wave_ref[...]
    cols = wave.shape[1] // 2
    from_real = jnp.dot(quarter[:, :width], wave, preferred_element_type=jnp.float32)
    from_imag = jnp.dot(quarter[:, width:], wave, preferred_element_type=jnp.float32)
    result = jnp.concatenate(
        [from_real[:, :cols] - from_imag[:, cols:], from_real[:, cols:] + from_imag[:, :cols]], axis=1
    )
    o_ref[...] = result.reshape(o_ref.shape).astype(o_ref.dtype)


def front(spectrum, filters, table, twist_cos, twist_sin, wave, block=8):
    _, basis, inner, freq = filters.shape
    cols = wave.shape[1]
    whole = lambda *shape: pl.BlockSpec(shape, lambda i: (0,) * len(shape))
    return pl.pallas_call(
        front_kernel,
        grid=(basis // block,),
        out_shape=jax.ShapeDtypeStruct((basis, inner, cols), jnp.bfloat16),
        in_specs=[
            whole(2, inner, freq),
            pl.BlockSpec((2, block, inner, freq), lambda i: (0, i, 0, 0)),
            whole(2 * inner, 2 * inner),
            whole(inner, freq),
            whole(inner, freq),
            whole(freq, cols),
        ],
        out_specs=pl.BlockSpec((block, inner, cols), lambda i: (i, 0, 0)),
        scratch_shapes=[pltpu.VMEM((block * inner, 2 * freq), jnp.bfloat16)],
        compiler_params=pltpu.CompilerParams(vmem_limit_bytes=48 * 1024 * 1024),
    )(spectrum, filters, table, twist_cos, twist_sin, wave)


def on_device(spectrum, filters, mixing):
    tm_index = lax.axis_index("tm")
    local_freq = filters.shape[3]
    local_basis = filters.shape[1]
    inner = INNER
    outer = NSAMP // INNER
    table = first_table(inner)
    freqs = tm_index * local_freq + jnp.arange(local_freq, dtype=jnp.int32)
    twist_cos, twist_sin = twist_tables(freqs, inner, NSAMP)
    lags = START + jnp.arange(WROWS, dtype=jnp.int32)
    wave = wave_block(freqs, lags, outer)
    partial = front(spectrum, filters, table, twist_cos, twist_sin, wave).transpose(1, 0, 2)
    slots = exchange(partial, lax.axis_size("tm"), lax.axis_size("bank"), 4)
    return mix(mixing, slots)


def solution(mesh):
    return jax.shard_map(
        on_device,
        mesh=mesh,
        in_specs=(P(None, None, "tm"), P(None, "bank", None, "tm"), P(None, "bank", None)),
        out_specs=P(None, "tm", "bank", None),
        check_vma=False,
    )
```

```python
import functools
import math

import jax
import jax.numpy as jnp
from jax import lax
from jax.experimental import pallas as pl
from jax.experimental.pallas import tpu as pltpu
from jax.sharding import PartitionSpec as P

NSAMP = 1048576
INNER = 64
WROWS = 128
START = 8128


def first_table(inner):
    index = jnp.arange(inner, dtype=jnp.int32)
    phase = index[:, None] * index[None, :] % inner
    angle = phase.astype(jnp.float32) * (2.0 * math.pi / inner)
    cosine = jnp.cos(angle).astype(jnp.bfloat16)
    sine = jnp.sin(angle).astype(jnp.bfloat16)
    upper = jnp.concatenate([cosine, -sine], axis=1)
    lower = jnp.concatenate([sine, cosine], axis=1)
    return jnp.concatenate([upper, lower], axis=0)


def wave_block(freqs, lags, period):
    phase = freqs[:, None] * lags[None, :] % period
    angle = phase.astype(jnp.float32) * (2.0 * math.pi / period)
    cosine = jnp.cos(angle).astype(jnp.bfloat16)
    sine = jnp.sin(angle).astype(jnp.bfloat16)
    return jnp.concatenate([cosine, sine], axis=1)


def twist_tables(freqs, inner, total):
    rows_index = jnp.arange(inner, dtype=jnp.int32)
    phase = rows_index[:, None] * freqs[None, :] % total
    angle = phase.astype(jnp.float32) * (2.0 * math.pi / total)
    return (jnp.cos(angle), jnp.sin(angle))


MESH = pl.DeviceIdType.MESH


def exchange_kernel(width, group, x_ref, o_ref, slots, scatter_send, scatter_recv, gather_send, gather_recv,
                    relay_send, relay_recv):
    n_tm, n_bank = slots.shape[1], o_ref.shape[0]
    depth = n_bank // width
    rows, basis = o_ref.shape[1], o_ref.shape[2]
    stages = rows // group
    half = basis // 2
    me_tm = lax.axis_index("tm")
    me_bank = lax.axis_index("bank")
    x = me_bank // depth
    z = me_bank % depth
    up = (z + 1) % depth
    down = (z + depth - 1) % depth
    at_tm = lambda peer: (peer, me_bank)
    at_bank = lambda peer: (me_tm, peer)
    near = [(x + step) % width * depth + z for step in range(1, width)]
    near += [xx * depth + up for xx in range(width)] + [xx * depth + down for xx in range(width)]
    barrier = pltpu.get_barrier_semaphore()
    for step in range(1, n_tm):
        pl.semaphore_signal(barrier, inc=1, device_id=at_tm((me_tm + step) % n_tm), device_id_type=MESH)
    for peer in near:
        pl.semaphore_signal(barrier, inc=1, device_id=at_bank(peer), device_id_type=MESH)
    pl.semaphore_wait(barrier, n_tm - 1 + len(near))

    def remote(src, dst, send, recv, device):
        return pltpu.make_async_remote_copy(
            src_ref=src, dst_ref=dst, send_sem=send, recv_sem=recv, device_id=device, device_id_type=MESH
        )

    def relays(g):
        out = []
        for xx in range(width):
            out.append((xx * depth + down, 0, x * depth + up, 0, xx))
            out.append((xx * depth + up, half, x * depth + down, 1, xx))
        return out

    sends = []
    for g in range(stages):
        part = pl.ds(g * group, group)
        for step in range(1, n_tm):
            peer = (me_tm + step) % n_tm
            copy = remote(
                x_ref.at[pl.ds(peer * rows + g * group, group)], slots.at[part, me_tm],
                scatter_send.at[g, peer], scatter_recv.at[g, me_tm], at_tm(peer),
            )
            copy.start()
            sends.append(copy)

    def forward(g):
        part = pl.ds(g * group, group)
        for source in near:
            remote(
                o_ref.at[source, part], o_ref.at[source, part],
                gather_send.at[g, source], gather_recv.at[g, source], at_bank(source),
            ).wait_recv()
        for slot, start, target, way, xx in relays(g):
            block = o_ref.at[slot, part, pl.ds(start, half)]
            copy = remote(block, block, relay_send.at[g, way, xx], relay_recv.at[g, way, xx], at_bank(target))
            copy.start()
            sends.append(copy)

    for g in range(stages):
        part = pl.ds(g * group, group)
        total = x_ref[pl.ds(me_tm * rows + g * group, group)].astype(jnp.float32)
        for step in range(1, n_tm):
            source = (me_tm + n_tm - step) % n_tm
            remote(
                x_ref.at[pl.ds(0, group)], slots.at[part, source],
                scatter_send.at[g, source], scatter_recv.at[g, source], at_tm(source),
            ).wait_recv()
            total = total + slots[part, source].astype(jnp.float32)
        o_ref[me_bank, part] = total.astype(o_ref.dtype)
        for peer in near:
            copy = remote(
                o_ref.at[me_bank, part], o_ref.at[me_bank, part],
                gather_send.at[g, peer], gather_recv.at[g, me_bank], at_bank(peer),
            )
            copy.start()
            sends.append(copy)
        if g >= 1:
            forward(g - 1)
    forward(stages - 1)
    across = (z + 2) % depth
    for g in range(stages):
        part = pl.ds(g * group, group)
        for xx in range(width):
            for way, start, via in ((0, 0, down), (1, half, up)):
                block = o_ref.at[xx * depth + across, part, pl.ds(start, half)]
                remote(
                    block, block, relay_send.at[g, way, xx], relay_recv.at[g, way, xx], at_bank(x * depth + via)
                ).wait_recv()
    for copy in sends:
        copy.wait_send()


def exchange(x, n_tm, n_bank, width, group=2):
    rows = x.shape[0] // n_tm
    stages = rows // group
    block = x.shape[1:]
    return pl.pallas_call(
        functools.partial(exchange_kernel, width, group),
        out_shape=jax.ShapeDtypeStruct((n_bank, rows) + block, x.dtype),
        in_specs=[pl.BlockSpec(memory_space=pltpu.VMEM)],
        out_specs=pl.BlockSpec(memory_space=pltpu.VMEM),
        scratch_shapes=[
            pltpu.VMEM((rows, n_tm) + block, x.dtype),
            pltpu.SemaphoreType.DMA((stages, n_tm)),
            pltpu.SemaphoreType.DMA((stages, n_tm)),
            pltpu.SemaphoreType.DMA((stages, n_bank)),
            pltpu.SemaphoreType.DMA((stages, n_bank)),
            pltpu.SemaphoreType.DMA((stages, 2, width)),
            pltpu.SemaphoreType.DMA((stages, 2, width)),
        ],
        compiler_params=pltpu.CompilerParams(collective_id=0, has_side_effects=True),
    )(x)


def mix_kernel(mix_ref, slots_ref, o_ref):
    n, rows, _, cols = slots_ref.shape
    half = cols // 2
    order = range(n)
    mix_real = mix_ref[0]
    mix_imag = mix_ref[1]
    for t in range(rows):
        plain = jnp.concatenate([slots_ref[slot, t] for slot in order], axis=0)
        turned = jnp.concatenate([-plain[:, half:], plain[:, :half]], axis=1)
        result = jnp.dot(mix_real, plain, preferred_element_type=jnp.float32) + jnp.dot(
            mix_imag, turned, preferred_element_type=jnp.float32
        )
        o_ref[0, t] = result[:, :half].astype(o_ref.dtype)
        o_ref[1, t] = result[:, half:].astype(o_ref.dtype)


def mix(mixing, slots):
    _, rows, _, cols = slots.shape
    templates = mixing.shape[1]
    return pl.pallas_call(
        mix_kernel,
        out_shape=jax.ShapeDtypeStruct((2, rows, templates, cols // 2), jnp.bfloat16),
        in_specs=[pl.BlockSpec(memory_space=pltpu.VMEM)] * 2,
        out_specs=pl.BlockSpec(memory_space=pltpu.VMEM),
    )(mixing, slots)


def front_kernel(spec_ref, filt_ref, table_ref, tcos_ref, tsin_ref, wave_ref, o_ref, quarter):
    block, inner = filt_ref.shape[1], filt_ref.shape[2]
    spec_real = spec_ref[0]
    spec_imag = spec_ref[1]
    table = table_ref[...]
    twist_cos = tcos_ref[...]
    twist_sin = tsin_ref[...]
    for kk in range(block):
        filt_real = filt_ref[0, kk].astype(jnp.float32)
        filt_imag = filt_ref[1, kk].astype(jnp.float32)
        prod_real = spec_real * filt_real + spec_imag * filt_imag
        prod_imag = spec_imag * filt_real - spec_real * filt_imag
        packed = jnp.concatenate([prod_real, prod_imag], axis=0).astype(jnp.bfloat16)
        section = jnp.dot(table, packed, preferred_element_type=jnp.float32)
        section_real = section[:inner]
        section_imag = section[inner:]
        quarter_real = section_real * twist_cos - section_imag * twist_sin
        quarter_imag = section_real * twist_sin + section_imag * twist_cos
        width = quarter_real.shape[1]
        rows = pl.ds(kk * inner, inner)
        quarter[rows, pl.ds(0, width)] = quarter_real.astype(jnp.bfloat16)
        quarter[rows, pl.ds(width, width)] = quarter_imag.astype(jnp.bfloat16)
    wave = wave_ref[...]
    cols = wave.shape[1] // 2
    from_real = jnp.dot(quarter[:, :width], wave, preferred_element_type=jnp.float32)
    from_imag = jnp.dot(quarter[:, width:], wave, preferred_element_type=jnp.float32)
    result = jnp.concatenate(
        [from_real[:, :cols] - from_imag[:, cols:], from_real[:, cols:] + from_imag[:, :cols]], axis=1
    )
    o_ref[...] = result.reshape(o_ref.shape).astype(o_ref.dtype)


def front(spectrum, filters, table, twist_cos, twist_sin, wave, block=8):
    _, basis, inner, freq = filters.shape
    cols = wave.shape[1]
    whole = lambda *shape: pl.BlockSpec(shape, lambda i: (0,) * len(shape))
    return pl.pallas_call(
        front_kernel,
        grid=(basis // block,),
        out_shape=jax.ShapeDtypeStruct((basis, inner, cols), jnp.bfloat16),
        in_specs=[
            whole(2, inner, freq),
            pl.BlockSpec((2, block, inner, freq), lambda i: (0, i, 0, 0)),
            whole(2 * inner, 2 * inner),
            whole(inner, freq),
            whole(inner, freq),
            whole(freq, cols),
        ],
        out_specs=pl.BlockSpec((block, inner, cols), lambda i: (i, 0, 0)),
        scratch_shapes=[pltpu.VMEM((block * inner, 2 * freq), jnp.bfloat16)],
        compiler_params=pltpu.CompilerParams(vmem_limit_bytes=48 * 1024 * 1024),
    )(spectrum, filters, table, twist_cos, twist_sin, wave)


def on_device(spectrum, filters, mixing):
    tm_index = lax.axis_index("tm")
    local_freq = filters.shape[3]
    local_basis = filters.shape[1]
    inner = INNER
    outer = NSAMP // INNER
    table = first_table(inner)
    freqs = tm_index * local_freq + jnp.arange(local_freq, dtype=jnp.int32)
    twist_cos, twist_sin = twist_tables(freqs, inner, NSAMP)
    lags = START + jnp.arange(WROWS, dtype=jnp.int32)
    wave = wave_block(freqs, lags, outer)
    partial = front(spectrum, filters, table, twist_cos, twist_sin, wave).transpose(1, 0, 2)
    slots = exchange(partial, lax.axis_size("tm"), lax.axis_size("bank"), 4)
    return mix(mixing, slots)


def solution(mesh):
    return jax.shard_map(
        on_device,
        mesh=mesh,
        in_specs=(P(None, None, "tm"), P(None, "bank", None, "tm"), P(None, "bank", None)),
        out_specs=P(None, "tm", "bank", None),
        check_vma=False,
    )
```

```python
import functools
import math

import jax
import jax.numpy as jnp
from jax import lax
from jax.experimental import pallas as pl
from jax.experimental.pallas import tpu as pltpu
from jax.sharding import PartitionSpec as P

NSAMP = 1048576
INNER = 64
WROWS = 128
START = 8128


def first_table(inner):
    index = jnp.arange(inner, dtype=jnp.int32)
    phase = index[:, None] * index[None, :] % inner
    angle = phase.astype(jnp.float32) * (2.0 * math.pi / inner)
    cosine = jnp.cos(angle).astype(jnp.bfloat16)
    sine = jnp.sin(angle).astype(jnp.bfloat16)
    upper = jnp.concatenate([cosine, -sine], axis=1)
    lower = jnp.concatenate([sine, cosine], axis=1)
    return jnp.concatenate([upper, lower], axis=0)


def wave_block(freqs, lags, period):
    phase = freqs[:, None] * lags[None, :] % period
    angle = phase.astype(jnp.float32) * (2.0 * math.pi / period)
    cosine = jnp.cos(angle).astype(jnp.bfloat16)
    sine = jnp.sin(angle).astype(jnp.bfloat16)
    return jnp.concatenate([cosine, sine], axis=1)


def twist_tables(freqs, inner, total):
    rows_index = jnp.arange(inner, dtype=jnp.int32)
    phase = rows_index[:, None] * freqs[None, :] % total
    angle = phase.astype(jnp.float32) * (2.0 * math.pi / total)
    return (jnp.cos(angle), jnp.sin(angle))


MESH = pl.DeviceIdType.MESH


def exchange_kernel(width, group, x_ref, o_ref, slots, scatter_send, scatter_recv, gather_send, gather_recv,
                    relay_send, relay_recv):
    n_tm, n_bank = slots.shape[1], o_ref.shape[0]
    depth = n_bank // width
    rows, basis = o_ref.shape[1], o_ref.shape[2]
    stages = rows // group
    half = basis // 2
    me_tm = lax.axis_index("tm")
    me_bank = lax.axis_index("bank")
    x = me_bank // depth
    z = me_bank % depth
    up = (z + 1) % depth
    down = (z + depth - 1) % depth
    at_tm = lambda peer: (peer, me_bank)
    at_bank = lambda peer: (me_tm, peer)
    near = [(x + step) % width * depth + z for step in range(1, width)]
    near += [xx * depth + up for xx in range(width)] + [xx * depth + down for xx in range(width)]
    barrier = pltpu.get_barrier_semaphore()
    for step in range(1, n_tm):
        pl.semaphore_signal(barrier, inc=1, device_id=at_tm((me_tm + step) % n_tm), device_id_type=MESH)
    for peer in near:
        pl.semaphore_signal(barrier, inc=1, device_id=at_bank(peer), device_id_type=MESH)
    pl.semaphore_wait(barrier, n_tm - 1 + len(near))

    def remote(src, dst, send, recv, device):
        return pltpu.make_async_remote_copy(
            src_ref=src, dst_ref=dst, send_sem=send, recv_sem=recv, device_id=device, device_id_type=MESH
        )

    def relays(g):
        out = []
        for xx in range(width):
            out.append((xx * depth + down, 0, x * depth + up, 0, xx))
            out.append((xx * depth + up, half, x * depth + down, 1, xx))
        return out

    sends = []
    for g in range(stages):
        part = pl.ds(g * group, group)
        for step in range(1, n_tm):
            peer = (me_tm + step) % n_tm
            copy = remote(
                x_ref.at[pl.ds(peer * rows + g * group, group)], slots.at[part, me_tm],
                scatter_send.at[g, peer], scatter_recv.at[g, me_tm], at_tm(peer),
            )
            copy.start()
            sends.append(copy)

    def forward(g):
        part = pl.ds(g * group, group)
        for source in near:
            remote(
                o_ref.at[source, part], o_ref.at[source, part],
                gather_send.at[g, source], gather_recv.at[g, source], at_bank(source),
            ).wait_recv()
        for slot, start, target, way, xx in relays(g):
            block = o_ref.at[slot, part, pl.ds(start, half)]
            copy = remote(block, block, relay_send.at[g, way, xx], relay_recv.at[g, way, xx], at_bank(target))
            copy.start()
            sends.append(copy)

    for g in range(stages):
        part = pl.ds(g * group, group)
        total = x_ref[pl.ds(me_tm * rows + g * group, group)].astype(jnp.float32)
        for step in range(1, n_tm):
            source = (me_tm + n_tm - step) % n_tm
            remote(
                x_ref.at[pl.ds(0, group)], slots.at[part, source],
                scatter_send.at[g, source], scatter_recv.at[g, source], at_tm(source),
            ).wait_recv()
            total = total + slots[part, source].astype(jnp.float32)
        o_ref[me_bank, part] = total.astype(o_ref.dtype)
        for peer in near:
            copy = remote(
                o_ref.at[me_bank, part], o_ref.at[me_bank, part],
                gather_send.at[g, peer], gather_recv.at[g, me_bank], at_bank(peer),
            )
            copy.start()
            sends.append(copy)
        if g >= 1:
            forward(g - 1)
    forward(stages - 1)
    across = (z + 2) % depth
    for g in range(stages):
        part = pl.ds(g * group, group)
        for xx in range(width):
            for way, start, via in ((0, 0, down), (1, half, up)):
                block = o_ref.at[xx * depth + across, part, pl.ds(start, half)]
                remote(
                    block, block, relay_send.at[g, way, xx], relay_recv.at[g, way, xx], at_bank(x * depth + via)
                ).wait_recv()
    for copy in sends:
        copy.wait_send()


def exchange(x, n_tm, n_bank, width, group=4):
    rows = x.shape[0] // n_tm
    stages = rows // group
    block = x.shape[1:]
    return pl.pallas_call(
        functools.partial(exchange_kernel, width, group),
        out_shape=jax.ShapeDtypeStruct((n_bank, rows) + block, x.dtype),
        in_specs=[pl.BlockSpec(memory_space=pltpu.VMEM)],
        out_specs=pl.BlockSpec(memory_space=pltpu.VMEM),
        scratch_shapes=[
            pltpu.VMEM((rows, n_tm) + block, x.dtype),
            pltpu.SemaphoreType.DMA((stages, n_tm)),
            pltpu.SemaphoreType.DMA((stages, n_tm)),
            pltpu.SemaphoreType.DMA((stages, n_bank)),
            pltpu.SemaphoreType.DMA((stages, n_bank)),
            pltpu.SemaphoreType.DMA((stages, 2, width)),
            pltpu.SemaphoreType.DMA((stages, 2, width)),
        ],
        compiler_params=pltpu.CompilerParams(collective_id=0, has_side_effects=True),
    )(x)


def mix_kernel(mix_ref, slots_ref, o_ref):
    n, rows, _, cols = slots_ref.shape
    half = cols // 2
    order = range(n)
    mix_real = mix_ref[0]
    mix_imag = mix_ref[1]
    for t in range(rows):
        plain = jnp.concatenate([slots_ref[slot, t] for slot in order], axis=0)
        turned = jnp.concatenate([-plain[:, half:], plain[:, :half]], axis=1)
        result = jnp.dot(mix_real, plain, preferred_element_type=jnp.float32) + jnp.dot(
            mix_imag, turned, preferred_element_type=jnp.float32
        )
        o_ref[0, t] = result[:, :half].astype(o_ref.dtype)
        o_ref[1, t] = result[:, half:].astype(o_ref.dtype)


def mix(mixing, slots):
    _, rows, _, cols = slots.shape
    templates = mixing.shape[1]
    return pl.pallas_call(
        mix_kernel,
        out_shape=jax.ShapeDtypeStruct((2, rows, templates, cols // 2), jnp.bfloat16),
        in_specs=[pl.BlockSpec(memory_space=pltpu.VMEM)] * 2,
        out_specs=pl.BlockSpec(memory_space=pltpu.VMEM),
    )(mixing, slots)


def front_kernel(spec_ref, filt_ref, table_ref, tcos_ref, tsin_ref, wave_ref, o_ref, quarter):
    block, inner = filt_ref.shape[1], filt_ref.shape[2]
    spec_real = spec_ref[0]
    spec_imag = spec_ref[1]
    table = table_ref[...]
    twist_cos = tcos_ref[...]
    twist_sin = tsin_ref[...]
    for kk in range(block):
        filt_real = filt_ref[0, kk].astype(jnp.float32)
        filt_imag = filt_ref[1, kk].astype(jnp.float32)
        prod_real = spec_real * filt_real + spec_imag * filt_imag
        prod_imag = spec_imag * filt_real - spec_real * filt_imag
        packed = jnp.concatenate([prod_real, prod_imag], axis=0).astype(jnp.bfloat16)
        section = jnp.dot(table, packed, preferred_element_type=jnp.float32)
        section_real = section[:inner]
        section_imag = section[inner:]
        quarter_real = section_real * twist_cos - section_imag * twist_sin
        quarter_imag = section_real * twist_sin + section_imag * twist_cos
        width = quarter_real.shape[1]
        rows = pl.ds(kk * inner, inner)
        quarter[rows, pl.ds(0, width)] = quarter_real.astype(jnp.bfloat16)
        quarter[rows, pl.ds(width, width)] = quarter_imag.astype(jnp.bfloat16)
    wave = wave_ref[...]
    cols = wave.shape[1] // 2
    from_real = jnp.dot(quarter[:, :width], wave, preferred_element_type=jnp.float32)
    from_imag = jnp.dot(quarter[:, width:], wave, preferred_element_type=jnp.float32)
    result = jnp.concatenate(
        [from_real[:, :cols] - from_imag[:, cols:], from_real[:, cols:] + from_imag[:, :cols]], axis=1
    )
    o_ref[...] = result.reshape(o_ref.shape).astype(o_ref.dtype)


def front(spectrum, filters, table, twist_cos, twist_sin, wave, block=8):
    _, basis, inner, freq = filters.shape
    cols = wave.shape[1]
    whole = lambda *shape: pl.BlockSpec(shape, lambda i: (0,) * len(shape))
    return pl.pallas_call(
        front_kernel,
        grid=(basis // block,),
        out_shape=jax.ShapeDtypeStruct((basis, inner, cols), jnp.bfloat16),
        in_specs=[
            whole(2, inner, freq),
            pl.BlockSpec((2, block, inner, freq), lambda i: (0, i, 0, 0)),
            whole(2 * inner, 2 * inner),
            whole(inner, freq),
            whole(inner, freq),
            whole(freq, cols),
        ],
        out_specs=pl.BlockSpec((block, inner, cols), lambda i: (i, 0, 0)),
        scratch_shapes=[pltpu.VMEM((block * inner, 2 * freq), jnp.bfloat16)],
        compiler_params=pltpu.CompilerParams(vmem_limit_bytes=48 * 1024 * 1024),
    )(spectrum, filters, table, twist_cos, twist_sin, wave)


def on_device(spectrum, filters, mixing):
    tm_index = lax.axis_index("tm")
    local_freq = filters.shape[3]
    local_basis = filters.shape[1]
    inner = INNER
    outer = NSAMP // INNER
    table = first_table(inner)
    freqs = tm_index * local_freq + jnp.arange(local_freq, dtype=jnp.int32)
    twist_cos, twist_sin = twist_tables(freqs, inner, NSAMP)
    lags = START + jnp.arange(WROWS, dtype=jnp.int32)
    wave = wave_block(freqs, lags, outer)
    partial = front(spectrum, filters, table, twist_cos, twist_sin, wave).transpose(1, 0, 2)
    slots = exchange(partial, lax.axis_size("tm"), lax.axis_size("bank"), 4)
    return mix(mixing, slots)


def solution(mesh):
    return jax.shard_map(
        on_device,
        mesh=mesh,
        in_specs=(P(None, None, "tm"), P(None, "bank", None, "tm"), P(None, "bank", None)),
        out_specs=P(None, "tm", "bank", None),
        check_vma=False,
    )
```

```python
import functools
import math

import jax
import jax.numpy as jnp
from jax import lax
from jax.experimental import pallas as pl
from jax.experimental.pallas import tpu as pltpu
from jax.sharding import PartitionSpec as P

NSAMP = 1048576
INNER = 64
WROWS = 128
START = 8128


def first_table(inner):
    index = jnp.arange(inner, dtype=jnp.int32)
    phase = index[:, None] * index[None, :] % inner
    angle = phase.astype(jnp.float32) * (2.0 * math.pi / inner)
    cosine = jnp.cos(angle).astype(jnp.bfloat16)
    sine = jnp.sin(angle).astype(jnp.bfloat16)
    upper = jnp.concatenate([cosine, -sine], axis=1)
    lower = jnp.concatenate([sine, cosine], axis=1)
    return jnp.concatenate([upper, lower], axis=0)


def wave_block(freqs, lags, period):
    phase = freqs[:, None] * lags[None, :] % period
    angle = phase.astype(jnp.float32) * (2.0 * math.pi / period)
    cosine = jnp.cos(angle).astype(jnp.bfloat16)
    sine = jnp.sin(angle).astype(jnp.bfloat16)
    return jnp.concatenate([cosine, sine], axis=1)


def twist_tables(freqs, inner, total):
    rows_index = jnp.arange(inner, dtype=jnp.int32)
    phase = rows_index[:, None] * freqs[None, :] % total
    angle = phase.astype(jnp.float32) * (2.0 * math.pi / total)
    return (jnp.cos(angle), jnp.sin(angle))


MESH = pl.DeviceIdType.MESH


def exchange_kernel(width, group, x_ref, o_ref, slots, scatter_send, scatter_recv, gather_send, gather_recv,
                    relay_send, relay_recv):
    n_tm, n_bank = slots.shape[1], o_ref.shape[0]
    depth = n_bank // width
    rows, basis = o_ref.shape[1], o_ref.shape[2]
    stages = rows // group
    half = basis // 2
    me_tm = lax.axis_index("tm")
    me_bank = lax.axis_index("bank")
    x = me_bank // depth
    z = me_bank % depth
    up = (z + 1) % depth
    down = (z + depth - 1) % depth
    at_tm = lambda peer: (peer, me_bank)
    at_bank = lambda peer: (me_tm, peer)
    near = [(x + step) % width * depth + z for step in range(1, width)]
    near += [xx * depth + up for xx in range(width)] + [xx * depth + down for xx in range(width)]
    barrier = pltpu.get_barrier_semaphore()
    for step in range(1, n_tm):
        pl.semaphore_signal(barrier, inc=1, device_id=at_tm((me_tm + step) % n_tm), device_id_type=MESH)
    for peer in near:
        pl.semaphore_signal(barrier, inc=1, device_id=at_bank(peer), device_id_type=MESH)
    pl.semaphore_wait(barrier, n_tm - 1 + len(near))

    def remote(src, dst, send, recv, device):
        return pltpu.make_async_remote_copy(
            src_ref=src, dst_ref=dst, send_sem=send, recv_sem=recv, device_id=device, device_id_type=MESH
        )

    def relays(g):
        out = []
        for xx in range(width):
            out.append((xx * depth + down, 0, x * depth + up, 0, xx))
            out.append((xx * depth + up, half, x * depth + down, 1, xx))
        return out

    sends = []
    for g in range(stages):
        part = pl.ds(g * group, group)
        for step in range(1, n_tm):
            peer = (me_tm + step) % n_tm
            copy = remote(
                x_ref.at[pl.ds(peer * rows + g * group, group)], slots.at[part, me_tm],
                scatter_send.at[g, peer], scatter_recv.at[g, me_tm], at_tm(peer),
            )
            copy.start()
            sends.append(copy)

    def forward(g):
        part = pl.ds(g * group, group)
        for source in near:
            remote(
                o_ref.at[source, part], o_ref.at[source, part],
                gather_send.at[g, source], gather_recv.at[g, source], at_bank(source),
            ).wait_recv()
        for slot, start, target, way, xx in relays(g):
            block = o_ref.at[slot, part, pl.ds(start, half)]
            copy = remote(block, block, relay_send.at[g, way, xx], relay_recv.at[g, way, xx], at_bank(target))
            copy.start()
            sends.append(copy)

    for g in range(stages):
        part = pl.ds(g * group, group)
        total = x_ref[pl.ds(me_tm * rows + g * group, group)].astype(jnp.float32)
        for step in range(1, n_tm):
            source = (me_tm + n_tm - step) % n_tm
            remote(
                x_ref.at[pl.ds(0, group)], slots.at[part, source],
                scatter_send.at[g, source], scatter_recv.at[g, source], at_tm(source),
            ).wait_recv()
            total = total + slots[part, source].astype(jnp.float32)
        o_ref[me_bank, part] = total.astype(o_ref.dtype)
        for peer in near:
            copy = remote(
                o_ref.at[me_bank, part], o_ref.at[me_bank, part],
                gather_send.at[g, peer], gather_recv.at[g, me_bank], at_bank(peer),
            )
            copy.start()
            sends.append(copy)
        if g >= 1:
            forward(g - 1)
    forward(stages - 1)
    across = (z + 2) % depth
    for g in range(stages):
        part = pl.ds(g * group, group)
        for xx in range(width):
            for way, start, via in ((0, 0, down), (1, half, up)):
                block = o_ref.at[xx * depth + across, part, pl.ds(start, half)]
                remote(
                    block, block, relay_send.at[g, way, xx], relay_recv.at[g, way, xx], at_bank(x * depth + via)
                ).wait_recv()
    for copy in sends:
        copy.wait_send()


def exchange(x, n_tm, n_bank, width, group=2):
    rows = x.shape[0] // n_tm
    stages = rows // group
    block = x.shape[1:]
    return pl.pallas_call(
        functools.partial(exchange_kernel, width, group),
        out_shape=jax.ShapeDtypeStruct((n_bank, rows) + block, x.dtype),
        in_specs=[pl.BlockSpec(memory_space=pltpu.VMEM)],
        out_specs=pl.BlockSpec(memory_space=pltpu.VMEM),
        scratch_shapes=[
            pltpu.VMEM((rows, n_tm) + block, x.dtype),
            pltpu.SemaphoreType.DMA((stages, n_tm)),
            pltpu.SemaphoreType.DMA((stages, n_tm)),
            pltpu.SemaphoreType.DMA((stages, n_bank)),
            pltpu.SemaphoreType.DMA((stages, n_bank)),
            pltpu.SemaphoreType.DMA((stages, 2, width)),
            pltpu.SemaphoreType.DMA((stages, 2, width)),
        ],
        compiler_params=pltpu.CompilerParams(collective_id=0, has_side_effects=True),
    )(x)


def mix_kernel(mix_ref, slots_ref, o_ref):
    n, rows, _, cols = slots_ref.shape
    half = cols // 2
    order = range(n)
    mix_real = mix_ref[0]
    mix_imag = mix_ref[1]
    for t in range(rows):
        plain = jnp.concatenate([slots_ref[slot, t] for slot in order], axis=0)
        turned = jnp.concatenate([-plain[:, half:], plain[:, :half]], axis=1)
        result = jnp.dot(mix_real, plain, preferred_element_type=jnp.float32) + jnp.dot(
            mix_imag, turned, preferred_element_type=jnp.float32
        )
        o_ref[0, t] = result[:, :half].astype(o_ref.dtype)
        o_ref[1, t] = result[:, half:].astype(o_ref.dtype)


def mix(mixing, slots):
    _, rows, _, cols = slots.shape
    templates = mixing.shape[1]
    return pl.pallas_call(
        mix_kernel,
        out_shape=jax.ShapeDtypeStruct((2, rows, templates, cols // 2), jnp.bfloat16),
        in_specs=[pl.BlockSpec(memory_space=pltpu.VMEM)] * 2,
        out_specs=pl.BlockSpec(memory_space=pltpu.VMEM),
    )(mixing, slots)


def front_kernel(spec_ref, filt_ref, table_ref, tcos_ref, tsin_ref, wave_ref, o_ref, quarter):
    block, inner = filt_ref.shape[1], filt_ref.shape[2]
    spec_real = spec_ref[0]
    spec_imag = spec_ref[1]
    table = table_ref[...]
    twist_cos = tcos_ref[...]
    twist_sin = tsin_ref[...]
    for kk in range(block):
        filt_real = filt_ref[0, kk].astype(jnp.float32)
        filt_imag = filt_ref[1, kk].astype(jnp.float32)
        prod_real = spec_real * filt_real + spec_imag * filt_imag
        prod_imag = spec_imag * filt_real - spec_real * filt_imag
        packed = jnp.concatenate([prod_real, prod_imag], axis=0).astype(jnp.bfloat16)
        section = jnp.dot(table, packed, preferred_element_type=jnp.float32)
        section_real = section[:inner]
        section_imag = section[inner:]
        quarter_real = section_real * twist_cos - section_imag * twist_sin
        quarter_imag = section_real * twist_sin + section_imag * twist_cos
        width = quarter_real.shape[1]
        rows = pl.ds(kk * inner, inner)
        quarter[rows, pl.ds(0, width)] = quarter_real.astype(jnp.bfloat16)
        quarter[rows, pl.ds(width, width)] = quarter_imag.astype(jnp.bfloat16)
    wave = wave_ref[...]
    cols = wave.shape[1] // 2
    from_real = jnp.dot(quarter[:, :width], wave, preferred_element_type=jnp.float32)
    from_imag = jnp.dot(quarter[:, width:], wave, preferred_element_type=jnp.float32)
    result = jnp.concatenate(
        [from_real[:, :cols] - from_imag[:, cols:], from_real[:, cols:] + from_imag[:, :cols]], axis=1
    )
    o_ref[...] = result.reshape(o_ref.shape).astype(o_ref.dtype)


def front(spectrum, filters, table, twist_cos, twist_sin, wave, block=16):
    _, basis, inner, freq = filters.shape
    cols = wave.shape[1]
    whole = lambda *shape: pl.BlockSpec(shape, lambda i: (0,) * len(shape))
    return pl.pallas_call(
        front_kernel,
        grid=(basis // block,),
        out_shape=jax.ShapeDtypeStruct((basis, inner, cols), jnp.bfloat16),
        in_specs=[
            whole(2, inner, freq),
            pl.BlockSpec((2, block, inner, freq), lambda i: (0, i, 0, 0)),
            whole(2 * inner, 2 * inner),
            whole(inner, freq),
            whole(inner, freq),
            whole(freq, cols),
        ],
        out_specs=pl.BlockSpec((block, inner, cols), lambda i: (i, 0, 0)),
        scratch_shapes=[pltpu.VMEM((block * inner, 2 * freq), jnp.bfloat16)],
        compiler_params=pltpu.CompilerParams(vmem_limit_bytes=48 * 1024 * 1024),
    )(spectrum, filters, table, twist_cos, twist_sin, wave)


def on_device(spectrum, filters, mixing):
    tm_index = lax.axis_index("tm")
    local_freq = filters.shape[3]
    local_basis = filters.shape[1]
    inner = INNER
    outer = NSAMP // INNER
    table = first_table(inner)
    freqs = tm_index * local_freq + jnp.arange(local_freq, dtype=jnp.int32)
    twist_cos, twist_sin = twist_tables(freqs, inner, NSAMP)
    lags = START + jnp.arange(WROWS, dtype=jnp.int32)
    wave = wave_block(freqs, lags, outer)
    partial = front(spectrum, filters, table, twist_cos, twist_sin, wave).transpose(1, 0, 2)
    slots = exchange(partial, lax.axis_size("tm"), lax.axis_size("bank"), 4)
    return mix(mixing, slots)


def solution(mesh):
    return jax.shard_map(
        on_device,
        mesh=mesh,
        in_specs=(P(None, None, "tm"), P(None, "bank", None, "tm"), P(None, "bank", None)),
        out_specs=P(None, "tm", "bank", None),
        check_vma=False,
    )
```

```python
import functools
import math

import jax
import jax.numpy as jnp
from jax import lax
from jax.experimental import pallas as pl
from jax.experimental.pallas import tpu as pltpu
from jax.sharding import PartitionSpec as P

NSAMP = 1048576
INNER = 64
WROWS = 128
START = 8128


def first_table(inner):
    index = jnp.arange(inner, dtype=jnp.int32)
    phase = index[:, None] * index[None, :] % inner
    angle = phase.astype(jnp.float32) * (2.0 * math.pi / inner)
    cosine = jnp.cos(angle).astype(jnp.bfloat16)
    sine = jnp.sin(angle).astype(jnp.bfloat16)
    upper = jnp.concatenate([cosine, -sine], axis=1)
    lower = jnp.concatenate([sine, cosine], axis=1)
    return jnp.concatenate([upper, lower], axis=0)


def wave_block(freqs, lags, period):
    phase = freqs[:, None] * lags[None, :] % period
    angle = phase.astype(jnp.float32) * (2.0 * math.pi / period)
    cosine = jnp.cos(angle).astype(jnp.bfloat16)
    sine = jnp.sin(angle).astype(jnp.bfloat16)
    return jnp.concatenate([cosine, sine], axis=1)


def twist_tables(freqs, inner, total):
    rows_index = jnp.arange(inner, dtype=jnp.int32)
    phase = rows_index[:, None] * freqs[None, :] % total
    angle = phase.astype(jnp.float32) * (2.0 * math.pi / total)
    return (jnp.cos(angle), jnp.sin(angle))


MESH = pl.DeviceIdType.MESH


def exchange_kernel(width, group, x_ref, o_ref, slots, scatter_send, scatter_recv, gather_send, gather_recv,
                    relay_send, relay_recv):
    n_tm, n_bank = slots.shape[1], o_ref.shape[0]
    depth = n_bank // width
    rows, basis = o_ref.shape[1], o_ref.shape[2]
    stages = rows // group
    half = basis // 2
    me_tm = lax.axis_index("tm")
    me_bank = lax.axis_index("bank")
    x = me_bank // depth
    z = me_bank % depth
    up = (z + 1) % depth
    down = (z + depth - 1) % depth
    at_tm = lambda peer: (peer, me_bank)
    at_bank = lambda peer: (me_tm, peer)
    near = [(x + step) % width * depth + z for step in range(1, width)]
    near += [xx * depth + up for xx in range(width)] + [xx * depth + down for xx in range(width)]
    barrier = pltpu.get_barrier_semaphore()
    for step in range(1, n_tm):
        pl.semaphore_signal(barrier, inc=1, device_id=at_tm((me_tm + step) % n_tm), device_id_type=MESH)
    for peer in near:
        pl.semaphore_signal(barrier, inc=1, device_id=at_bank(peer), device_id_type=MESH)
    pl.semaphore_wait(barrier, n_tm - 1 + len(near))

    def remote(src, dst, send, recv, device):
        return pltpu.make_async_remote_copy(
            src_ref=src, dst_ref=dst, send_sem=send, recv_sem=recv, device_id=device, device_id_type=MESH
        )

    def relays(g):
        out = []
        for xx in range(width):
            out.append((xx * depth + down, 0, x * depth + up, 0, xx))
            out.append((xx * depth + up, half, x * depth + down, 1, xx))
        return out

    sends = []
    for g in range(stages):
        part = pl.ds(g * group, group)
        for step in range(1, n_tm):
            peer = (me_tm + step) % n_tm
            copy = remote(
                x_ref.at[pl.ds(peer * rows + g * group, group)], slots.at[part, me_tm],
                scatter_send.at[g, peer], scatter_recv.at[g, me_tm], at_tm(peer),
            )
            copy.start()
            sends.append(copy)

    def forward(g):
        part = pl.ds(g * group, group)
        for source in near:
            remote(
                o_ref.at[source, part], o_ref.at[source, part],
                gather_send.at[g, source], gather_recv.at[g, source], at_bank(source),
            ).wait_recv()
        for slot, start, target, way, xx in relays(g):
            block = o_ref.at[slot, part, pl.ds(start, half)]
            copy = remote(block, block, relay_send.at[g, way, xx], relay_recv.at[g, way, xx], at_bank(target))
            copy.start()
            sends.append(copy)

    for g in range(stages):
        part = pl.ds(g * group, group)
        total = x_ref[pl.ds(me_tm * rows + g * group, group)].astype(jnp.float32)
        for step in range(1, n_tm):
            source = (me_tm + n_tm - step) % n_tm
            remote(
                x_ref.at[pl.ds(0, group)], slots.at[part, source],
                scatter_send.at[g, source], scatter_recv.at[g, source], at_tm(source),
            ).wait_recv()
            total = total + slots[part, source].astype(jnp.float32)
        o_ref[me_bank, part] = total.astype(o_ref.dtype)
        for peer in near:
            copy = remote(
                o_ref.at[me_bank, part], o_ref.at[me_bank, part],
                gather_send.at[g, peer], gather_recv.at[g, me_bank], at_bank(peer),
            )
            copy.start()
            sends.append(copy)
        if g >= 1:
            forward(g - 1)
    forward(stages - 1)
    across = (z + 2) % depth
    for g in range(stages):
        part = pl.ds(g * group, group)
        for xx in range(width):
            for way, start, via in ((0, 0, down), (1, half, up)):
                block = o_ref.at[xx * depth + across, part, pl.ds(start, half)]
                remote(
                    block, block, relay_send.at[g, way, xx], relay_recv.at[g, way, xx], at_bank(x * depth + via)
                ).wait_recv()
    for copy in sends:
        copy.wait_send()


def exchange(x, n_tm, n_bank, width, group=2):
    rows = x.shape[0] // n_tm
    stages = rows // group
    block = x.shape[1:]
    return pl.pallas_call(
        functools.partial(exchange_kernel, width, group),
        out_shape=jax.ShapeDtypeStruct((n_bank, rows) + block, x.dtype),
        in_specs=[pl.BlockSpec(memory_space=pltpu.VMEM)],
        out_specs=pl.BlockSpec(memory_space=pltpu.VMEM),
        scratch_shapes=[
            pltpu.VMEM((rows, n_tm) + block, x.dtype),
            pltpu.SemaphoreType.DMA((stages, n_tm)),
            pltpu.SemaphoreType.DMA((stages, n_tm)),
            pltpu.SemaphoreType.DMA((stages, n_bank)),
            pltpu.SemaphoreType.DMA((stages, n_bank)),
            pltpu.SemaphoreType.DMA((stages, 2, width)),
            pltpu.SemaphoreType.DMA((stages, 2, width)),
        ],
        compiler_params=pltpu.CompilerParams(collective_id=0, has_side_effects=True),
    )(x)


def mix_kernel(mix_ref, slots_ref, o_ref):
    n, rows, _, cols = slots_ref.shape
    half = cols // 2
    order = range(n)
    mix_real = mix_ref[0]
    mix_imag = mix_ref[1]
    for t in range(rows):
        plain = jnp.concatenate([slots_ref[slot, t] for slot in order], axis=0)
        turned = jnp.concatenate([-plain[:, half:], plain[:, :half]], axis=1)
        result = jnp.dot(mix_real, plain, preferred_element_type=jnp.float32) + jnp.dot(
            mix_imag, turned, preferred_element_type=jnp.float32
        )
        o_ref[0, t] = result[:, :half].astype(o_ref.dtype)
        o_ref[1, t] = result[:, half:].astype(o_ref.dtype)


def mix(mixing, slots):
    _, rows, _, cols = slots.shape
    templates = mixing.shape[1]
    return pl.pallas_call(
        mix_kernel,
        out_shape=jax.ShapeDtypeStruct((2, rows, templates, cols // 2), jnp.bfloat16),
        in_specs=[pl.BlockSpec(memory_space=pltpu.VMEM)] * 2,
        out_specs=pl.BlockSpec(memory_space=pltpu.VMEM),
    )(mixing, slots)


def front_kernel(spec_ref, filt_ref, table_ref, tcos_ref, tsin_ref, wave_ref, o_ref, quarter):
    block, inner = filt_ref.shape[1], filt_ref.shape[2]
    spec_real = spec_ref[0]
    spec_imag = spec_ref[1]
    table = table_ref[...]
    twist_cos = tcos_ref[...]
    twist_sin = tsin_ref[...]
    for kk in range(block):
        filt_real = filt_ref[0, kk].astype(jnp.float32)
        filt_imag = filt_ref[1, kk].astype(jnp.float32)
        prod_real = spec_real * filt_real + spec_imag * filt_imag
        prod_imag = spec_imag * filt_real - spec_real * filt_imag
        packed = jnp.concatenate([prod_real, prod_imag], axis=0).astype(jnp.bfloat16)
        section = jnp.dot(table, packed, preferred_element_type=jnp.float32)
        section_real = section[:inner]
        section_imag = section[inner:]
        quarter_real = section_real * twist_cos - section_imag * twist_sin
        quarter_imag = section_real * twist_sin + section_imag * twist_cos
        width = quarter_real.shape[1]
        rows = pl.ds(kk * inner, inner)
        quarter[rows, pl.ds(0, width)] = quarter_real.astype(jnp.bfloat16)
        quarter[rows, pl.ds(width, width)] = quarter_imag.astype(jnp.bfloat16)
    wave = wave_ref[...]
    cols = wave.shape[1] // 2
    from_real = jnp.dot(quarter[:, :width], wave, preferred_element_type=jnp.float32)
    from_imag = jnp.dot(quarter[:, width:], wave, preferred_element_type=jnp.float32)
    result = jnp.concatenate(
        [from_real[:, :cols] - from_imag[:, cols:], from_real[:, cols:] + from_imag[:, :cols]], axis=1
    )
    for kk in range(block):
        o_ref[:, kk, :] = result[kk * inner:(kk + 1) * inner].astype(o_ref.dtype)


def front(spectrum, filters, table, twist_cos, twist_sin, wave, block=8):
    _, basis, inner, freq = filters.shape
    cols = wave.shape[1]
    whole = lambda *shape: pl.BlockSpec(shape, lambda i: (0,) * len(shape))
    return pl.pallas_call(
        front_kernel,
        grid=(basis // block,),
        out_shape=jax.ShapeDtypeStruct((inner, basis, cols), jnp.bfloat16),
        in_specs=[
            whole(2, inner, freq),
            pl.BlockSpec((2, block, inner, freq), lambda i: (0, i, 0, 0)),
            whole(2 * inner, 2 * inner),
            whole(inner, freq),
            whole(inner, freq),
            whole(freq, cols),
        ],
        out_specs=pl.BlockSpec((inner, block, cols), lambda i: (0, i, 0)),
        scratch_shapes=[pltpu.VMEM((block * inner, 2 * freq), jnp.bfloat16)],
        compiler_params=pltpu.CompilerParams(vmem_limit_bytes=48 * 1024 * 1024),
    )(spectrum, filters, table, twist_cos, twist_sin, wave)


def on_device(spectrum, filters, mixing):
    tm_index = lax.axis_index("tm")
    local_freq = filters.shape[3]
    local_basis = filters.shape[1]
    inner = INNER
    outer = NSAMP // INNER
    table = first_table(inner)
    freqs = tm_index * local_freq + jnp.arange(local_freq, dtype=jnp.int32)
    twist_cos, twist_sin = twist_tables(freqs, inner, NSAMP)
    lags = START + jnp.arange(WROWS, dtype=jnp.int32)
    wave = wave_block(freqs, lags, outer)
    partial = front(spectrum, filters, table, twist_cos, twist_sin, wave)
    slots = exchange(partial, lax.axis_size("tm"), lax.axis_size("bank"), 4)
    return mix(mixing, slots)


def solution(mesh):
    return jax.shard_map(
        on_device,
        mesh=mesh,
        in_specs=(P(None, None, "tm"), P(None, "bank", None, "tm"), P(None, "bank", None)),
        out_specs=P(None, "tm", "bank", None),
        check_vma=False,
    )
```

```python
import functools
import math

import jax
import jax.numpy as jnp
from jax import lax
from jax.experimental import pallas as pl
from jax.experimental.pallas import tpu as pltpu
from jax.sharding import PartitionSpec as P

NSAMP = 1048576
INNER = 64
WROWS = 128
START = 8128


def first_table(inner):
    index = jnp.arange(inner, dtype=jnp.int32)
    phase = index[:, None] * index[None, :] % inner
    angle = phase.astype(jnp.float32) * (2.0 * math.pi / inner)
    cosine = jnp.cos(angle).astype(jnp.bfloat16)
    sine = jnp.sin(angle).astype(jnp.bfloat16)
    upper = jnp.concatenate([cosine, -sine], axis=1)
    lower = jnp.concatenate([sine, cosine], axis=1)
    return jnp.concatenate([upper, lower], axis=0)


def wave_block(freqs, lags, period):
    phase = freqs[:, None] * lags[None, :] % period
    angle = phase.astype(jnp.float32) * (2.0 * math.pi / period)
    cosine = jnp.cos(angle).astype(jnp.bfloat16)
    sine = jnp.sin(angle).astype(jnp.bfloat16)
    return jnp.concatenate([cosine, sine], axis=1)


def twist_tables(freqs, inner, total):
    rows_index = jnp.arange(inner, dtype=jnp.int32)
    phase = rows_index[:, None] * freqs[None, :] % total
    angle = phase.astype(jnp.float32) * (2.0 * math.pi / total)
    return (jnp.cos(angle), jnp.sin(angle))


MESH = pl.DeviceIdType.MESH


def exchange_kernel(width, group, x_ref, o_ref, slots, scatter_send, scatter_recv, gather_send, gather_recv,
                    relay_send, relay_recv):
    n_tm, n_bank = slots.shape[1], o_ref.shape[0]
    depth = n_bank // width
    rows, basis = o_ref.shape[1], o_ref.shape[2]
    stages = rows // group
    half = basis // 2
    me_tm = lax.axis_index("tm")
    me_bank = lax.axis_index("bank")
    x = me_bank // depth
    z = me_bank % depth
    up = (z + 1) % depth
    down = (z + depth - 1) % depth
    at_tm = lambda peer: (peer, me_bank)
    at_bank = lambda peer: (me_tm, peer)
    near = [xx * depth + up for xx in range(width)] + [xx * depth + down for xx in range(width)]
    near += [(x + step) % width * depth + z for step in range(1, width)]
    barrier = pltpu.get_barrier_semaphore()
    for step in range(1, n_tm):
        pl.semaphore_signal(barrier, inc=1, device_id=at_tm((me_tm + step) % n_tm), device_id_type=MESH)
    for peer in near:
        pl.semaphore_signal(barrier, inc=1, device_id=at_bank(peer), device_id_type=MESH)
    pl.semaphore_wait(barrier, n_tm - 1 + len(near))

    def remote(src, dst, send, recv, device):
        return pltpu.make_async_remote_copy(
            src_ref=src, dst_ref=dst, send_sem=send, recv_sem=recv, device_id=device, device_id_type=MESH
        )

    def relays(g):
        out = []
        for xx in range(width):
            out.append((xx * depth + down, 0, x * depth + up, 0, xx))
            out.append((xx * depth + up, half, x * depth + down, 1, xx))
        return out

    sends = []
    for g in range(stages):
        part = pl.ds(g * group, group)
        for step in range(1, n_tm):
            peer = (me_tm + step) % n_tm
            copy = remote(
                x_ref.at[pl.ds(peer * rows + g * group, group)], slots.at[part, me_tm],
                scatter_send.at[g, peer], scatter_recv.at[g, me_tm], at_tm(peer),
            )
            copy.start()
            sends.append(copy)

    def forward(g):
        part = pl.ds(g * group, group)
        for source in near:
            remote(
                o_ref.at[source, part], o_ref.at[source, part],
                gather_send.at[g, source], gather_recv.at[g, source], at_bank(source),
            ).wait_recv()
        for slot, start, target, way, xx in relays(g):
            block = o_ref.at[slot, part, pl.ds(start, half)]
            copy = remote(block, block, relay_send.at[g, way, xx], relay_recv.at[g, way, xx], at_bank(target))
            copy.start()
            sends.append(copy)

    for g in range(stages):
        part = pl.ds(g * group, group)
        total = x_ref[pl.ds(me_tm * rows + g * group, group)].astype(jnp.float32)
        for step in range(1, n_tm):
            source = (me_tm + n_tm - step) % n_tm
            remote(
                x_ref.at[pl.ds(0, group)], slots.at[part, source],
                scatter_send.at[g, source], scatter_recv.at[g, source], at_tm(source),
            ).wait_recv()
            total = total + slots[part, source].astype(jnp.float32)
        o_ref[me_bank, part] = total.astype(o_ref.dtype)
        for peer in near:
            copy = remote(
                o_ref.at[me_bank, part], o_ref.at[me_bank, part],
                gather_send.at[g, peer], gather_recv.at[g, me_bank], at_bank(peer),
            )
            copy.start()
            sends.append(copy)
        if g >= 1:
            forward(g - 1)
    forward(stages - 1)
    across = (z + 2) % depth
    for g in range(stages):
        part = pl.ds(g * group, group)
        for xx in range(width):
            for way, start, via in ((0, 0, down), (1, half, up)):
                block = o_ref.at[xx * depth + across, part, pl.ds(start, half)]
                remote(
                    block, block, relay_send.at[g, way, xx], relay_recv.at[g, way, xx], at_bank(x * depth + via)
                ).wait_recv()
    for copy in sends:
        copy.wait_send()


def exchange(x, n_tm, n_bank, width, group=2):
    rows = x.shape[0] // n_tm
    stages = rows // group
    block = x.shape[1:]
    return pl.pallas_call(
        functools.partial(exchange_kernel, width, group),
        out_shape=jax.ShapeDtypeStruct((n_bank, rows) + block, x.dtype),
        in_specs=[pl.BlockSpec(memory_space=pltpu.VMEM)],
        out_specs=pl.BlockSpec(memory_space=pltpu.VMEM),
        scratch_shapes=[
            pltpu.VMEM((rows, n_tm) + block, x.dtype),
            pltpu.SemaphoreType.DMA((stages, n_tm)),
            pltpu.SemaphoreType.DMA((stages, n_tm)),
            pltpu.SemaphoreType.DMA((stages, n_bank)),
            pltpu.SemaphoreType.DMA((stages, n_bank)),
            pltpu.SemaphoreType.DMA((stages, 2, width)),
            pltpu.SemaphoreType.DMA((stages, 2, width)),
        ],
        compiler_params=pltpu.CompilerParams(collective_id=0, has_side_effects=True),
    )(x)


def mix_kernel(mix_ref, slots_ref, o_ref):
    n, rows, _, cols = slots_ref.shape
    half = cols // 2
    order = range(n)
    mix_real = mix_ref[0]
    mix_imag = mix_ref[1]
    for t in range(rows):
        plain = jnp.concatenate([slots_ref[slot, t] for slot in order], axis=0)
        turned = jnp.concatenate([-plain[:, half:], plain[:, :half]], axis=1)
        result = jnp.dot(mix_real, plain, preferred_element_type=jnp.float32) + jnp.dot(
            mix_imag, turned, preferred_element_type=jnp.float32
        )
        o_ref[0, t] = result[:, :half].astype(o_ref.dtype)
        o_ref[1, t] = result[:, half:].astype(o_ref.dtype)


def mix(mixing, slots):
    _, rows, _, cols = slots.shape
    templates = mixing.shape[1]
    return pl.pallas_call(
        mix_kernel,
        out_shape=jax.ShapeDtypeStruct((2, rows, templates, cols // 2), jnp.bfloat16),
        in_specs=[pl.BlockSpec(memory_space=pltpu.VMEM)] * 2,
        out_specs=pl.BlockSpec(memory_space=pltpu.VMEM),
    )(mixing, slots)


def front_kernel(spec_ref, filt_ref, table_ref, tcos_ref, tsin_ref, wave_ref, o_ref, quarter):
    block, inner = filt_ref.shape[1], filt_ref.shape[2]
    spec_real = spec_ref[0]
    spec_imag = spec_ref[1]
    table = table_ref[...]
    twist_cos = tcos_ref[...]
    twist_sin = tsin_ref[...]
    for kk in range(block):
        filt_real = filt_ref[0, kk].astype(jnp.float32)
        filt_imag = filt_ref[1, kk].astype(jnp.float32)
        prod_real = spec_real * filt_real + spec_imag * filt_imag
        prod_imag = spec_imag * filt_real - spec_real * filt_imag
        packed = jnp.concatenate([prod_real, prod_imag], axis=0).astype(jnp.bfloat16)
        section = jnp.dot(table, packed, preferred_element_type=jnp.float32)
        section_real = section[:inner]
        section_imag = section[inner:]
        quarter_real = section_real * twist_cos - section_imag * twist_sin
        quarter_imag = section_real * twist_sin + section_imag * twist_cos
        width = quarter_real.shape[1]
        rows = pl.ds(kk * inner, inner)
        quarter[rows, pl.ds(0, width)] = quarter_real.astype(jnp.bfloat16)
        quarter[rows, pl.ds(width, width)] = quarter_imag.astype(jnp.bfloat16)
    wave = wave_ref[...]
    cols = wave.shape[1] // 2
    from_real = jnp.dot(quarter[:, :width], wave, preferred_element_type=jnp.float32)
    from_imag = jnp.dot(quarter[:, width:], wave, preferred_element_type=jnp.float32)
    result = jnp.concatenate(
        [from_real[:, :cols] - from_imag[:, cols:], from_real[:, cols:] + from_imag[:, :cols]], axis=1
    )
    o_ref[...] = result.reshape(o_ref.shape).astype(o_ref.dtype)


def front(spectrum, filters, table, twist_cos, twist_sin, wave, block=8):
    _, basis, inner, freq = filters.shape
    cols = wave.shape[1]
    whole = lambda *shape: pl.BlockSpec(shape, lambda i: (0,) * len(shape))
    return pl.pallas_call(
        front_kernel,
        grid=(basis // block,),
        out_shape=jax.ShapeDtypeStruct((basis, inner, cols), jnp.bfloat16),
        in_specs=[
            whole(2, inner, freq),
            pl.BlockSpec((2, block, inner, freq), lambda i: (0, i, 0, 0)),
            whole(2 * inner, 2 * inner),
            whole(inner, freq),
            whole(inner, freq),
            whole(freq, cols),
        ],
        out_specs=pl.BlockSpec((block, inner, cols), lambda i: (i, 0, 0)),
        scratch_shapes=[pltpu.VMEM((block * inner, 2 * freq), jnp.bfloat16)],
        compiler_params=pltpu.CompilerParams(vmem_limit_bytes=48 * 1024 * 1024),
    )(spectrum, filters, table, twist_cos, twist_sin, wave)


def on_device(spectrum, filters, mixing):
    tm_index = lax.axis_index("tm")
    local_freq = filters.shape[3]
    local_basis = filters.shape[1]
    inner = INNER
    outer = NSAMP // INNER
    table = first_table(inner)
    freqs = tm_index * local_freq + jnp.arange(local_freq, dtype=jnp.int32)
    twist_cos, twist_sin = twist_tables(freqs, inner, NSAMP)
    lags = START + jnp.arange(WROWS, dtype=jnp.int32)
    wave = wave_block(freqs, lags, outer)
    partial = front(spectrum, filters, table, twist_cos, twist_sin, wave).transpose(1, 0, 2)
    slots = exchange(partial, lax.axis_size("tm"), lax.axis_size("bank"), 4)
    return mix(mixing, slots)


def solution(mesh):
    return jax.shard_map(
        on_device,
        mesh=mesh,
        in_specs=(P(None, None, "tm"), P(None, "bank", None, "tm"), P(None, "bank", None)),
        out_specs=P(None, "tm", "bank", None),
        check_vma=False,
    )
```

```python
import functools
import math

import jax
import jax.numpy as jnp
from jax import lax
from jax.experimental import pallas as pl
from jax.experimental.pallas import tpu as pltpu
from jax.sharding import PartitionSpec as P

NSAMP = 1048576
INNER = 64
WROWS = 128
START = 8128


def first_table(inner):
    index = jnp.arange(inner, dtype=jnp.int32)
    phase = index[:, None] * index[None, :] % inner
    angle = phase.astype(jnp.float32) * (2.0 * math.pi / inner)
    cosine = jnp.cos(angle).astype(jnp.bfloat16)
    sine = jnp.sin(angle).astype(jnp.bfloat16)
    upper = jnp.concatenate([cosine, -sine], axis=1)
    lower = jnp.concatenate([sine, cosine], axis=1)
    return jnp.concatenate([upper, lower], axis=0)


def wave_block(freqs, lags, period):
    phase = freqs[:, None] * lags[None, :] % period
    angle = phase.astype(jnp.float32) * (2.0 * math.pi / period)
    cosine = jnp.cos(angle).astype(jnp.bfloat16)
    sine = jnp.sin(angle).astype(jnp.bfloat16)
    return jnp.concatenate([cosine, sine], axis=1)


def twist_tables(freqs, inner, total):
    rows_index = jnp.arange(inner, dtype=jnp.int32)
    phase = rows_index[:, None] * freqs[None, :] % total
    angle = phase.astype(jnp.float32) * (2.0 * math.pi / total)
    return (jnp.cos(angle), jnp.sin(angle))


MESH = pl.DeviceIdType.MESH


def exchange_kernel(width, group, x_ref, o_ref, slots, scatter_send, scatter_recv, gather_send, gather_recv,
                    relay_send, relay_recv):
    n_tm, n_bank = slots.shape[1], o_ref.shape[0]
    depth = n_bank // width
    rows, basis = o_ref.shape[1], o_ref.shape[2]
    stages = rows // group
    half = basis // 2
    me_tm = lax.axis_index("tm")
    me_bank = lax.axis_index("bank")
    x = me_bank // depth
    z = me_bank % depth
    up = (z + 1) % depth
    down = (z + depth - 1) % depth
    at_tm = lambda peer: (peer, me_bank)
    at_bank = lambda peer: (me_tm, peer)
    near = [(x + step) % width * depth + z for step in range(1, width)]
    near += [xx * depth + up for xx in range(width)] + [xx * depth + down for xx in range(width)]
    barrier = pltpu.get_barrier_semaphore()
    for step in range(1, n_tm):
        pl.semaphore_signal(barrier, inc=1, device_id=at_tm((me_tm + step) % n_tm), device_id_type=MESH)
    for peer in near:
        pl.semaphore_signal(barrier, inc=1, device_id=at_bank(peer), device_id_type=MESH)
    pl.semaphore_wait(barrier, n_tm - 1 + len(near))

    def remote(src, dst, send, recv, device):
        return pltpu.make_async_remote_copy(
            src_ref=src, dst_ref=dst, send_sem=send, recv_sem=recv, device_id=device, device_id_type=MESH
        )

    def relays(g):
        out = []
        for xx in range(width):
            out.append((xx * depth + down, 0, x * depth + up, 0, xx))
            out.append((xx * depth + up, half, x * depth + down, 1, xx))
        return out

    sends = []
    for g in range(stages):
        part = pl.ds(g * group, group)
        for step in range(1, n_tm):
            peer = (me_tm + step) % n_tm
            copy = remote(
                x_ref.at[pl.ds(peer * rows + g * group, group)], slots.at[part, me_tm],
                scatter_send.at[g, peer], scatter_recv.at[g, me_tm], at_tm(peer),
            )
            copy.start()
            sends.append(copy)

    def forward(g):
        part = pl.ds(g * group, group)
        for source in near:
            remote(
                o_ref.at[source, part], o_ref.at[source, part],
                gather_send.at[g, source], gather_recv.at[g, source], at_bank(source),
            ).wait_recv()
        for slot, start, target, way, xx in relays(g):
            block = o_ref.at[slot, part, pl.ds(start, half)]
            copy = remote(block, block, relay_send.at[g, way, xx], relay_recv.at[g, way, xx], at_bank(target))
            copy.start()
            sends.append(copy)

    for g in range(stages):
        part = pl.ds(g * group, group)
        total = x_ref[pl.ds(me_tm * rows + g * group, group)].astype(jnp.float32)
        for step in range(1, n_tm):
            source = (me_tm + n_tm - step) % n_tm
            remote(
                x_ref.at[pl.ds(0, group)], slots.at[part, source],
                scatter_send.at[g, source], scatter_recv.at[g, source], at_tm(source),
            ).wait_recv()
            total = total + slots[part, source].astype(jnp.float32)
        o_ref[me_bank, part] = total.astype(o_ref.dtype)
        for peer in near:
            copy = remote(
                o_ref.at[me_bank, part], o_ref.at[me_bank, part],
                gather_send.at[g, peer], gather_recv.at[g, me_bank], at_bank(peer),
            )
            copy.start()
            sends.append(copy)
        if g >= 1:
            forward(g - 1)
    forward(stages - 1)
    across = (z + 2) % depth
    for g in range(stages):
        part = pl.ds(g * group, group)
        for xx in range(width):
            for way, start, via in ((0, 0, down), (1, half, up)):
                block = o_ref.at[xx * depth + across, part, pl.ds(start, half)]
                remote(
                    block, block, relay_send.at[g, way, xx], relay_recv.at[g, way, xx], at_bank(x * depth + via)
                ).wait_recv()
    for copy in sends:
        copy.wait_send()


def exchange(x, n_tm, n_bank, width, group=2):
    rows = x.shape[0] // n_tm
    stages = rows // group
    block = x.shape[1:]
    return pl.pallas_call(
        functools.partial(exchange_kernel, width, group),
        out_shape=jax.ShapeDtypeStruct((n_bank, rows) + block, x.dtype),
        in_specs=[pl.BlockSpec(memory_space=pltpu.VMEM)],
        out_specs=pl.BlockSpec(memory_space=pltpu.VMEM),
        scratch_shapes=[
            pltpu.VMEM((rows, n_tm) + block, x.dtype),
            pltpu.SemaphoreType.DMA((stages, n_tm)),
            pltpu.SemaphoreType.DMA((stages, n_tm)),
            pltpu.SemaphoreType.DMA((stages, n_bank)),
            pltpu.SemaphoreType.DMA((stages, n_bank)),
            pltpu.SemaphoreType.DMA((stages, 2, width)),
            pltpu.SemaphoreType.DMA((stages, 2, width)),
        ],
        compiler_params=pltpu.CompilerParams(collective_id=0, has_side_effects=True),
    )(x)


def mix_kernel(mix_ref, slots_ref, o_ref):
    n, _, _, cols = slots_ref.shape
    half = cols // 2
    mix_real = mix_ref[0]
    mix_imag = mix_ref[1]
    plain = jnp.concatenate([slots_ref[slot, 0] for slot in range(n)], axis=0)
    turned = jnp.concatenate([-plain[:, half:], plain[:, :half]], axis=1)
    result = jnp.dot(mix_real, plain, preferred_element_type=jnp.float32) + jnp.dot(
        mix_imag, turned, preferred_element_type=jnp.float32
    )
    o_ref[0, 0] = result[:, :half].astype(o_ref.dtype)
    o_ref[1, 0] = result[:, half:].astype(o_ref.dtype)


def mix(mixing, slots):
    n, rows, basis, cols = slots.shape
    templates = mixing.shape[1]
    return pl.pallas_call(
        mix_kernel,
        grid=(rows,),
        out_shape=jax.ShapeDtypeStruct((2, rows, templates, cols // 2), jnp.bfloat16),
        in_specs=[
            pl.BlockSpec(mixing.shape, lambda t: (0, 0, 0)),
            pl.BlockSpec((n, 1, basis, cols), lambda t: (0, t, 0, 0)),
        ],
        out_specs=pl.BlockSpec((2, 1, templates, cols // 2), lambda t: (0, t, 0, 0)),
    )(mixing, slots)


def front_kernel(spec_ref, filt_ref, table_ref, tcos_ref, tsin_ref, wave_ref, o_ref, quarter):
    block, inner = filt_ref.shape[1], filt_ref.shape[2]
    spec_real = spec_ref[0]
    spec_imag = spec_ref[1]
    table = table_ref[...]
    twist_cos = tcos_ref[...]
    twist_sin = tsin_ref[...]
    for kk in range(block):
        filt_real = filt_ref[0, kk].astype(jnp.float32)
        filt_imag = filt_ref[1, kk].astype(jnp.float32)
        prod_real = spec_real * filt_real + spec_imag * filt_imag
        prod_imag = spec_imag * filt_real - spec_real * filt_imag
        packed = jnp.concatenate([prod_real, prod_imag], axis=0).astype(jnp.bfloat16)
        section = jnp.dot(table, packed, preferred_element_type=jnp.float32)
        section_real = section[:inner]
        section_imag = section[inner:]
        quarter_real = section_real * twist_cos - section_imag * twist_sin
        quarter_imag = section_real * twist_sin + section_imag * twist_cos
        width = quarter_real.shape[1]
        rows = pl.ds(kk * inner, inner)
        quarter[rows, pl.ds(0, width)] = quarter_real.astype(jnp.bfloat16)
        quarter[rows, pl.ds(width, width)] = quarter_imag.astype(jnp.bfloat16)
    wave = wave_ref[...]
    cols = wave.shape[1] // 2
    from_real = jnp.dot(quarter[:, :width], wave, preferred_element_type=jnp.float32)
    from_imag = jnp.dot(quarter[:, width:], wave, preferred_element_type=jnp.float32)
    result = jnp.concatenate(
        [from_real[:, :cols] - from_imag[:, cols:], from_real[:, cols:] + from_imag[:, :cols]], axis=1
    )
    o_ref[...] = result.reshape(o_ref.shape).astype(o_ref.dtype)


def front(spectrum, filters, table, twist_cos, twist_sin, wave, block=8):
    _, basis, inner, freq = filters.shape
    cols = wave.shape[1]
    whole = lambda *shape: pl.BlockSpec(shape, lambda i: (0,) * len(shape))
    return pl.pallas_call(
        front_kernel,
        grid=(basis // block,),
        out_shape=jax.ShapeDtypeStruct((basis, inner, cols), jnp.bfloat16),
        in_specs=[
            whole(2, inner, freq),
            pl.BlockSpec((2, block, inner, freq), lambda i: (0, i, 0, 0)),
            whole(2 * inner, 2 * inner),
            whole(inner, freq),
            whole(inner, freq),
            whole(freq, cols),
        ],
        out_specs=pl.BlockSpec((block, inner, cols), lambda i: (i, 0, 0)),
        scratch_shapes=[pltpu.VMEM((block * inner, 2 * freq), jnp.bfloat16)],
        compiler_params=pltpu.CompilerParams(vmem_limit_bytes=48 * 1024 * 1024),
    )(spectrum, filters, table, twist_cos, twist_sin, wave)


def on_device(spectrum, filters, mixing):
    tm_index = lax.axis_index("tm")
    local_freq = filters.shape[3]
    local_basis = filters.shape[1]
    inner = INNER
    outer = NSAMP // INNER
    table = first_table(inner)
    freqs = tm_index * local_freq + jnp.arange(local_freq, dtype=jnp.int32)
    twist_cos, twist_sin = twist_tables(freqs, inner, NSAMP)
    lags = START + jnp.arange(WROWS, dtype=jnp.int32)
    wave = wave_block(freqs, lags, outer)
    partial = front(spectrum, filters, table, twist_cos, twist_sin, wave).transpose(1, 0, 2)
    slots = exchange(partial, lax.axis_size("tm"), lax.axis_size("bank"), 4)
    return mix(mixing, slots)


def solution(mesh):
    return jax.shard_map(
        on_device,
        mesh=mesh,
        in_specs=(P(None, None, "tm"), P(None, "bank", None, "tm"), P(None, "bank", None)),
        out_specs=P(None, "tm", "bank", None),
        check_vma=False,
    )
```

```python
import functools
import math

import jax
import jax.numpy as jnp
from jax import lax
from jax.experimental import pallas as pl
from jax.experimental.pallas import tpu as pltpu
from jax.sharding import PartitionSpec as P

NSAMP = 1048576
INNER = 64
WROWS = 128
START = 8128


def first_table(inner):
    index = jnp.arange(inner, dtype=jnp.int32)
    phase = index[:, None] * index[None, :] % inner
    angle = phase.astype(jnp.float32) * (2.0 * math.pi / inner)
    cosine = jnp.cos(angle).astype(jnp.bfloat16)
    sine = jnp.sin(angle).astype(jnp.bfloat16)
    upper = jnp.concatenate([cosine, -sine], axis=1)
    lower = jnp.concatenate([sine, cosine], axis=1)
    return jnp.concatenate([upper, lower], axis=0)


def wave_block(freqs, lags, period):
    phase = freqs[:, None] * lags[None, :] % period
    angle = phase.astype(jnp.float32) * (2.0 * math.pi / period)
    cosine = jnp.cos(angle).astype(jnp.bfloat16)
    sine = jnp.sin(angle).astype(jnp.bfloat16)
    return jnp.concatenate([cosine, sine], axis=1)


def twist_tables(freqs, inner, total):
    rows_index = jnp.arange(inner, dtype=jnp.int32)
    phase = rows_index[:, None] * freqs[None, :] % total
    angle = phase.astype(jnp.float32) * (2.0 * math.pi / total)
    return (jnp.cos(angle), jnp.sin(angle))


MESH = pl.DeviceIdType.MESH


def exchange_kernel(width, group, x_ref, o_ref, slots, scatter_send, scatter_recv, gather_send, gather_recv,
                    relay_send, relay_recv):
    n_tm, n_bank = slots.shape[1], o_ref.shape[0]
    depth = n_bank // width
    rows, basis = o_ref.shape[1], o_ref.shape[2]
    stages = rows // group
    half = basis // 2
    me_tm = lax.axis_index("tm")
    me_bank = lax.axis_index("bank")
    x = me_bank // depth
    z = me_bank % depth
    up = (z + 1) % depth
    down = (z + depth - 1) % depth
    at_tm = lambda peer: (peer, me_bank)
    at_bank = lambda peer: (me_tm, peer)
    near = [(x + step) % width * depth + z for step in range(1, width)]
    near += [xx * depth + up for xx in range(width)] + [xx * depth + down for xx in range(width)]
    slot_of = lambda b: (b % depth) * width + b // depth
    me_slot = z * width + x
    barrier = pltpu.get_barrier_semaphore()
    for step in range(1, n_tm):
        pl.semaphore_signal(barrier, inc=1, device_id=at_tm((me_tm + step) % n_tm), device_id_type=MESH)
    for peer in near:
        pl.semaphore_signal(barrier, inc=1, device_id=at_bank(peer), device_id_type=MESH)
    pl.semaphore_wait(barrier, n_tm - 1 + len(near))

    def remote(src, dst, send, recv, device):
        return pltpu.make_async_remote_copy(
            src_ref=src, dst_ref=dst, send_sem=send, recv_sem=recv, device_id=device, device_id_type=MESH
        )

    def relays(g):
        return [(down * width, 0, x * depth + up, 0), (up * width, half, x * depth + down, 1)]

    sends = []
    for g in range(stages):
        part = pl.ds(g * group, group)
        for step in range(1, n_tm):
            peer = (me_tm + step) % n_tm
            copy = remote(
                x_ref.at[pl.ds(peer * rows + g * group, group)], slots.at[part, me_tm],
                scatter_send.at[g, peer], scatter_recv.at[g, me_tm], at_tm(peer),
            )
            copy.start()
            sends.append(copy)

    def forward(g):
        part = pl.ds(g * group, group)
        for source in near:
            remote(
                o_ref.at[slot_of(source), part], o_ref.at[slot_of(source), part],
                gather_send.at[g, source], gather_recv.at[g, source], at_bank(source),
            ).wait_recv()
        for first, start, target, way in relays(g):
            block = o_ref.at[pl.ds(first, width), part, pl.ds(start, half)]
            copy = remote(block, block, relay_send.at[g, way], relay_recv.at[g, way], at_bank(target))
            copy.start()
            sends.append(copy)

    for g in range(stages):
        part = pl.ds(g * group, group)
        total = x_ref[pl.ds(me_tm * rows + g * group, group)].astype(jnp.float32)
        for step in range(1, n_tm):
            source = (me_tm + n_tm - step) % n_tm
            remote(
                x_ref.at[pl.ds(0, group)], slots.at[part, source],
                scatter_send.at[g, source], scatter_recv.at[g, source], at_tm(source),
            ).wait_recv()
            total = total + slots[part, source].astype(jnp.float32)
        o_ref[me_slot, part] = total.astype(o_ref.dtype)
        for peer in near:
            copy = remote(
                o_ref.at[me_slot, part], o_ref.at[me_slot, part],
                gather_send.at[g, peer], gather_recv.at[g, me_bank], at_bank(peer),
            )
            copy.start()
            sends.append(copy)
        if g >= 1:
            forward(g - 1)
    forward(stages - 1)
    across = (z + 2) % depth
    for g in range(stages):
        part = pl.ds(g * group, group)
        for way, start, via in ((0, 0, down), (1, half, up)):
            block = o_ref.at[pl.ds(across * width, width), part, pl.ds(start, half)]
            remote(
                block, block, relay_send.at[g, way], relay_recv.at[g, way], at_bank(x * depth + via)
            ).wait_recv()
    for copy in sends:
        copy.wait_send()


def exchange(x, n_tm, n_bank, width, group=2):
    rows = x.shape[0] // n_tm
    stages = rows // group
    block = x.shape[1:]
    return pl.pallas_call(
        functools.partial(exchange_kernel, width, group),
        out_shape=jax.ShapeDtypeStruct((n_bank, rows) + block, x.dtype),
        in_specs=[pl.BlockSpec(memory_space=pltpu.VMEM)],
        out_specs=pl.BlockSpec(memory_space=pltpu.VMEM),
        scratch_shapes=[
            pltpu.VMEM((rows, n_tm) + block, x.dtype),
            pltpu.SemaphoreType.DMA((stages, n_tm)),
            pltpu.SemaphoreType.DMA((stages, n_tm)),
            pltpu.SemaphoreType.DMA((stages, n_bank)),
            pltpu.SemaphoreType.DMA((stages, n_bank)),
            pltpu.SemaphoreType.DMA((stages, 2)),
            pltpu.SemaphoreType.DMA((stages, 2)),
        ],
        compiler_params=pltpu.CompilerParams(collective_id=0, has_side_effects=True),
    )(x)


def mix_kernel(width, mix_ref, slots_ref, o_ref):
    n, rows, _, cols = slots_ref.shape
    half = cols // 2
    depth = n // width
    order = [z * width + x for x in range(width) for z in range(depth)]
    mix_real = mix_ref[0]
    mix_imag = mix_ref[1]
    for t in range(rows):
        plain = jnp.concatenate([slots_ref[slot, t] for slot in order], axis=0)
        turned = jnp.concatenate([-plain[:, half:], plain[:, :half]], axis=1)
        result = jnp.dot(mix_real, plain, preferred_element_type=jnp.float32) + jnp.dot(
            mix_imag, turned, preferred_element_type=jnp.float32
        )
        o_ref[0, t] = result[:, :half].astype(o_ref.dtype)
        o_ref[1, t] = result[:, half:].astype(o_ref.dtype)


def mix(mixing, slots, width):
    _, rows, _, cols = slots.shape
    templates = mixing.shape[1]
    return pl.pallas_call(
        functools.partial(mix_kernel, width),
        out_shape=jax.ShapeDtypeStruct((2, rows, templates, cols // 2), jnp.bfloat16),
        in_specs=[pl.BlockSpec(memory_space=pltpu.VMEM)] * 2,
        out_specs=pl.BlockSpec(memory_space=pltpu.VMEM),
    )(mixing, slots)


def front_kernel(spec_ref, filt_ref, table_ref, tcos_ref, tsin_ref, wave_ref, o_ref, quarter):
    block, inner = filt_ref.shape[1], filt_ref.shape[2]
    spec_real = spec_ref[0]
    spec_imag = spec_ref[1]
    table = table_ref[...]
    twist_cos = tcos_ref[...]
    twist_sin = tsin_ref[...]
    for kk in range(block):
        filt_real = filt_ref[0, kk].astype(jnp.float32)
        filt_imag = filt_ref[1, kk].astype(jnp.float32)
        prod_real = spec_real * filt_real + spec_imag * filt_imag
        prod_imag = spec_imag * filt_real - spec_real * filt_imag
        packed = jnp.concatenate([prod_real, prod_imag], axis=0).astype(jnp.bfloat16)
        section = jnp.dot(table, packed, preferred_element_type=jnp.float32)
        section_real = section[:inner]
        section_imag = section[inner:]
        quarter_real = section_real * twist_cos - section_imag * twist_sin
        quarter_imag = section_real * twist_sin + section_imag * twist_cos
        width = quarter_real.shape[1]
        rows = pl.ds(kk * inner, inner)
        quarter[rows, pl.ds(0, width)] = quarter_real.astype(jnp.bfloat16)
        quarter[rows, pl.ds(width, width)] = quarter_imag.astype(jnp.bfloat16)
    wave = wave_ref[...]
    cols = wave.shape[1] // 2
    from_real = jnp.dot(quarter[:, :width], wave, preferred_element_type=jnp.float32)
    from_imag = jnp.dot(quarter[:, width:], wave, preferred_element_type=jnp.float32)
    result = jnp.concatenate(
        [from_real[:, :cols] - from_imag[:, cols:], from_real[:, cols:] + from_imag[:, :cols]], axis=1
    )
    o_ref[...] = result.reshape(o_ref.shape).astype(o_ref.dtype)


def front(spectrum, filters, table, twist_cos, twist_sin, wave, block=8):
    _, basis, inner, freq = filters.shape
    cols = wave.shape[1]
    whole = lambda *shape: pl.BlockSpec(shape, lambda i: (0,) * len(shape))
    return pl.pallas_call(
        front_kernel,
        grid=(basis // block,),
        out_shape=jax.ShapeDtypeStruct((basis, inner, cols), jnp.bfloat16),
        in_specs=[
            whole(2, inner, freq),
            pl.BlockSpec((2, block, inner, freq), lambda i: (0, i, 0, 0)),
            whole(2 * inner, 2 * inner),
            whole(inner, freq),
            whole(inner, freq),
            whole(freq, cols),
        ],
        out_specs=pl.BlockSpec((block, inner, cols), lambda i: (i, 0, 0)),
        scratch_shapes=[pltpu.VMEM((block * inner, 2 * freq), jnp.bfloat16)],
        compiler_params=pltpu.CompilerParams(vmem_limit_bytes=48 * 1024 * 1024),
    )(spectrum, filters, table, twist_cos, twist_sin, wave)


def on_device(spectrum, filters, mixing):
    tm_index = lax.axis_index("tm")
    local_freq = filters.shape[3]
    local_basis = filters.shape[1]
    inner = INNER
    outer = NSAMP // INNER
    table = first_table(inner)
    freqs = tm_index * local_freq + jnp.arange(local_freq, dtype=jnp.int32)
    twist_cos, twist_sin = twist_tables(freqs, inner, NSAMP)
    lags = START + jnp.arange(WROWS, dtype=jnp.int32)
    wave = wave_block(freqs, lags, outer)
    partial = front(spectrum, filters, table, twist_cos, twist_sin, wave).transpose(1, 0, 2)
    slots = exchange(partial, lax.axis_size("tm"), lax.axis_size("bank"), 4)
    return mix(mixing, slots, 4)


def solution(mesh):
    return jax.shard_map(
        on_device,
        mesh=mesh,
        in_specs=(P(None, None, "tm"), P(None, "bank", None, "tm"), P(None, "bank", None)),
        out_specs=P(None, "tm", "bank", None),
        check_vma=False,
    )
```

```python
import functools
import math

import jax
import jax.numpy as jnp
from jax import lax
from jax.experimental import pallas as pl
from jax.experimental.pallas import tpu as pltpu
from jax.sharding import PartitionSpec as P

NSAMP = 1048576
INNER = 64
WROWS = 128
START = 8128


def first_table(inner):
    index = jnp.arange(inner, dtype=jnp.int32)
    phase = index[:, None] * index[None, :] % inner
    angle = phase.astype(jnp.float32) * (2.0 * math.pi / inner)
    cosine = jnp.cos(angle).astype(jnp.bfloat16)
    sine = jnp.sin(angle).astype(jnp.bfloat16)
    upper = jnp.concatenate([cosine, -sine], axis=1)
    lower = jnp.concatenate([sine, cosine], axis=1)
    return jnp.concatenate([upper, lower], axis=0)


def wave_block(freqs, lags, period):
    phase = freqs[:, None] * lags[None, :] % period
    angle = phase.astype(jnp.float32) * (2.0 * math.pi / period)
    cosine = jnp.cos(angle).astype(jnp.bfloat16)
    sine = jnp.sin(angle).astype(jnp.bfloat16)
    return jnp.concatenate([cosine, sine], axis=1)


def twist_tables(freqs, inner, total):
    rows_index = jnp.arange(inner, dtype=jnp.int32)
    phase = rows_index[:, None] * freqs[None, :] % total
    angle = phase.astype(jnp.float32) * (2.0 * math.pi / total)
    return (jnp.cos(angle), jnp.sin(angle))


MESH = pl.DeviceIdType.MESH


def exchange_kernel(width, group, x_ref, o_ref, slots, scatter_send, scatter_recv, gather_send, gather_recv,
                    relay_send, relay_recv):
    n_tm, n_bank = slots.shape[1], o_ref.shape[0]
    depth = n_bank // width
    rows, basis = o_ref.shape[1], o_ref.shape[2]
    stages = rows // group
    half = basis // 2
    me_tm = lax.axis_index("tm")
    me_bank = lax.axis_index("bank")
    x = me_bank // depth
    z = me_bank % depth
    up = (z + 1) % depth
    down = (z + depth - 1) % depth
    at_tm = lambda peer: (peer, me_bank)
    at_bank = lambda peer: (me_tm, peer)
    near = [(x + step) % width * depth + z for step in range(1, width)]
    near += [xx * depth + up for xx in range(width)] + [xx * depth + down for xx in range(width)]
    slot_of = lambda b: (b % depth) * width + b // depth
    me_slot = z * width + x
    barrier = pltpu.get_barrier_semaphore()
    for step in range(1, n_tm):
        pl.semaphore_signal(barrier, inc=1, device_id=at_tm((me_tm + step) % n_tm), device_id_type=MESH)
    for peer in near:
        pl.semaphore_signal(barrier, inc=1, device_id=at_bank(peer), device_id_type=MESH)
    pl.semaphore_wait(barrier, n_tm - 1 + len(near))

    def remote(src, dst, send, recv, device):
        return pltpu.make_async_remote_copy(
            src_ref=src, dst_ref=dst, send_sem=send, recv_sem=recv, device_id=device, device_id_type=MESH
        )

    def relays(g):
        return [(down * width, 0, x * depth + up, 0), (up * width, half, x * depth + down, 1)]

    sends = []
    for g in range(stages):
        part = pl.ds(g * group, group)
        for step in range(1, n_tm):
            peer = (me_tm + step) % n_tm
            copy = remote(
                x_ref.at[pl.ds(peer * rows + g * group, group)], slots.at[part, me_tm],
                scatter_send.at[g, peer], scatter_recv.at[g, me_tm], at_tm(peer),
            )
            copy.start()
            sends.append(copy)

    def forward(g):
        part = pl.ds(g * group, group)
        for source in near:
            remote(
                o_ref.at[slot_of(source), part], o_ref.at[slot_of(source), part],
                gather_send.at[g, source], gather_recv.at[g, source], at_bank(source),
            ).wait_recv()
        for first, start, target, way in relays(g):
            block = o_ref.at[pl.ds(first, width), part, pl.ds(start, half)]
            copy = remote(block, block, relay_send.at[g, way], relay_recv.at[g, way], at_bank(target))
            copy.start()
            sends.append(copy)

    for g in range(stages):
        part = pl.ds(g * group, group)
        total = x_ref[pl.ds(me_tm * rows + g * group, group)].astype(jnp.float32)
        for step in range(1, n_tm):
            source = (me_tm + n_tm - step) % n_tm
            remote(
                x_ref.at[pl.ds(0, group)], slots.at[part, source],
                scatter_send.at[g, source], scatter_recv.at[g, source], at_tm(source),
            ).wait_recv()
            total = total + slots[part, source].astype(jnp.float32)
        o_ref[me_slot, part] = total.astype(o_ref.dtype)
        for peer in near:
            copy = remote(
                o_ref.at[me_slot, part], o_ref.at[me_slot, part],
                gather_send.at[g, peer], gather_recv.at[g, me_bank], at_bank(peer),
            )
            copy.start()
            sends.append(copy)
        if g >= 1:
            forward(g - 1)
    forward(stages - 1)
    across = (z + 2) % depth
    for g in range(stages):
        part = pl.ds(g * group, group)
        for way, start, via in ((0, 0, down), (1, half, up)):
            block = o_ref.at[pl.ds(across * width, width), part, pl.ds(start, half)]
            remote(
                block, block, relay_send.at[g, way], relay_recv.at[g, way], at_bank(x * depth + via)
            ).wait_recv()
    for copy in sends:
        copy.wait_send()


def exchange(x, n_tm, n_bank, width, group=2):
    rows = x.shape[0] // n_tm
    stages = rows // group
    block = x.shape[1:]
    return pl.pallas_call(
        functools.partial(exchange_kernel, width, group),
        out_shape=jax.ShapeDtypeStruct((n_bank, rows) + block, x.dtype),
        in_specs=[pl.BlockSpec(memory_space=pltpu.VMEM)],
        out_specs=pl.BlockSpec(memory_space=pltpu.VMEM),
        scratch_shapes=[
            pltpu.VMEM((rows, n_tm) + block, x.dtype),
            pltpu.SemaphoreType.DMA((stages, n_tm)),
            pltpu.SemaphoreType.DMA((stages, n_tm)),
            pltpu.SemaphoreType.DMA((stages, n_bank)),
            pltpu.SemaphoreType.DMA((stages, n_bank)),
            pltpu.SemaphoreType.DMA((stages, 2)),
            pltpu.SemaphoreType.DMA((stages, 2)),
        ],
        compiler_params=pltpu.CompilerParams(collective_id=0, has_side_effects=True),
    )(x)


def mix_kernel(width, mix_ref, slots_ref, o_ref):
    n, rows, _, cols = slots_ref.shape
    half = cols // 2
    depth = n // width
    order = [z * width + x for x in range(width) for z in range(depth)]
    mix_real = mix_ref[0]
    mix_imag = mix_ref[1]
    for t in range(rows):
        plain = jnp.concatenate([slots_ref[slot, t] for slot in order], axis=0)
        turned = jnp.concatenate([-plain[:, half:], plain[:, :half]], axis=1)
        result = jnp.dot(mix_real, plain, preferred_element_type=jnp.float32) + jnp.dot(
            mix_imag, turned, preferred_element_type=jnp.float32
        )
        o_ref[0, t] = result[:, :half].astype(o_ref.dtype)
        o_ref[1, t] = result[:, half:].astype(o_ref.dtype)


def mix(mixing, slots, width):
    _, rows, _, cols = slots.shape
    templates = mixing.shape[1]
    return pl.pallas_call(
        functools.partial(mix_kernel, width),
        out_shape=jax.ShapeDtypeStruct((2, rows, templates, cols // 2), jnp.bfloat16),
        in_specs=[pl.BlockSpec(memory_space=pltpu.VMEM)] * 2,
        out_specs=pl.BlockSpec(memory_space=pltpu.VMEM),
    )(mixing, slots)


def front_kernel(spec_ref, filt_ref, table_ref, tcos_ref, tsin_ref, wave_ref, o_ref, quarter):
    block, inner = filt_ref.shape[1], filt_ref.shape[2]
    spec_real = spec_ref[0]
    spec_imag = spec_ref[1]
    table = table_ref[...]
    twist_cos = tcos_ref[...]
    twist_sin = tsin_ref[...]
    for kk in range(block):
        filt_real = filt_ref[0, kk].astype(jnp.float32)
        filt_imag = filt_ref[1, kk].astype(jnp.float32)
        prod_real = spec_real * filt_real + spec_imag * filt_imag
        prod_imag = spec_imag * filt_real - spec_real * filt_imag
        packed = jnp.concatenate([prod_real, prod_imag], axis=0).astype(jnp.bfloat16)
        section = jnp.dot(table, packed, preferred_element_type=jnp.float32)
        section_real = section[:inner]
        section_imag = section[inner:]
        quarter_real = section_real * twist_cos - section_imag * twist_sin
        quarter_imag = section_real * twist_sin + section_imag * twist_cos
        width = quarter_real.shape[1]
        rows = pl.ds(kk * inner, inner)
        quarter[rows, pl.ds(0, width)] = quarter_real.astype(jnp.bfloat16)
        quarter[rows, pl.ds(width, width)] = quarter_imag.astype(jnp.bfloat16)
    wave = wave_ref[...]
    cols = wave.shape[1] // 2
    from_real = jnp.dot(quarter[:, :width], wave, preferred_element_type=jnp.float32)
    from_imag = jnp.dot(quarter[:, width:], wave, preferred_element_type=jnp.float32)
    result = jnp.concatenate(
        [from_real[:, :cols] - from_imag[:, cols:], from_real[:, cols:] + from_imag[:, :cols]], axis=1
    )
    o_ref[...] = result.reshape(o_ref.shape).astype(o_ref.dtype)


def front(spectrum, filters, table, twist_cos, twist_sin, wave, block=4):
    _, basis, inner, freq = filters.shape
    cols = wave.shape[1]
    whole = lambda *shape: pl.BlockSpec(shape, lambda i: (0,) * len(shape))
    return pl.pallas_call(
        front_kernel,
        grid=(basis // block,),
        out_shape=jax.ShapeDtypeStruct((basis, inner, cols), jnp.bfloat16),
        in_specs=[
            whole(2, inner, freq),
            pl.BlockSpec((2, block, inner, freq), lambda i: (0, i, 0, 0)),
            whole(2 * inner, 2 * inner),
            whole(inner, freq),
            whole(inner, freq),
            whole(freq, cols),
        ],
        out_specs=pl.BlockSpec((block, inner, cols), lambda i: (i, 0, 0)),
        scratch_shapes=[pltpu.VMEM((block * inner, 2 * freq), jnp.bfloat16)],
        compiler_params=pltpu.CompilerParams(vmem_limit_bytes=48 * 1024 * 1024),
    )(spectrum, filters, table, twist_cos, twist_sin, wave)


def on_device(spectrum, filters, mixing):
    tm_index = lax.axis_index("tm")
    local_freq = filters.shape[3]
    local_basis = filters.shape[1]
    inner = INNER
    outer = NSAMP // INNER
    table = first_table(inner)
    freqs = tm_index * local_freq + jnp.arange(local_freq, dtype=jnp.int32)
    twist_cos, twist_sin = twist_tables(freqs, inner, NSAMP)
    lags = START + jnp.arange(WROWS, dtype=jnp.int32)
    wave = wave_block(freqs, lags, outer)
    partial = front(spectrum, filters, table, twist_cos, twist_sin, wave).transpose(1, 0, 2)
    slots = exchange(partial, lax.axis_size("tm"), lax.axis_size("bank"), 4)
    return mix(mixing, slots, 4)


def solution(mesh):
    return jax.shard_map(
        on_device,
        mesh=mesh,
        in_specs=(P(None, None, "tm"), P(None, "bank", None, "tm"), P(None, "bank", None)),
        out_specs=P(None, "tm", "bank", None),
        check_vma=False,
    )
```

```python
import functools
import math

import jax
import jax.numpy as jnp
from jax import lax
from jax.experimental import pallas as pl
from jax.experimental.pallas import tpu as pltpu
from jax.sharding import PartitionSpec as P

NSAMP = 1048576
INNER = 64
WROWS = 128
START = 8128


def first_table(inner):
    index = jnp.arange(inner, dtype=jnp.int32)
    phase = index[:, None] * index[None, :] % inner
    angle = phase.astype(jnp.float32) * (2.0 * math.pi / inner)
    cosine = jnp.cos(angle).astype(jnp.bfloat16)
    sine = jnp.sin(angle).astype(jnp.bfloat16)
    upper = jnp.concatenate([cosine, -sine], axis=1)
    lower = jnp.concatenate([sine, cosine], axis=1)
    return jnp.concatenate([upper, lower], axis=0)


def wave_block(freqs, lags, period):
    phase = freqs[:, None] * lags[None, :] % period
    angle = phase.astype(jnp.float32) * (2.0 * math.pi / period)
    cosine = jnp.cos(angle).astype(jnp.bfloat16)
    sine = jnp.sin(angle).astype(jnp.bfloat16)
    return jnp.concatenate([cosine, sine], axis=1)


def twist_tables(freqs, inner, total):
    rows_index = jnp.arange(inner, dtype=jnp.int32)
    phase = rows_index[:, None] * freqs[None, :] % total
    angle = phase.astype(jnp.float32) * (2.0 * math.pi / total)
    return (jnp.cos(angle), jnp.sin(angle))


MESH = pl.DeviceIdType.MESH


def exchange_kernel(width, group, x_ref, o_ref, slots, scatter_send, scatter_recv, gather_send, gather_recv,
                    relay_send, relay_recv):
    n_tm, n_bank = slots.shape[1], o_ref.shape[0]
    depth = n_bank // width
    rows, basis = o_ref.shape[1], o_ref.shape[2]
    stages = rows // group
    half = basis // 2
    me_tm = lax.axis_index("tm")
    me_bank = lax.axis_index("bank")
    x = me_bank // depth
    z = me_bank % depth
    up = (z + 1) % depth
    down = (z + depth - 1) % depth
    at_tm = lambda peer: (peer, me_bank)
    at_bank = lambda peer: (me_tm, peer)
    near = [(x + step) % width * depth + z for step in range(1, width)]
    near += [xx * depth + up for xx in range(width)] + [xx * depth + down for xx in range(width)]
    slot_of = lambda b: (b % depth) * width + b // depth
    me_slot = z * width + x
    barrier = pltpu.get_barrier_semaphore()
    for step in range(1, n_tm):
        pl.semaphore_signal(barrier, inc=1, device_id=at_tm((me_tm + step) % n_tm), device_id_type=MESH)
    for peer in near:
        pl.semaphore_signal(barrier, inc=1, device_id=at_bank(peer), device_id_type=MESH)
    pl.semaphore_wait(barrier, n_tm - 1 + len(near))

    def remote(src, dst, send, recv, device):
        return pltpu.make_async_remote_copy(
            src_ref=src, dst_ref=dst, send_sem=send, recv_sem=recv, device_id=device, device_id_type=MESH
        )

    def relays(g):
        return [(down * width, 0, x * depth + up, 0), (up * width, half, x * depth + down, 1)]

    sends = []
    for g in range(stages):
        part = pl.ds(g * group, group)
        for step in range(1, n_tm):
            peer = (me_tm + step) % n_tm
            copy = remote(
                x_ref.at[pl.ds(peer * rows + g * group, group)], slots.at[part, me_tm],
                scatter_send.at[g, peer], scatter_recv.at[g, me_tm], at_tm(peer),
            )
            copy.start()
            sends.append(copy)

    def forward(g):
        part = pl.ds(g * group, group)
        for source in near:
            remote(
                o_ref.at[slot_of(source), part], o_ref.at[slot_of(source), part],
                gather_send.at[g, source], gather_recv.at[g, source], at_bank(source),
            ).wait_recv()
        for first, start, target, way in relays(g):
            block = o_ref.at[pl.ds(first, width), part, pl.ds(start, half)]
            copy = remote(block, block, relay_send.at[g, way], relay_recv.at[g, way], at_bank(target))
            copy.start()
            sends.append(copy)

    for g in range(stages):
        part = pl.ds(g * group, group)
        if g >= 1:
            forward(g - 1)
        total = x_ref[pl.ds(me_tm * rows + g * group, group)].astype(jnp.float32)
        for step in range(1, n_tm):
            source = (me_tm + n_tm - step) % n_tm
            remote(
                x_ref.at[pl.ds(0, group)], slots.at[part, source],
                scatter_send.at[g, source], scatter_recv.at[g, source], at_tm(source),
            ).wait_recv()
            total = total + slots[part, source].astype(jnp.float32)
        o_ref[me_slot, part] = total.astype(o_ref.dtype)
        for peer in near:
            copy = remote(
                o_ref.at[me_slot, part], o_ref.at[me_slot, part],
                gather_send.at[g, peer], gather_recv.at[g, me_bank], at_bank(peer),
            )
            copy.start()
            sends.append(copy)
    forward(stages - 1)
    across = (z + 2) % depth
    for g in range(stages):
        part = pl.ds(g * group, group)
        for way, start, via in ((0, 0, down), (1, half, up)):
            block = o_ref.at[pl.ds(across * width, width), part, pl.ds(start, half)]
            remote(
                block, block, relay_send.at[g, way], relay_recv.at[g, way], at_bank(x * depth + via)
            ).wait_recv()
    for copy in sends:
        copy.wait_send()


def exchange(x, n_tm, n_bank, width, group=2):
    rows = x.shape[0] // n_tm
    stages = rows // group
    block = x.shape[1:]
    return pl.pallas_call(
        functools.partial(exchange_kernel, width, group),
        out_shape=jax.ShapeDtypeStruct((n_bank, rows) + block, x.dtype),
        in_specs=[pl.BlockSpec(memory_space=pltpu.VMEM)],
        out_specs=pl.BlockSpec(memory_space=pltpu.VMEM),
        scratch_shapes=[
            pltpu.VMEM((rows, n_tm) + block, x.dtype),
            pltpu.SemaphoreType.DMA((stages, n_tm)),
            pltpu.SemaphoreType.DMA((stages, n_tm)),
            pltpu.SemaphoreType.DMA((stages, n_bank)),
            pltpu.SemaphoreType.DMA((stages, n_bank)),
            pltpu.SemaphoreType.DMA((stages, 2)),
            pltpu.SemaphoreType.DMA((stages, 2)),
        ],
        compiler_params=pltpu.CompilerParams(collective_id=0, has_side_effects=True),
    )(x)


def mix_kernel(width, mix_ref, slots_ref, o_ref):
    n, rows, _, cols = slots_ref.shape
    half = cols // 2
    depth = n // width
    order = [z * width + x for x in range(width) for z in range(depth)]
    mix_real = mix_ref[0]
    mix_imag = mix_ref[1]
    for t in range(rows):
        plain = jnp.concatenate([slots_ref[slot, t] for slot in order], axis=0)
        turned = jnp.concatenate([-plain[:, half:], plain[:, :half]], axis=1)
        result = jnp.dot(mix_real, plain, preferred_element_type=jnp.float32) + jnp.dot(
            mix_imag, turned, preferred_element_type=jnp.float32
        )
        o_ref[0, t] = result[:, :half].astype(o_ref.dtype)
        o_ref[1, t] = result[:, half:].astype(o_ref.dtype)


def mix(mixing, slots, width):
    _, rows, _, cols = slots.shape
    templates = mixing.shape[1]
    return pl.pallas_call(
        functools.partial(mix_kernel, width),
        out_shape=jax.ShapeDtypeStruct((2, rows, templates, cols // 2), jnp.bfloat16),
        in_specs=[pl.BlockSpec(memory_space=pltpu.VMEM)] * 2,
        out_specs=pl.BlockSpec(memory_space=pltpu.VMEM),
    )(mixing, slots)


def front_kernel(spec_ref, filt_ref, table_ref, tcos_ref, tsin_ref, wave_ref, o_ref, quarter):
    block, inner = filt_ref.shape[1], filt_ref.shape[2]
    spec_real = spec_ref[0]
    spec_imag = spec_ref[1]
    table = table_ref[...]
    twist_cos = tcos_ref[...]
    twist_sin = tsin_ref[...]
    for kk in range(block):
        filt_real = filt_ref[0, kk].astype(jnp.float32)
        filt_imag = filt_ref[1, kk].astype(jnp.float32)
        prod_real = spec_real * filt_real + spec_imag * filt_imag
        prod_imag = spec_imag * filt_real - spec_real * filt_imag
        packed = jnp.concatenate([prod_real, prod_imag], axis=0).astype(jnp.bfloat16)
        section = jnp.dot(table, packed, preferred_element_type=jnp.float32)
        section_real = section[:inner]
        section_imag = section[inner:]
        quarter_real = section_real * twist_cos - section_imag * twist_sin
        quarter_imag = section_real * twist_sin + section_imag * twist_cos
        width = quarter_real.shape[1]
        rows = pl.ds(kk * inner, inner)
        quarter[rows, pl.ds(0, width)] = quarter_real.astype(jnp.bfloat16)
        quarter[rows, pl.ds(width, width)] = quarter_imag.astype(jnp.bfloat16)
    wave = wave_ref[...]
    cols = wave.shape[1] // 2
    from_real = jnp.dot(quarter[:, :width], wave, preferred_element_type=jnp.float32)
    from_imag = jnp.dot(quarter[:, width:], wave, preferred_element_type=jnp.float32)
    result = jnp.concatenate(
        [from_real[:, :cols] - from_imag[:, cols:], from_real[:, cols:] + from_imag[:, :cols]], axis=1
    )
    o_ref[...] = result.reshape(o_ref.shape).astype(o_ref.dtype)


def front(spectrum, filters, table, twist_cos, twist_sin, wave, block=8):
    _, basis, inner, freq = filters.shape
    cols = wave.shape[1]
    whole = lambda *shape: pl.BlockSpec(shape, lambda i: (0,) * len(shape))
    return pl.pallas_call(
        front_kernel,
        grid=(basis // block,),
        out_shape=jax.ShapeDtypeStruct((basis, inner, cols), jnp.bfloat16),
        in_specs=[
            whole(2, inner, freq),
            pl.BlockSpec((2, block, inner, freq), lambda i: (0, i, 0, 0)),
            whole(2 * inner, 2 * inner),
            whole(inner, freq),
            whole(inner, freq),
            whole(freq, cols),
        ],
        out_specs=pl.BlockSpec((block, inner, cols), lambda i: (i, 0, 0)),
        scratch_shapes=[pltpu.VMEM((block * inner, 2 * freq), jnp.bfloat16)],
        compiler_params=pltpu.CompilerParams(vmem_limit_bytes=48 * 1024 * 1024),
    )(spectrum, filters, table, twist_cos, twist_sin, wave)


def on_device(spectrum, filters, mixing):
    tm_index = lax.axis_index("tm")
    local_freq = filters.shape[3]
    local_basis = filters.shape[1]
    inner = INNER
    outer = NSAMP // INNER
    table = first_table(inner)
    freqs = tm_index * local_freq + jnp.arange(local_freq, dtype=jnp.int32)
    twist_cos, twist_sin = twist_tables(freqs, inner, NSAMP)
    lags = START + jnp.arange(WROWS, dtype=jnp.int32)
    wave = wave_block(freqs, lags, outer)
    partial = front(spectrum, filters, table, twist_cos, twist_sin, wave).transpose(1, 0, 2)
    slots = exchange(partial, lax.axis_size("tm"), lax.axis_size("bank"), 4)
    return mix(mixing, slots, 4)


def solution(mesh):
    return jax.shard_map(
        on_device,
        mesh=mesh,
        in_specs=(P(None, None, "tm"), P(None, "bank", None, "tm"), P(None, "bank", None)),
        out_specs=P(None, "tm", "bank", None),
        check_vma=False,
    )
```
